256 devices in a mesh: pool: 4 (over x), section: 2 (over core), tensor: 32 (over z, y).
Axes of the slice: x: 4, y: 4, z: 8, core: 2. Of those that a mesh axis runs over, the one named last changes fastest.
Arguments:
- hidden_input: bfloat16 [2048, 8192], P('pool', 'tensor'), may hold values from -6 to 6
- attention_output: bfloat16 [2, 2048, 8192], P('section', 'pool', 'tensor'), may hold values from -6 to 6
- projection_weight: bfloat16 [2, 8192, 8192], P('section', 'tensor'), may hold values from -0.125 to 0.125
- lowrank_down_factor: bfloat16 [2, 128, 64, 8192], P('section', 'pool', None, 'tensor'), may hold values from -0.0625 to 0.0625
- lowrank_up_factor: bfloat16 [2, 128, 64, 8192], P('section', 'pool', None, 'tensor'), may hold values from -0.75 to 0.75
- residual_block_mats: bfloat16 [2, 128, 32, 128, 128], P('section', 'pool', 'tensor'), may hold values from -0.5 to 0.5
- diagonal_block_index: int32 [2, 128, 32], P('section', 'pool', 'tensor'), may hold values from 0 to 63, as said below
- row_variant_index: int32 [2048], P('pool'), may hold values from 0 to 127, as said below
Outputs:
- hidden_out: bfloat16 [2, 2048, 8192], P('section', 'pool', 'tensor')
The draws below stay inside these ranges and needn't reach their ends.
Inputs may be any that keep to these rules, and one draw needn't show every extreme that they name: `row_variant_index`: within each aligned block of 512 rows the ids never fall; at most 256 rows of a block name variants of one owner q (ids q * 32 to (q + 1) * 32 - 1), and some owner receives exactly 256 rows from every block. `diagonal_block_index`: entry j of each list lies in j * 2 to (j + 1) * 2 - 1.
All inputs are finite; a program needn't handle non-finite values.
Results may differ from the reference program's by a relative error of at most 0.017.
Values may be sent and summed in bfloat16 or wider, within the bound.
No kernel may reach another device: no remote copies, remote signals or barrier semaphores. Data moves between devices by JAX's collectives and lax.ppermute only.
A program may use at most 128 MiB of HBM per device.

```python
import math
import jax
import jax.numpy as jnp
from jax import lax

MODEL_WIDTH = 8192
DELTA_RANK = 64
BLK = 128
VAR_DEV = 32
ROWS_DEV = 512
LAYER_COUNT = 2
FEAT_GROUPS = 32
NBLK = 32
BPS = 2
POOLS = 4
VARIANT_COUNT = 128
ROWS = 2048
CAP = 256


def draw_row_variant_index(key, part):
    base_key = jax.random.fold_in(key, 17)
    hot_key, owner_key, local_key = jax.random.split(base_key, 3)
    hot_owner = jax.random.randint(hot_key, (), 0, POOLS)
    others = jax.random.randint(owner_key, (POOLS, ROWS_DEV), 0, POOLS - 1)
    others = others + (others >= hot_owner).astype(jnp.int32)
    position = jnp.arange(ROWS_DEV)[None, :]
    owners = jnp.where(position < CAP, hot_owner, others)
    local_var = jax.random.randint(local_key, (POOLS, ROWS_DEV), 0, VAR_DEV)
    chosen = jnp.sort(owners * VAR_DEV + local_var, axis=1)
    return chosen.reshape(ROWS).astype(jnp.int32)


def draw_diagonal_block_index(key, part):
    offsets = jax.random.randint(jax.random.fold_in(key, 29), (LAYER_COUNT, VARIANT_COUNT, NBLK), 0, BPS)
    return (jnp.arange(NBLK, dtype=jnp.int32)[None, None, :] * BPS + offsets).astype(jnp.int32)


def strengthened(entries, own_key, source, target, parts, factor):
    owner, partner = [(jnp.arange(entries.shape[dim]) // (entries.shape[dim] // parts)).reshape([-1 if axis == dim else 1 for axis in range(entries.ndim)]) for dim in (source, target)]
    chosen = jax.random.permutation(own_key, parts)[partner]
    strong = (owner == chosen) | (owner == (partner + parts // 2) % parts)
    return jnp.where(strong, factor * entries, entries)


def level_of(rng, shape, cuts, least, top_value):
    gain, own = 1.0, jax.random.fold_in(rng, 6)
    for axis_at, blocks in cuts:
        steps = jnp.exp(jax.random.uniform(jax.random.fold_in(own, axis_at), (blocks,), jnp.float32, least / len(cuts), top_value / len(cuts)))
        gain = gain * jnp.repeat(steps, shape[axis_at] // blocks).reshape([-1 if axis == axis_at else 1 for axis in range(len(shape))])
    return gain


def centred(key, dims, deviation, limit, cuts=(), held_as=jnp.bfloat16):
    factor_of = level_of(key, dims, cuts, -0.22, 0.18) if cuts else 1.0
    array = jax.random.normal(key, dims, jnp.float32) * deviation * factor_of
    return jnp.minimum(jnp.maximum(array, -limit), limit).astype(held_as)


def bell_draw_with(rng, shape, deviation, most, pieces, heavy, held_as=jnp.bfloat16):
    result = deviation * jax.random.normal(rng, shape, jnp.float32)
    if pieces:
        result = result * level_of(rng, shape, pieces, -0.22, 0.18)
    return jnp.clip(strengthened(result, jax.random.fold_in(rng, 3), *heavy), -most, most).astype(held_as)


def setup_inputs(seed: int = 0) -> dict:
    splits = jax.random.split(jax.random.key(seed), 9)
    return {
        "hidden_input": centred(splits[0], (ROWS, MODEL_WIDTH), 1.0, 6.0, ((0, 4), (1, 32))),
        "attention_output": centred(splits[1], (LAYER_COUNT, ROWS, MODEL_WIDTH), 1.0, 6.0, ((0, 2), (1, 4), (2, 32))),
        "projection_weight": bell_draw_with(splits[2], (LAYER_COUNT, MODEL_WIDTH, MODEL_WIDTH), MODEL_WIDTH ** -0.5, 0.125, ((0, 2), (1, 32)), (1, 2, 32, 2.75)),
        "lowrank_down_factor": centred(splits[3], (LAYER_COUNT, VARIANT_COUNT, DELTA_RANK, MODEL_WIDTH), MODEL_WIDTH ** -0.5, 0.0625, ((0, 2), (1, 4), (3, 32))),
        "lowrank_up_factor": centred(splits[4], (LAYER_COUNT, VARIANT_COUNT, DELTA_RANK, MODEL_WIDTH), DELTA_RANK ** -0.5, 0.75, ((0, 2), (1, 4), (3, 32))),
        "residual_block_mats": centred(splits[5], (LAYER_COUNT, VARIANT_COUNT, NBLK, BLK, BLK), BLK ** -0.5, 0.5, ((0, 2), (1, 4), (2, 32))),
        "diagonal_block_index": draw_diagonal_block_index(jax.random.fold_in(splits[8], 71), 0),
        "row_variant_index": draw_row_variant_index(jax.random.fold_in(splits[8], 71), 0),
    }


def group_sum(features, weight):
    group_width = MODEL_WIDTH // FEAT_GROUPS
    feat_groups = jnp.transpose(features.reshape(ROWS, FEAT_GROUPS, group_width), (1, 0, 2))
    weight_groups = weight.reshape(FEAT_GROUPS, group_width, MODEL_WIDTH)

    def add_group(running, operands):
        feat_part, weight_part = operands
        product = jnp.dot(feat_part, weight_part, preferred_element_type=jnp.float32).astype(jnp.bfloat16)
        product = lax.optimization_barrier(product)
        return running + product.astype(jnp.float32), None

    return lax.scan(add_group, jnp.zeros((ROWS, MODEL_WIDTH), jnp.float32), (feat_groups, weight_groups))[0]


def adapter_row_values(features, row_vars, down_all, up_all, block_all, index_all):
    row_block = math.gcd(ROWS, 64)
    feat_split = features.reshape(ROWS // row_block, row_block, MODEL_WIDTH)
    var_split = row_vars.reshape(ROWS // row_block, row_block)

    def one_block(operands):
        feat_rows, block_vars = operands
        down_factor_rows = jnp.take(down_all, block_vars, axis=0)
        lowrank_product = jnp.einsum("rkd,rd->rk", down_factor_rows.astype(jnp.float32), feat_rows.astype(jnp.float32)).astype(jnp.bfloat16)
        up_factor_rows = jnp.take(up_all, block_vars, axis=0)
        lowrank_output = jnp.einsum("la,lat->lt", lowrank_product.astype(jnp.float32), up_factor_rows.astype(jnp.float32))
        block_mats = jnp.take(block_all, block_vars, axis=0)
        places = jnp.take(index_all, block_vars, axis=0).astype(jnp.int32)
        feat_blocks = feat_rows.reshape(row_block, MODEL_WIDTH // BLK, BLK)
        picked = jnp.take_along_axis(feat_blocks, places[:, :, None], axis=1)
        block_y = jnp.einsum("rjk,rjkm->rjm", picked.astype(jnp.float32), block_mats.astype(jnp.float32))
        place_hot = (places[:, :, None] == jnp.arange(MODEL_WIDTH // BLK, dtype=jnp.int32)[None, None, :]).astype(jnp.float32)
        block_output = jnp.einsum("rjm,rjb->rbm", block_y, place_hot).reshape(row_block, MODEL_WIDTH)
        return (lowrank_output + block_output).astype(jnp.bfloat16)

    return lax.map(one_block, (feat_split, var_split)).reshape(ROWS, MODEL_WIDTH)


def reference(hidden_input, attention_output, projection_weight, lowrank_down_factor, lowrank_up_factor, residual_block_mats, diagonal_block_index, row_variant_index):
    current = hidden_input
    outputs = []
    for layer_number in range(LAYER_COUNT):
        base_sum = group_sum(attention_output[layer_number], projection_weight[layer_number])
        adapter_output = adapter_row_values(attention_output[layer_number], row_variant_index, lowrank_down_factor[layer_number], lowrank_up_factor[layer_number], residual_block_mats[layer_number], diagonal_block_index[layer_number])
        current = (current.astype(jnp.float32) + base_sum + adapter_output.astype(jnp.float32)).astype(jnp.bfloat16)
        outputs.append(current)
    return jnp.stack(outputs)
```

```python
import jax
import jax.numpy as jnp
from jax import lax
from jax.sharding import Mesh
from jax.sharding import PartitionSpec as P

TENSOR = ("tensor_0", "tensor_1")


def summed_rows(terms, axes):
    total = terms.astype(jnp.bfloat16)
    total = lax.psum_scatter(total, axes, scatter_dimension=0, tiled=True)
    return total.astype(jnp.float32)


def rows_for(lines, peers):
    spare = -lines.shape[0] % peers
    if not spare:
        return lines
    return jnp.concatenate([lines, jnp.zeros((spare, *lines.shape[1:]), lines.dtype)])


def sent_to_all(x, axis):
    peers = lax.axis_size(axis)
    return lax.all_to_all(jnp.broadcast_to(x[None], (peers, *x.shape)), axis, 0, 0, tiled=True)


def joined_along(parts, dim):
    dims = list(parts.shape[1:])
    dims[dim] *= parts.shape[0]
    return jnp.moveaxis(parts, 0, dim).reshape(dims)


def gather_directly(x, axis, dim):
    parts = sent_to_all(x, axis)
    return joined_along(parts, dim)


def in_blocks(x, dim, peers):
    before, after = (x.shape[:dim], x.shape[dim + 1 :])
    return jnp.moveaxis(x.reshape(*before, peers, -1, *after), dim, 0)


def summed_on_arrival(x, axis, dim):
    parts = in_blocks(x, dim, lax.axis_size(axis))
    arrived = lax.all_to_all(parts, axis, split_axis=0, concat_axis=0, tiled=True)
    return arrived.astype(jnp.float32).sum(axis=0)


def total_of(x, axes):
    lines = x.reshape(-1, x.shape[-1])
    padded = rows_for(lines, lax.axis_size(axes))
    whole = gather_directly(summed_on_arrival(padded, axes, 0).astype(jnp.bfloat16), axes, 0)
    return lax.slice_in_dim(whole, 0, len(lines)).reshape(x.shape).astype(jnp.float32)


def shifted(value, axis, steps):
    count = lax.axis_size(axis)
    first, last = (max(0, -steps), min(count, count - steps))
    return lax.ppermute(value, axis, [(source, source + steps) for source in range(first, last)])


def adapter_delta(
    features, select, down_factor_rows, up_factor_rows, block_mats, place_hot, reducer
):
    var_count, low_dim, shard_width = down_factor_rows.shape
    block_size = block_mats.shape[-1]
    per_shard = shard_width // block_size
    projected = lax.dot_general(
        features,
        down_factor_rows.reshape(var_count * low_dim, shard_width),
        (((1,), (1,)), ((), ())),
        preferred_element_type=jnp.float32,
    )
    partial_value = jnp.einsum("svr,sv->sr", projected.reshape(-1, var_count, low_dim), select)
    lowrank_product = reducer(partial_value).astype(jnp.bfloat16)
    spread = (select.astype(jnp.bfloat16)[:, :, None] * lowrank_product[:, None, :]).reshape(
        -1, var_count * low_dim
    )
    lowrank_output = jnp.dot(
        spread,
        up_factor_rows.reshape(var_count * low_dim, shard_width),
        preferred_element_type=jnp.float32,
    )
    row_place = jnp.dot(select, place_hot.astype(jnp.float32))
    feat_blocks = features.reshape(-1, per_shard, block_size)
    picked = jnp.sum(feat_blocks * row_place.astype(jnp.bfloat16)[:, :, None], axis=1)
    stacked = jnp.transpose(block_mats, (1, 0, 2)).reshape(block_size, var_count * block_size)
    block_y = jnp.dot(picked, stacked, preferred_element_type=jnp.float32).reshape(
        -1, var_count, block_size
    )
    block_sel = jnp.einsum("svj,sv->sj", block_y, select)
    block_output = (row_place[:, :, None] * block_sel[:, None, :]).reshape(-1, shard_width)
    return (lowrank_output + block_output).astype(jnp.bfloat16)


def per_device(
    hidden_input,
    attention_output,
    projection_weight,
    lowrank_down_factor,
    lowrank_up_factor,
    residual_block_mats,
    diagonal_block_index,
    row_variant_index,
):
    features = attention_output[0]
    weight = projection_weight[0]
    row_count_dev, shard_width = features.shape
    down_factor_rows = lowrank_down_factor[0]
    up_factor_rows = lowrank_up_factor[0]
    block_mats = residual_block_mats[0][:, 0]
    var_count = down_factor_rows.shape[0]
    block_size = block_mats.shape[-1]
    per_shard = shard_width // block_size
    tensor_pos = lax.axis_index(TENSOR)
    section_pos = lax.axis_index("section")
    place_hot = (
        (diagonal_block_index[0][:, 0] - tensor_pos * per_shard)[:, None]
        == jnp.arange(per_shard)[None, :]
    ).astype(jnp.bfloat16)
    base_sum = summed_rows(
        lax.dot_general(
            weight, features, (((0,), (1,)), ((), ())), preferred_element_type=jnp.float32
        ),
        TENSOR,
    )
    pool_count = lax.axis_size("pool")
    capacity = row_count_dev // 2
    owners = row_variant_index // var_count
    owner_hot = (owners[:, None] == jnp.arange(pool_count)[None, :]).astype(jnp.int32)
    counts = jnp.sum(owner_hot, axis=0)
    starts = jnp.cumsum(counts) - counts
    slot_pos = jnp.arange(row_count_dev) - jnp.sum(owner_hot * starts[None, :], axis=1)
    filled = jnp.arange(capacity)[None, :] < counts[:, None]
    source = jnp.minimum(starts[:, None] + jnp.arange(capacity)[None, :], row_count_dev - 1)
    send_feat = jnp.where(
        filled[:, :, None], jnp.take(features, source, axis=0), jnp.zeros((), jnp.bfloat16)
    )
    send_var = jnp.where(
        filled,
        jnp.take(row_variant_index, source) - jnp.arange(pool_count)[:, None] * var_count,
        -1,
    ).astype(jnp.bfloat16)
    recv_feat = lax.all_to_all(send_feat, "pool", split_axis=0, concat_axis=0, tiled=True)
    recv_var = lax.all_to_all(send_var, "pool", split_axis=0, concat_axis=0, tiled=True)
    group_count, item_count = recv_var.shape
    flat_var = recv_var.reshape(group_count * item_count)
    select = (flat_var[:, None] == jnp.arange(var_count).astype(jnp.bfloat16)[None, :]).astype(
        jnp.float32
    )

    def slot_reduce(partial_value):
        return total_of(partial_value.astype(jnp.bfloat16), TENSOR)

    served = adapter_delta(
        recv_feat.reshape(group_count * item_count, shard_width),
        select,
        down_factor_rows,
        up_factor_rows,
        block_mats,
        place_hot,
        slot_reduce,
    )
    returned = lax.all_to_all(
        served.reshape(group_count, item_count, shard_width),
        "pool",
        split_axis=0,
        concat_axis=0,
        tiled=True,
    )
    flat_back = returned.reshape(pool_count * capacity, shard_width)
    adapter_output = jnp.take(flat_back, owners * capacity + slot_pos, axis=0)
    branch = jnp.transpose(base_sum) + adapter_output.astype(jnp.float32)
    first_out = (hidden_input.astype(jnp.float32) + branch).astype(jnp.bfloat16)
    carried = shifted(first_out, "section", 1)
    start_rows = jnp.where(section_pos == 0, hidden_input, carried)
    return (start_rows.astype(jnp.float32) + branch).astype(jnp.bfloat16)[None]


def solution(mesh):
    finer = Mesh(
        mesh.devices.reshape(mesh.shape["pool"], mesh.shape["section"], 8, 4),
        ("pool", "section", "tensor_0", "tensor_1"),
    )
    placed = (
        P("pool", TENSOR),
        P("section", "pool", TENSOR),
        P("section", TENSOR, None),
        P("section", "pool", None, TENSOR),
        P("section", "pool", None, TENSOR),
        P("section", "pool", TENSOR, None, None),
        P("section", "pool", TENSOR),
        P("pool"),
    )
    return jax.shard_map(
        per_device,
        mesh=finer,
        in_specs=placed,
        out_specs=P("section", "pool", TENSOR),
        check_vma=False,
    )
```

```python
import functools

import jax
import jax.numpy as jnp
from jax import lax
from jax.experimental import pallas as pl
from jax.experimental.pallas import tpu as pltpu
from jax.sharding import Mesh
from jax.sharding import PartitionSpec as P


Z, Y = "tensor_0", "tensor_1"
TENSOR = (Z, Y)
NZ, NY, NX = 8, 4, 4
ROWS, WIDTH, TILE = 512, 256, 256
WINDOW = 256
IDROWS = 16
VARS, RANK, BLK = 32, 64, 128
HOPS = (1, 3, 2)
F32, BF16 = jnp.float32, jnp.bfloat16
ANY = pl.BlockSpec(memory_space=pl.ANY)
SMEM = pl.BlockSpec(memory_space=pltpu.SMEM)


def shift(value, axis, steps):
    count = lax.axis_size(axis)
    return lax.ppermute(value, axis, [(i, (i + steps) % count) for i in range(count)])


def cost(flops, nbytes):
    return pl.CostEstimate(flops=flops, bytes_accessed=nbytes, transcendentals=0)


def shape(dims, dtype=BF16):
    return jax.ShapeDtypeStruct(dims, dtype)


def whole(dims, at=None):
    at = at or (0,) * len(dims)
    return pl.BlockSpec(dims, lambda: at)


def tiles_of(group):
    z = lax.axis_index(Z)
    return lax.rem(z + (4 - group), NZ), lax.rem(z + (group + NZ - 3), NZ)


def column(ztile, ytile):
    return pl.multiple_of((ztile * NY + ytile) * TILE, TILE)


def pack_kernel(groups, with_features, *refs):
    n_in = 2 if with_features else 1
    w_ref = refs[0]
    outs = refs[n_in : n_in + 3 * len(groups)]
    buf, in_sem, out_sem = refs[n_in + 3 * len(groups) :][:3]
    y = lax.axis_index(Y)
    reads, writes = [], []
    for gi, group in enumerate(groups):
        for ti, ztile in enumerate(tiles_of(group)):
            for ki, hop in enumerate(HOPS):
                slot = (gi * 3 + ki) * 2 + ti
                col = column(ztile, lax.rem(y + hop, NY))
                first = ti * TILE + (ROWS if with_features else 0)
                reads.append(
                    pltpu.make_async_copy(w_ref.at[:, pl.ds(col, TILE)], buf.at[slot], in_sem.at[slot])
                )
                writes.append(
                    pltpu.make_async_copy(
                        buf.at[slot], outs[gi * 3 + ki].at[pl.ds(first, TILE), :], out_sem.at[slot]
                    )
                )
    extra = []
    if with_features:
        x_ref = refs[1]
        xbuf, xin, xout = refs[-3:]
        read = pltpu.make_async_copy(x_ref, xbuf, xin)
        read.start()
        for ki in range(3):
            extra.append(pltpu.make_async_copy(xbuf, outs[ki].at[pl.ds(0, ROWS), :], xout.at[ki]))
    for copy in reads:
        copy.start()
    if with_features:
        read.wait()
        for copy in extra:
            copy.start()
    for got, put in zip(reads, writes):
        got.wait()
        put.start()
    for copy in writes + extra:
        copy.wait()


def pack(groups, weight, features=None):
    with_features = features is not None
    rows = 2 * TILE + (ROWS if with_features else 0)
    count = len(groups) * 6
    scratch = [
        pltpu.VMEM((count, TILE, TILE), BF16),
        pltpu.SemaphoreType.DMA((count,)),
        pltpu.SemaphoreType.DMA((count,)),
    ]
    args = [weight]
    if with_features:
        scratch += [
            pltpu.VMEM((ROWS, WIDTH), BF16),
            pltpu.SemaphoreType.DMA,
            pltpu.SemaphoreType.DMA((3,)),
        ]
        args.append(features)
    return pl.pallas_call(
        functools.partial(pack_kernel, groups, with_features),
        out_shape=[shape((rows, TILE))] * (3 * len(groups)),
        in_specs=[ANY] * len(args),
        out_specs=[ANY] * (3 * len(groups)),
        scratch_shapes=scratch,
        cost_estimate=cost(0, 4 * count * TILE * TILE),
        name="pack",
    )(*args)


def project_kernel(group, which, has_in, *refs):
    w_ref, x_ref = refs[:2]
    peers = refs[2:5]
    pos = 5
    blocks = peers
    if group:
        blocks = refs[5:8]
        pos = 8
    base = 0 if group else ROWS
    carried = []
    for _ in which:
        carried.append(refs[pos] if has_in else None)
        pos += 1 if has_in else 0
    outs = refs[pos : pos + len(which)]
    own, sem = refs[pos + len(which) :]
    y = lax.axis_index(Y)
    ztiles = tiles_of(group)
    copies = [
        pltpu.make_async_copy(w_ref.at[:, pl.ds(column(ztiles[ti], y), TILE)], own.at[n], sem.at[n])
        for n, ti in enumerate(which)
    ]
    for copy in copies:
        copy.start()
    lhs = jnp.concatenate([peer[0:ROWS, :] for peer in peers], axis=1)
    for n, ti in enumerate(which):
        rows = slice(base + ti * TILE, base + (ti + 1) * TILE)
        rhs = jnp.concatenate([block[rows, :] for block in blocks], axis=0)
        total = jnp.dot(lhs, rhs, preferred_element_type=F32)
        copies[n].wait()
        total = total + jnp.dot(x_ref[...], own[n], preferred_element_type=F32)
        if carried[n] is not None:
            total = total + carried[n][...].astype(F32)
        outs[n][...] = total.astype(outs[n].dtype)


def project(group, which, weight, features, first_got, got, carried, out_dtype=BF16):
    half = (ROWS, WIDTH)
    in_specs = [ANY, whole(half)] + [whole((2 * ROWS, TILE))] * 3
    args = [weight, features, *first_got]
    if group:
        in_specs += [whole((2 * TILE, TILE))] * 3
        args += list(got)
    in_specs += [whole(half)] * len(carried)
    args += list(carried)
    n = len(which)
    return pl.pallas_call(
        functools.partial(project_kernel, group, which, bool(carried)),
        out_shape=[shape((ROWS, TILE), out_dtype)] * n,
        in_specs=in_specs,
        out_specs=[whole((ROWS, TILE))] * n,
        scratch_shapes=[pltpu.VMEM((n, TILE, TILE), BF16), pltpu.SemaphoreType.DMA((n,))],
        cost_estimate=cost(2 * ROWS * 1024 * TILE * n, 2 << 20),
        name="project",
    )(*args)


def window_start(ids, owner):
    before = jnp.sum((ids < owner * VARS).astype(jnp.int32))
    return jnp.minimum(before, ROWS - WINDOW)


def dispatch_kernel(ids_ref, x_ref, *outs):
    me = lax.axis_index("pool")
    ids = ids_ref[...]
    features = x_ref[...]
    for k in range(NX):
        owner = lax.rem(me + k, NX)
        start = window_start(ids, owner)
        at = lax.broadcasted_iota(jnp.int32, (WINDOW, ROWS), 0) + start
        hot = (at == lax.broadcasted_iota(jnp.int32, (WINDOW, ROWS), 1)).astype(F32).astype(BF16)
        outs[k][0:WINDOW, :] = jnp.dot(hot, features, preferred_element_type=F32).astype(BF16)
        local = jnp.broadcast_to((ids - owner * VARS).astype(F32), (IDROWS, ROWS)).astype(BF16)
        outs[k][WINDOW : WINDOW + IDROWS, :] = lax.dot_general(
            local, hot, (((1,), (1,)), ((), ())), preferred_element_type=F32
        ).astype(BF16)


def dispatch(ids, features):
    return pl.pallas_call(
        dispatch_kernel,
        out_shape=[shape((WINDOW + IDROWS, WIDTH))] * NX,
        in_specs=[whole((1, ROWS)), whole((ROWS, WIDTH))],
        out_specs=[whole((WINDOW + IDROWS, WIDTH))] * NX,
        cost_estimate=cost(2 * 1024 * 512 * 256, 1 << 20),
        name="dispatch",
    )(ids, features)


def variant_columns(item_ref, lanes):
    row = jnp.broadcast_to(item_ref[WINDOW : WINDOW + 1, :].astype(F32), (WINDOW, WINDOW))
    diagonal = lax.broadcasted_iota(jnp.int32, (WINDOW, WINDOW), 0) == lax.broadcasted_iota(
        jnp.int32, (WINDOW, WINDOW), 1
    )
    spread = jnp.where(diagonal, row, 0.0).astype(BF16)
    return jnp.dot(spread, jnp.ones((WINDOW, lanes), BF16), preferred_element_type=F32)


def down_kernel(i0, i1, i2, i3, down_ref, out_ref, var_ref, acc_ref):
    items = (i0, i1, i2, i3)
    for k in range(NX):
        var_ref[k] = variant_columns(items[k], 256)
        acc_ref[k] = jnp.zeros((WINDOW, 256), F32)
    lane = lax.broadcasted_iota(jnp.int32, (1, 256), 1)
    part = lax.div(lane, jnp.int32(RANK)).astype(F32)

    def step(j, carry):
        factor = down_ref[pl.ds(pl.multiple_of(j * 256, 256), 256), :]
        wanted = part + (j * 4).astype(F32)
        for k in range(NX):
            value = lax.dot_general(
                items[k][0:WINDOW, :],
                factor,
                (((1,), (1,)), ((), ())),
                preferred_element_type=F32,
            )
            acc_ref[k] += jnp.where(var_ref[k] == wanted, value, 0.0)
        return carry

    lax.fori_loop(0, VARS * RANK // 256, step, 0)
    folded = []
    for k in range(NX):
        two = acc_ref[k, :, 0:128] + acc_ref[k, :, 128:256]
        folded.append(two + pltpu.roll(two, RANK, 1))
    low = lax.broadcasted_iota(jnp.int32, (WINDOW, 128), 1) < RANK
    for h in range(2):
        packed = jnp.where(low, folded[h], folded[h + 2]).astype(BF16)
        out_ref[h * 16 : (h + 1) * 16] = packed.reshape(16, 16, 128)


def down(items, factor):
    return pl.pallas_call(
        down_kernel,
        out_shape=shape((32, 16, 128)),
        in_specs=[whole((WINDOW + IDROWS, WIDTH))] * NX + [whole((VARS * RANK, WIDTH))],
        out_specs=whole((32, 16, 128)),
        scratch_shapes=[pltpu.VMEM((NX, WINDOW, 256), F32), pltpu.VMEM((NX, WINDOW, 256), F32)],
        cost_estimate=cost(2 * 1024 * 256 * 2048, 2 << 20),
        name="down",
    )(*items, factor)


def block_kernel(i0, i1, i2, i3, mats_ref, place_ref, out_ref, var_ref, rhs_ref):
    items = (i0, i1, i2, i3)
    shard = lax.axis_index(Z) * NY + lax.axis_index(Y)
    for k in range(NX):
        var_ref[k] = variant_columns(items[k], 128)
        out_ref[k] = jnp.zeros((WINDOW, 256), F32)

    def lanes_of(v):
        return pl.ds(pl.multiple_of((place_ref[v] - shard * 2) * BLK, BLK), BLK)

    def fill(v, carry):
        rhs_ref[v] = jnp.zeros((BLK, 256), BF16)
        rhs_ref[v, :, lanes_of(v)] = mats_ref[v]
        return carry

    lax.fori_loop(0, VARS, fill, 0)

    def step(c, carry):
        rhs = rhs_ref[pl.ds(c * 4, 4)].reshape(4 * BLK, 256)
        for k in range(NX):
            pieces = []
            for i in range(4):
                v = c * 4 + i
                piece = items[k][0:WINDOW, lanes_of(v)].astype(F32)
                pieces.append(jnp.where(var_ref[k] == v.astype(F32), piece, 0.0).astype(BF16))
            lhs = jnp.concatenate(pieces, axis=1)
            out_ref[k] += jnp.dot(lhs, rhs, preferred_element_type=F32)
        return carry

    lax.fori_loop(0, VARS // 4, step, 0)


def block_terms(items, mats, places):
    return pl.pallas_call(
        block_kernel,
        out_shape=shape((NX, WINDOW, 256), F32),
        in_specs=[whole((WINDOW + IDROWS, WIDTH))] * NX + [whole((VARS, BLK, BLK)), SMEM],
        out_specs=whole((NX, WINDOW, 256)),
        scratch_shapes=[pltpu.VMEM((NX, WINDOW, 128), F32), pltpu.VMEM((VARS, BLK, 256), BF16)],
        cost_estimate=cost(2 * 1024 * 4096 * 256, 3 << 20),
        name="blocks",
    )(*items, mats, places)


def total_kernel(in_ref, out_ref):
    total = jnp.sum(in_ref[...].astype(F32), axis=0).astype(BF16)
    out_ref[...] = jnp.broadcast_to(total[None], out_ref.shape)


def total(parts):
    return pl.pallas_call(
        total_kernel,
        out_shape=shape((32, 16, 128)),
        in_specs=[whole((32, 16, 128))],
        out_specs=whole((32, 16, 128)),
        cost_estimate=cost(1 << 16, 1 << 18),
        name="total",
    )(parts)


def up_kernel(i0, i1, i2, i3, low_ref, up_ref, block_ref, o0, o1, o2, o3, acc_ref, var_ref, two_ref):
    items, outs = (i0, i1, i2, i3), (o0, o1, o2, o3)
    first = lax.broadcasted_iota(jnp.int32, (WINDOW, 128), 1) < RANK
    for h in range(2):
        packed = low_ref[h * 16 : (h + 1) * 16].reshape(WINDOW, 128).astype(F32)
        turned = pltpu.roll(packed, RANK, 1)
        two_ref[h] = jnp.where(first, packed, turned)
        two_ref[h + 2] = jnp.where(first, turned, packed)
    for k in range(NX):
        var_ref[k] = variant_columns(items[k], 128)
        acc_ref[k] = block_ref[k]
    half = lax.div(lax.broadcasted_iota(jnp.int32, (1, 128), 1), jnp.int32(RANK)).astype(F32)

    def step(c, carry):
        rhs = up_ref[pl.ds(pl.multiple_of(c * 512, 512), 512), :]
        for k in range(NX):
            pieces = []
            for i in range(4):
                wanted = half + (c * 8 + i * 2).astype(F32)
                pieces.append(jnp.where(var_ref[k] == wanted, two_ref[k], 0.0).astype(BF16))
            lhs = jnp.concatenate(pieces, axis=1)
            acc_ref[k] += jnp.dot(lhs, rhs, preferred_element_type=F32)
        return carry

    lax.fori_loop(0, VARS * RANK // 512, step, 0)
    for k in range(NX):
        outs[k][...] = acc_ref[k].astype(BF16)


def up(items, lowrank, factor, blocks):
    return pl.pallas_call(
        up_kernel,
        out_shape=[shape((WINDOW, WIDTH))] * NX,
        in_specs=[whole((WINDOW + IDROWS, WIDTH))] * NX
        + [whole((32, 16, 128)), whole((VARS * RANK, WIDTH)), whole((NX, WINDOW, 256))],
        out_specs=[whole((WINDOW, WIDTH))] * NX,
        scratch_shapes=[
            pltpu.VMEM((NX, WINDOW, 256), F32),
            pltpu.VMEM((NX, WINDOW, 128), F32),
            pltpu.VMEM((NX, WINDOW, 128), F32),
        ],
        cost_estimate=cost(2 * 1024 * 256 * 2048, 3 << 20),
        name="up",
    )(*items, lowrank, factor, blocks)


def combine_kernel(ids_ref, h_ref, own_ref, plus_ref, r0, r1, r2, r3, first_ref, branch_ref):
    me = lax.axis_index("pool")
    ids = ids_ref[...]
    branch = own_ref[...] + plus_ref[...].astype(F32)
    delta = None
    for k, back in enumerate((r0, r1, r2, r3)):
        start = window_start(ids, lax.rem(me + k, NX))
        at = lax.broadcasted_iota(jnp.int32, (ROWS, WINDOW), 1) + start
        hot = (at == lax.broadcasted_iota(jnp.int32, (ROWS, WINDOW), 0)).astype(F32).astype(BF16)
        part = jnp.dot(hot, back[...], preferred_element_type=F32)
        delta = part if delta is None else delta + part
    branch = branch + delta
    branch_ref[...] = branch
    first_ref[...] = (h_ref[...].astype(F32) + branch).astype(BF16)


def combine(ids, hidden, own, plus, returned):
    half = (ROWS, WIDTH)
    return pl.pallas_call(
        combine_kernel,
        out_shape=[shape(half), shape(half, F32)],
        in_specs=[whole((1, ROWS))] + [whole(half)] * 3 + [whole((WINDOW, WIDTH))] * NX,
        out_specs=[whole(half)] * 2,
        cost_estimate=cost(2 * 512 * 1024 * 256, 2 << 20),
        name="combine",
    )(ids, hidden, own, plus, *returned)


def per_device(
    hidden_input,
    attention_output,
    projection_weight,
    lowrank_down_factor,
    lowrank_up_factor,
    residual_block_mats,
    diagonal_block_index,
    row_variant_index,
):
    features = attention_output[0]
    weight = projection_weight[0]
    down_factor = lowrank_down_factor[0].reshape(VARS * RANK, WIDTH)
    up_factor = lowrank_up_factor[0].reshape(VARS * RANK, WIDTH)
    mats = residual_block_mats[0][:, 0]
    places = diagonal_block_index[0][:, 0]
    ids = row_variant_index.reshape(1, ROWS)

    sent = dispatch(ids, features)
    items = [sent[0]] + [shift(sent[k], "pool", k) for k in (1, 2, 3)]

    first = pack((0,), weight, features)
    first_got = [shift(value, Y, hop) for value, hop in zip(first, HOPS)]
    later = pack((1, 2, 3), weight)
    got = [[shift(later[g * 3 + ki], Y, hop) for ki, hop in enumerate(HOPS)] for g in range(3)]

    parts = lax.all_to_all(down(items, down_factor), TENSOR, 0, 0, tiled=True)
    blocks = block_terms(items, mats, places)
    lowrank = lax.all_to_all(total(parts), TENSOR, 0, 0, tiled=True)

    plus, minus = project(0, (0, 1), weight, features, first_got, None, ())
    for g in (1, 2):
        carried = (shift(plus, Z, 1), shift(minus, Z, -1))
        plus, minus = project(g, (0, 1), weight, features, first_got, got[g - 1], carried)
    carried = (shift(plus, Z, 1), shift(minus, Z, -1))
    (plus,) = project(3, (0,), weight, features, first_got, got[2], carried[:1])
    plus = shift(plus, Z, 1)
    (own,) = project(3, (1,), weight, features, first_got, got[2], carried[1:], F32)

    served = up(items, lowrank, up_factor, blocks)
    returned = [served[0]] + [shift(served[k], "pool", -k) for k in (1, 2, 3)]

    first_out, branch = combine(ids, hidden_input, own, plus, returned)
    carried = lax.ppermute(first_out, "section", [(0, 1)])
    begin = jnp.where(lax.axis_index("section") == 0, hidden_input, carried)
    return (begin.astype(F32) + branch).astype(BF16)[None]


def solution(mesh):
    finer = Mesh(
        mesh.devices.reshape(mesh.shape["pool"], mesh.shape["section"], NZ, NY),
        ("pool", "section", Z, Y),
    )
    placed = (
        P("pool", TENSOR),
        P("section", "pool", TENSOR),
        P("section", TENSOR, None),
        P("section", "pool", None, TENSOR),
        P("section", "pool", None, TENSOR),
        P("section", "pool", TENSOR, None, None),
        P("section", "pool", TENSOR),
        P("pool"),
    )
    return jax.shard_map(
        per_device,
        mesh=finer,
        in_specs=placed,
        out_specs=P("section", "pool", TENSOR),
        check_vma=False,
    )
```

```python
import functools

import jax
import jax.numpy as jnp
from jax import lax
from jax.experimental import pallas as pl
from jax.experimental.pallas import tpu as pltpu
from jax.sharding import Mesh
from jax.sharding import PartitionSpec as P


Z, Y = "tensor_0", "tensor_1"
TENSOR = (Z, Y)
NZ, NY, NX = 8, 4, 4
ROWS, WIDTH, TILE = 512, 256, 256
WINDOW = 256
IDROWS = 16
VARS, RANK, BLK = 32, 64, 128
HOPS = (1, 3, 2)
F32, BF16 = jnp.float32, jnp.bfloat16
ANY = pl.BlockSpec(memory_space=pl.ANY)
HBM = pl.BlockSpec(memory_space=pltpu.HBM)
SMEM = pl.BlockSpec(memory_space=pltpu.SMEM)


def shift(value, axis, steps):
    count = lax.axis_size(axis)
    return lax.ppermute(value, axis, [(i, (i + steps) % count) for i in range(count)])


def cost(flops, nbytes):
    return pl.CostEstimate(flops=flops, bytes_accessed=nbytes, transcendentals=0)


def shape(dims, dtype=BF16):
    return pltpu.VMEM(dims, dtype)


def whole(dims, at=None):
    at = at or (0,) * len(dims)
    return pl.BlockSpec(dims, lambda: at)


def tiles_of(group):
    z = lax.axis_index(Z)
    return lax.rem(z + (4 - group), NZ), lax.rem(z + (group + NZ - 3), NZ)


def column(ztile, ytile):
    return pl.multiple_of((ztile * NY + ytile) * TILE, TILE)


def placed(value, spec):
    space = pltpu.HBM if spec is HBM else pltpu.VMEM
    if spec is SMEM:
        return value
    return pltpu.with_memory_space_constraint(value, space)


def call(kernel, args, in_specs, outs, out_specs, scratch, work, name, limit, after=()):
    n, m = len(args), len(after)
    args = [placed(arg, spec) for arg, spec in zip(args, in_specs)]

    def body(*refs):
        kernel(*refs[:n], *refs[n + m :])

    return pl.pallas_call(
        body,
        out_shape=outs,
        in_specs=list(in_specs) + [ANY] * m,
        out_specs=out_specs,
        scratch_shapes=scratch,
        cost_estimate=cost(*work),
        compiler_params=pltpu.CompilerParams(vmem_limit_bytes=limit << 20),
        name=name,
    )(*args, *after)


def pack_kernel(groups, with_features, *refs):
    n_in = 2 if with_features else 1
    w_ref = refs[0]
    outs = refs[n_in : n_in + 3 * len(groups)]
    sems = refs[-1]
    y = lax.axis_index(Y)
    copies = []
    for gi, group in enumerate(groups):
        for ki, hop in enumerate(HOPS):
            out = outs[gi * 3 + ki]
            if with_features:
                copies.append((refs[1], out.at[pl.ds(0, ROWS), :]))
            for ti, ztile in enumerate(tiles_of(group)):
                col = column(ztile, lax.rem(y + hop, NY))
                first = ti * TILE + (ROWS if with_features else 0)
                copies.append((w_ref.at[:, pl.ds(col, TILE)], out.at[pl.ds(first, TILE), :]))
    copies = [
        pltpu.make_async_copy(source, target, sems.at[i])
        for i, (source, target) in enumerate(copies)
    ]
    for copy in copies:
        copy.start()
    for copy in copies:
        copy.wait()


def pack(groups, weight, features=None, after=()):
    with_features = features is not None
    rows = 2 * TILE + (ROWS if with_features else 0)
    count = 3 * len(groups)
    args, specs = [weight], [HBM]
    if with_features:
        args.append(features)
        specs.append(HBM)
    return call(
        functools.partial(pack_kernel, groups, with_features),
        args,
        specs,
        [shape((rows, TILE))] * count,
        [whole((rows, TILE))] * count,
        [pltpu.SemaphoreType.DMA((count * 3,))],
        (0, 4 * count * rows * TILE),
        "pack",
        8,
        after,
    )


def project_kernel(group, which, has_in, *refs):
    w_ref, x_ref = refs[:2]
    peers = refs[2:5]
    pos = 5
    blocks = peers
    if group:
        blocks = refs[5:8]
        pos = 8
    base = 0 if group else ROWS
    carried = []
    for _ in which:
        carried.append(refs[pos] if has_in else None)
        pos += 1 if has_in else 0
    outs = refs[pos : pos + len(which)]
    own, sem = refs[pos + len(which) :]
    y = lax.axis_index(Y)
    ztiles = tiles_of(group)
    copies = [
        pltpu.make_async_copy(w_ref.at[:, pl.ds(column(ztiles[ti], y), TILE)], own.at[n], sem.at[n])
        for n, ti in enumerate(which)
    ]
    for copy in copies:
        copy.start()
    lhs = jnp.concatenate([peer[0:ROWS, :] for peer in peers], axis=1)
    for n, ti in enumerate(which):
        rows = slice(base + ti * TILE, base + (ti + 1) * TILE)
        rhs = jnp.concatenate([block[rows, :] for block in blocks], axis=0)
        total = jnp.dot(lhs, rhs, preferred_element_type=F32)
        copies[n].wait()
        total = total + jnp.dot(x_ref[...], own[n], preferred_element_type=F32)
        if carried[n] is not None:
            total = total + carried[n][...].astype(F32)
        outs[n][...] = total.astype(outs[n].dtype)


def project(group, which, weight, features, first_got, got, carried, after=(), out_dtype=BF16):
    half = (ROWS, WIDTH)
    in_specs = [HBM, whole(half)] + [whole((2 * ROWS, TILE))] * 3
    args = [weight, features, *first_got]
    if group:
        in_specs += [whole((2 * TILE, TILE))] * 3
        args += list(got)
    in_specs += [whole(half)] * len(carried)
    args += list(carried)
    n = len(which)
    return call(
        functools.partial(project_kernel, group, which, bool(carried)),
        args,
        in_specs,
        [shape((ROWS, TILE), out_dtype)] * n,
        [whole((ROWS, TILE))] * n,
        [pltpu.VMEM((n, TILE, TILE), BF16), pltpu.SemaphoreType.DMA((n,))],
        (2 * ROWS * 1024 * TILE * n, 2 << 20),
        "project",
        8,
        after,
    )


def window_start(ids, owner):
    before = jnp.sum((ids < owner * VARS).astype(jnp.int32))
    return jnp.minimum(before, ROWS - WINDOW)


def dispatch_kernel(ids_ref, x_ref, *outs):
    me = lax.axis_index("pool")
    ids = ids_ref[...]
    features = x_ref[...]
    for k in range(NX):
        owner = lax.rem(me + k, NX)
        start = window_start(ids, owner)
        at = lax.broadcasted_iota(jnp.int32, (WINDOW, ROWS), 0) + start
        hot = (at == lax.broadcasted_iota(jnp.int32, (WINDOW, ROWS), 1)).astype(F32).astype(BF16)
        outs[k][0:WINDOW, :] = jnp.dot(hot, features, preferred_element_type=F32).astype(BF16)
        local = jnp.broadcast_to((ids - owner * VARS).astype(F32), (IDROWS, ROWS)).astype(BF16)
        outs[k][WINDOW : WINDOW + IDROWS, :] = lax.dot_general(
            local, hot, (((1,), (1,)), ((), ())), preferred_element_type=F32
        ).astype(BF16)


def dispatch(ids, features, after=()):
    return call(
        dispatch_kernel,
        (ids, features),
        [whole((1, ROWS)), whole((ROWS, WIDTH))],
        [shape((WINDOW + IDROWS, WIDTH))] * NX,
        [whole((WINDOW + IDROWS, WIDTH))] * NX,
        [],
        (2 * 1024 * 512 * 256, 1 << 20),
        "dispatch",
        6,
        after,
    )


def variant_columns(item_ref, lanes):
    row = jnp.broadcast_to(item_ref[WINDOW : WINDOW + 1, :].astype(F32), (WINDOW, WINDOW))
    diagonal = lax.broadcasted_iota(jnp.int32, (WINDOW, WINDOW), 0) == lax.broadcasted_iota(
        jnp.int32, (WINDOW, WINDOW), 1
    )
    spread = jnp.where(diagonal, row, 0.0).astype(BF16)
    return jnp.dot(spread, jnp.ones((WINDOW, lanes), BF16), preferred_element_type=F32)


def down_kernel(i0, i1, i2, i3, down_ref, out_ref, var_ref, acc_ref):
    items = (i0, i1, i2, i3)
    for k in range(NX):
        var_ref[k] = variant_columns(items[k], 256)
        acc_ref[k] = jnp.zeros((WINDOW, 256), F32)
    lane = lax.broadcasted_iota(jnp.int32, (1, 256), 1)
    part = lax.div(lane, jnp.int32(RANK)).astype(F32)

    def step(j, carry):
        factor = down_ref[pl.ds(pl.multiple_of(j * 256, 256), 256), :]
        wanted = part + (j * 4).astype(F32)
        for k in range(NX):
            value = lax.dot_general(
                items[k][0:WINDOW, :],
                factor,
                (((1,), (1,)), ((), ())),
                preferred_element_type=F32,
            )
            acc_ref[k] += jnp.where(var_ref[k] == wanted, value, 0.0)
        return carry

    lax.fori_loop(0, VARS * RANK // 256, step, 0)
    folded = []
    for k in range(NX):
        two = acc_ref[k, :, 0:128] + acc_ref[k, :, 128:256]
        folded.append(two + pltpu.roll(two, RANK, 1))
    low = lax.broadcasted_iota(jnp.int32, (WINDOW, 128), 1) < RANK
    for h in range(2):
        packed = jnp.where(low, folded[h], folded[h + 2]).astype(BF16)
        out_ref[h * WINDOW : (h + 1) * WINDOW, :] = packed


def down(items, factor, after=()):
    return call(
        down_kernel,
        (*items, factor),
        [whole((WINDOW + IDROWS, WIDTH))] * NX + [whole((VARS * RANK, WIDTH))],
        shape((512, 128)),
        whole((512, 128)),
        [pltpu.VMEM((NX, WINDOW, 256), F32), pltpu.VMEM((NX, WINDOW, 256), F32)],
        (2 * 1024 * 256 * 2048, 2 << 20),
        "down",
        8,
        after,
    )


def block_kernel(i0, i1, i2, i3, mats_ref, place_ref, out_ref, var_ref, rhs_ref):
    items = (i0, i1, i2, i3)
    shard = lax.axis_index(Z) * NY + lax.axis_index(Y)
    for k in range(NX):
        var_ref[k] = variant_columns(items[k], 128)
        out_ref[k] = jnp.zeros((WINDOW, 256), F32)

    def lanes_of(v):
        return pl.ds(pl.multiple_of((place_ref[v] - shard * 2) * BLK, BLK), BLK)

    def fill(v, carry):
        rhs_ref[v] = jnp.zeros((BLK, 256), BF16)
        rhs_ref[v, :, lanes_of(v)] = mats_ref[v]
        return carry

    lax.fori_loop(0, VARS, fill, 0)

    def step(c, carry):
        rhs = rhs_ref[pl.ds(c * 4, 4)].reshape(4 * BLK, 256)
        for k in range(NX):
            pieces = []
            for i in range(4):
                v = c * 4 + i
                piece = items[k][0:WINDOW, lanes_of(v)].astype(F32)
                pieces.append(jnp.where(var_ref[k] == v.astype(F32), piece, 0.0).astype(BF16))
            lhs = jnp.concatenate(pieces, axis=1)
            out_ref[k] += jnp.dot(lhs, rhs, preferred_element_type=F32)
        return carry

    lax.fori_loop(0, VARS // 4, step, 0)


def block_terms(items, mats, places, after=()):
    return call(
        block_kernel,
        (*items, mats, places),
        [whole((WINDOW + IDROWS, WIDTH))] * NX + [whole((VARS, BLK, BLK)), SMEM],
        shape((NX, WINDOW, 256), F32),
        whole((NX, WINDOW, 256)),
        [pltpu.VMEM((NX, WINDOW, 128), F32), pltpu.VMEM((VARS, BLK, 256), BF16)],
        (2 * 1024 * 4096 * 256, 3 << 20),
        "blocks",
        10,
        after,
    )


def add_kernel(a_ref, b_ref, out_ref):
    out_ref[...] = (a_ref[...].astype(F32) + b_ref[...].astype(F32)).astype(BF16)


def exchanged_sum(value, axis, bit, after=()):
    count = lax.axis_size(axis)
    other = lax.ppermute(value, axis, [(i, i ^ bit) for i in range(count)])
    return call(
        add_kernel,
        (value, other),
        [whole((512, 128))] * 2,
        shape((512, 128)),
        whole((512, 128)),
        [],
        (1 << 16, 3 << 17),
        "add",
        2,
        after,
    )


def up_kernel(i0, i1, i2, i3, low_ref, up_ref, block_ref, o0, o1, o2, o3, acc_ref, var_ref, two_ref):
    items, outs = (i0, i1, i2, i3), (o0, o1, o2, o3)
    first = lax.broadcasted_iota(jnp.int32, (WINDOW, 128), 1) < RANK
    for h in range(2):
        packed = low_ref[h * WINDOW : (h + 1) * WINDOW, :].astype(F32)
        turned = pltpu.roll(packed, RANK, 1)
        two_ref[h] = jnp.where(first, packed, turned)
        two_ref[h + 2] = jnp.where(first, turned, packed)
    for k in range(NX):
        var_ref[k] = variant_columns(items[k], 128)
        acc_ref[k] = block_ref[k]
    half = lax.div(lax.broadcasted_iota(jnp.int32, (1, 128), 1), jnp.int32(RANK)).astype(F32)

    def step(c, carry):
        rhs = up_ref[pl.ds(pl.multiple_of(c * 512, 512), 512), :]
        for k in range(NX):
            pieces = []
            for i in range(4):
                wanted = half + (c * 8 + i * 2).astype(F32)
                pieces.append(jnp.where(var_ref[k] == wanted, two_ref[k], 0.0).astype(BF16))
            lhs = jnp.concatenate(pieces, axis=1)
            acc_ref[k] += jnp.dot(lhs, rhs, preferred_element_type=F32)
        return carry

    lax.fori_loop(0, VARS * RANK // 512, step, 0)
    for k in range(NX):
        outs[k][...] = acc_ref[k].astype(BF16)


def up(items, lowrank, factor, blocks, after=()):
    return call(
        up_kernel,
        (*items, lowrank, factor, blocks),
        [whole((WINDOW + IDROWS, WIDTH))] * NX + [whole((512, 128)), whole((VARS * RANK, WIDTH)), whole((NX, WINDOW, 256))],
        [shape((WINDOW, WIDTH))] * NX,
        [whole((WINDOW, WIDTH))] * NX,
        [pltpu.VMEM((NX, WINDOW, 256), F32), pltpu.VMEM((NX, WINDOW, 128), F32), pltpu.VMEM((NX, WINDOW, 128), F32)],
        (2 * 1024 * 256 * 2048, 3 << 20),
        "up",
        10,
        after,
    )


def combine_kernel(ids_ref, h_ref, own_ref, plus_ref, r0, r1, r2, r3, first_ref, branch_ref):
    me = lax.axis_index("pool")
    ids = ids_ref[...]
    branch = own_ref[...] + plus_ref[...].astype(F32)
    delta = None
    for k, back in enumerate((r0, r1, r2, r3)):
        start = window_start(ids, lax.rem(me + k, NX))
        at = lax.broadcasted_iota(jnp.int32, (ROWS, WINDOW), 1) + start
        hot = (at == lax.broadcasted_iota(jnp.int32, (ROWS, WINDOW), 0)).astype(F32).astype(BF16)
        part = jnp.dot(hot, back[...], preferred_element_type=F32)
        delta = part if delta is None else delta + part
    branch = branch + delta
    branch_ref[...] = branch
    first_ref[...] = (h_ref[...].astype(F32) + branch).astype(BF16)


def combine(ids, hidden, own, plus, returned, after=()):
    half = (ROWS, WIDTH)
    return call(
        combine_kernel,
        (ids, hidden, own, plus, *returned),
        [whole((1, ROWS))] + [whole(half)] * 3 + [whole((WINDOW, WIDTH))] * NX,
        [shape(half), shape(half, F32)],
        [whole(half)] * 2,
        [],
        (2 * 512 * 1024 * 256, 2 << 20),
        "combine",
        8,
        after,
    )


def per_device(
    hidden_input,
    attention_output,
    projection_weight,
    lowrank_down_factor,
    lowrank_up_factor,
    residual_block_mats,
    diagonal_block_index,
    row_variant_index,
):
    features = attention_output[0]
    weight = projection_weight[0]
    down_factor = lowrank_down_factor[0].reshape(VARS * RANK, WIDTH)
    up_factor = lowrank_up_factor[0].reshape(VARS * RANK, WIDTH)
    mats = residual_block_mats[0][:, 0]
    places = diagonal_block_index[0][:, 0]
    ids = row_variant_index.reshape(1, ROWS)

    first = pack((0,), weight, features)
    first_got = [shift(value, Y, hop) for value, hop in zip(first, HOPS)]
    sent = dispatch(ids, features, (first[0],))
    items = [sent[0]] + [shift(sent[k], "pool", k) for k in (1, 2, 3)]
    low = down(items, down_factor)
    low1 = exchanged_sum(low, Z, 1)
    later = pack((1, 2, 3), weight, None, (low,))
    got = [[shift(later[g * 3 + ki], Y, hop) for ki, hop in enumerate(HOPS)] for g in range(3)]
    blocks = block_terms(items, mats, places, (low1,))
    low2 = exchanged_sum(low1, Z, 2, (blocks,))

    plus, minus = project(0, (0, 1), weight, features, first_got, None, (), (low2,))
    carried = (shift(plus, Z, 1), shift(minus, Z, -1))
    low3 = exchanged_sum(low2, Z, 4, (plus,))
    plus, minus = project(1, (0, 1), weight, features, first_got, got[0], carried, (low3,))
    carried = (shift(plus, Z, 1), shift(minus, Z, -1))
    low4 = exchanged_sum(low3, Y, 1, (plus,))
    plus, minus = project(2, (0, 1), weight, features, first_got, got[1], carried, (low4,))
    carried = (shift(plus, Z, 1), shift(minus, Z, -1))
    low5 = exchanged_sum(low4, Y, 2, (plus,))
    served = up(items, low5, up_factor, blocks)
    returned = [served[0]] + [shift(served[k], "pool", -k) for k in (1, 2, 3)]
    (plus,) = project(3, (0,), weight, features, first_got, got[2], carried[:1], (served[1],))
    arrived = shift(plus, Z, 1)
    (own,) = project(
        3, (1,), weight, features, first_got, got[2], carried[1:], (plus,), F32
    )
    plus = arrived

    first_out, branch = combine(ids, hidden_input, own, plus, returned)
    carried = lax.ppermute(first_out, "section", [(0, 1)])
    begin = jnp.where(lax.axis_index("section") == 0, hidden_input, carried)
    return (begin.astype(F32) + branch).astype(BF16)[None]


def solution(mesh):
    finer = Mesh(
        mesh.devices.reshape(mesh.shape["pool"], mesh.shape["section"], NZ, NY),
        ("pool", "section", Z, Y),
    )
    placed = (
        P("pool", TENSOR),
        P("section", "pool", TENSOR),
        P("section", TENSOR, None),
        P("section", "pool", None, TENSOR),
        P("section", "pool", None, TENSOR),
        P("section", "pool", TENSOR, None, None),
        P("section", "pool", TENSOR),
        P("pool"),
    )
    return jax.shard_map(
        per_device,
        mesh=finer,
        in_specs=placed,
        out_specs=P("section", "pool", TENSOR),
        check_vma=False,
    )
```

```python
import functools

import jax
import jax.numpy as jnp
from jax import lax
from jax.experimental import pallas as pl
from jax.experimental.pallas import tpu as pltpu
from jax.sharding import Mesh
from jax.sharding import PartitionSpec as P


Z, Y = "tensor_0", "tensor_1"
TENSOR = (Z, Y)
NZ, NY, NX = 8, 4, 4
ROWS, WIDTH, TILE = 512, 256, 256
WINDOW = 256
IDROWS = 16
VARS, RANK, BLK = 32, 64, 128
HOPS = (1, 3, 2)
F32, BF16 = jnp.float32, jnp.bfloat16
ANY = pl.BlockSpec(memory_space=pl.ANY)
HBM = pl.BlockSpec(memory_space=pltpu.HBM)
SMEM = pl.BlockSpec(memory_space=pltpu.SMEM)


def shift(value, axis, steps):
    count = lax.axis_size(axis)
    return lax.ppermute(value, axis, [(i, (i + steps) % count) for i in range(count)])


def cost(flops, nbytes):
    return pl.CostEstimate(flops=flops, bytes_accessed=nbytes, transcendentals=0)


def shape(dims, dtype=BF16):
    return pltpu.VMEM(dims, dtype)


def whole(dims, at=None):
    at = at or (0,) * len(dims)
    return pl.BlockSpec(dims, lambda: at)


def tiles_of(group):
    z = lax.axis_index(Z)
    return lax.rem(z + (4 - group), NZ), lax.rem(z + (group + NZ - 3), NZ)


def column(ztile, ytile):
    return pl.multiple_of((ztile * NY + ytile) * TILE, TILE)


def placed(value, spec):
    space = pltpu.HBM if spec is HBM else pltpu.VMEM
    if spec is SMEM:
        return value
    return pltpu.with_memory_space_constraint(value, space)


def call(kernel, args, in_specs, outs, out_specs, scratch, work, limit, after=()):
    n, m = len(args), len(after)
    args = [placed(arg, spec) for arg, spec in zip(args, in_specs)]

    def body(*refs):
        kernel(*refs[:n], *refs[n + m :])

    return pl.pallas_call(
        body,
        out_shape=outs,
        in_specs=list(in_specs) + [ANY] * m,
        out_specs=out_specs,
        scratch_shapes=scratch,
        cost_estimate=cost(*work),
        compiler_params=pltpu.CompilerParams(vmem_limit_bytes=limit << 20),
    )(*args, *after)


def pack_kernel(groups, ahead, extra, *refs):
    w_ref = refs[0]
    n_in = 1 + bool(ahead or extra)
    outs = refs[n_in : n_in + 4 * len(groups)]
    sems = refs[-1]
    y = lax.axis_index(Y)
    copies = []
    for gi, group in enumerate(groups):
        for ki, hop in enumerate((0,) + HOPS):
            out = outs[gi * 4 + ki]
            before = ahead if hop else 0
            if before:
                copies.append((refs[1], out.at[pl.ds(0, ROWS), :]))
            for ti, ztile in enumerate(tiles_of(group)):
                col = column(ztile, lax.rem(y + hop, NY))
                first = ti * TILE + before
                copies.append((w_ref.at[:, pl.ds(col, TILE)], out.at[pl.ds(first, TILE), :]))
    copies = [
        pltpu.make_async_copy(source, target, sems.at[i])
        for i, (source, target) in enumerate(copies)
    ]
    for copy in copies:
        copy.start()
    if extra:
        for ki in range(1, 4):
            outs[ki][2 * TILE : 2 * TILE + extra, :] = refs[1][...]
    for copy in copies:
        copy.wait()


def pack(groups, weight, features=None, low=None, after=()):
    ahead = 0 if features is None else ROWS
    extra = 0 if low is None else WINDOW
    rows = 2 * TILE + ahead + extra
    args, specs = [weight], [HBM]
    if ahead:
        args.append(features)
        specs.append(HBM)
    if extra:
        args.append(low)
        specs.append(whole((WINDOW, 256)))
    dims = [(2 * TILE, TILE)] + [(rows, TILE)] * 3
    dims = dims * len(groups)
    return call(
        functools.partial(pack_kernel, groups, ahead, extra),
        args,
        specs,
        [shape(d) for d in dims],
        [whole(d) for d in dims],
        [pltpu.SemaphoreType.DMA((len(groups) * 12,))],
        (0, 8 * len(groups) * rows * TILE),
        8,
        after,
    )


def project_kernel(group, which, has_in, *refs):
    own_ref, x_ref = refs[:2]
    peers = refs[2:5]
    pos = 5
    blocks = peers
    if group:
        blocks = refs[5:8]
        pos = 8
    base = 0 if group else ROWS
    carried = []
    for _ in which:
        carried.append(refs[pos] if has_in else None)
        pos += 1 if has_in else 0
    outs = refs[pos : pos + len(which)]
    rhs = []
    for ti in which:
        rows = slice(base + ti * TILE, base + (ti + 1) * TILE)
        mine = own_ref[ti * TILE : (ti + 1) * TILE, :]
        rhs.append(jnp.concatenate([mine] + [block[rows, :] for block in blocks], axis=0))
    lhs = jnp.concatenate([x_ref[...]] + [peer[0:ROWS, :] for peer in peers], axis=1)
    for n in range(len(which)):
        total = jnp.dot(lhs, rhs[n], preferred_element_type=F32)
        if has_in:
            total = total + carried[n][...].astype(F32)
        outs[n][...] = total.astype(outs[n].dtype)


def project(group, which, own, features, first_got, got, carried, after=(), out_dtype=BF16):
    half = (ROWS, WIDTH)
    in_specs = [whole((2 * TILE, TILE)), whole(half)] + [whole((2 * ROWS, TILE))] * 3
    args = [own, features, *first_got]
    if group:
        in_specs += [whole(got[0].shape)] * 3
        args += list(got)
    in_specs += [whole(half)] * len(carried)
    args += list(carried)
    n = len(which)
    return call(
        functools.partial(project_kernel, group, which, bool(carried)),
        args,
        in_specs,
        [shape((ROWS, TILE), out_dtype)] * n,
        [whole((ROWS, TILE))] * n,
        [],
        (2 * ROWS * 1024 * TILE * n, 2 << 20),
        8,
        after,
    )


def window_start(ids, owner):
    before = jnp.sum((ids < owner * VARS).astype(jnp.int32))
    return jnp.minimum(before, ROWS - WINDOW)


def dispatch_kernel(ids_ref, x_ref, *outs):
    me = lax.axis_index("pool")
    ids = ids_ref[...]
    features = x_ref[...]
    for k in range(NX):
        owner = lax.rem(me + k, NX)
        start = window_start(ids, owner)
        at = lax.broadcasted_iota(jnp.int32, (WINDOW, ROWS), 0) + start
        hot = (at == lax.broadcasted_iota(jnp.int32, (WINDOW, ROWS), 1)).astype(F32).astype(BF16)
        outs[k][0:WINDOW, :] = jnp.dot(hot, features, preferred_element_type=F32).astype(BF16)
        local = jnp.broadcast_to((ids - owner * VARS).astype(F32), (IDROWS, ROWS)).astype(BF16)
        outs[k][WINDOW : WINDOW + IDROWS, :] = lax.dot_general(
            local, hot, (((1,), (1,)), ((), ())), preferred_element_type=F32
        ).astype(BF16)


def dispatch(ids, features, after=()):
    return call(
        dispatch_kernel,
        (ids, features),
        [whole((1, ROWS)), whole((ROWS, WIDTH))],
        [shape((WINDOW + IDROWS, WIDTH))] * NX,
        [whole((WINDOW + IDROWS, WIDTH))] * NX,
        [],
        (2 * 1024 * 512 * 256, 1 << 20),
        6,
        after,
    )


def variant_columns(item_ref, lanes):
    row = jnp.broadcast_to(item_ref[WINDOW : WINDOW + 1, :].astype(F32), (WINDOW, WINDOW))
    diagonal = lax.broadcasted_iota(jnp.int32, (WINDOW, WINDOW), 0) == lax.broadcasted_iota(
        jnp.int32, (WINDOW, WINDOW), 1
    )
    spread = jnp.where(diagonal, row, 0.0).astype(BF16)
    return jnp.dot(spread, jnp.ones((WINDOW, lanes), BF16), preferred_element_type=F32)


def down_kernel(i0, i1, i2, i3, down_ref, out_ref, var_ref, acc_ref):
    items = (i0, i1, i2, i3)
    for k in range(NX):
        var_ref[k] = variant_columns(items[k], 256)
        acc_ref[k] = jnp.zeros((WINDOW, 256), F32)
    lane = lax.broadcasted_iota(jnp.int32, (1, 256), 1)
    part = lax.div(lane, jnp.int32(RANK)).astype(F32)

    def step(j, carry):
        factor = down_ref[pl.ds(pl.multiple_of(j * 256, 256), 256), :]
        wanted = part + (j * 4).astype(F32)
        for k in range(NX):
            value = lax.dot_general(
                items[k][0:WINDOW, :],
                factor,
                (((1,), (1,)), ((), ())),
                preferred_element_type=F32,
            )
            acc_ref[k] += jnp.where(var_ref[k] == wanted, value, 0.0)
        return carry

    lax.fori_loop(0, VARS * RANK // 256, step, 0)
    folded = []
    for k in range(NX):
        two = acc_ref[k, :, 0:128] + acc_ref[k, :, 128:256]
        folded.append(two + pltpu.roll(two, RANK, 1))
    low = lax.broadcasted_iota(jnp.int32, (WINDOW, 128), 1) < RANK
    for h in range(2):
        packed = jnp.where(low, folded[h], folded[h + 2]).astype(BF16)
        out_ref[:, h * 128 : (h + 1) * 128] = packed


def down(items, factor, after=()):
    return call(
        down_kernel,
        (*items, factor),
        [whole((WINDOW + IDROWS, WIDTH))] * NX + [whole((VARS * RANK, WIDTH))],
        shape((WINDOW, 256)),
        whole((WINDOW, 256)),
        [pltpu.VMEM((NX, WINDOW, 256), F32), pltpu.VMEM((NX, WINDOW, 256), F32)],
        (2 * 1024 * 256 * 2048, 2 << 20),
        8,
        after,
    )


def block_kernel(i0, i1, i2, i3, mats_ref, place_ref, out_ref, var_ref, rhs_ref):
    items = (i0, i1, i2, i3)
    shard = lax.axis_index(Z) * NY + lax.axis_index(Y)
    for k in range(NX):
        var_ref[k] = variant_columns(items[k], 128)
        out_ref[k] = jnp.zeros((WINDOW, 256), F32)

    def lanes_of(v):
        return pl.ds(pl.multiple_of((place_ref[v] - shard * 2) * BLK, BLK), BLK)

    def fill(v, carry):
        rhs_ref[v] = jnp.zeros((BLK, 256), BF16)
        rhs_ref[v, :, lanes_of(v)] = mats_ref[v]
        return carry

    lax.fori_loop(0, VARS, fill, 0)

    def step(c, carry):
        rhs = rhs_ref[pl.ds(c * 4, 4)].reshape(4 * BLK, 256)
        for k in range(NX):
            pieces = []
            for i in range(4):
                v = c * 4 + i
                piece = items[k][0:WINDOW, lanes_of(v)].astype(F32)
                pieces.append(jnp.where(var_ref[k] == v.astype(F32), piece, 0.0).astype(BF16))
            lhs = jnp.concatenate(pieces, axis=1)
            out_ref[k] += jnp.dot(lhs, rhs, preferred_element_type=F32)
        return carry

    lax.fori_loop(0, VARS // 4, step, 0)


def block_terms(items, mats, places, after=()):
    return call(
        block_kernel,
        (*items, mats, places),
        [whole((WINDOW + IDROWS, WIDTH))] * NX + [whole((VARS, BLK, BLK)), SMEM],
        shape((NX, WINDOW, 256), F32),
        whole((NX, WINDOW, 256)),
        [pltpu.VMEM((NX, WINDOW, 128), F32), pltpu.VMEM((VARS, BLK, 256), BF16)],
        (2 * 1024 * 4096 * 256, 3 << 20),
        10,
        after,
    )


def add_kernel(a_ref, b_ref, out_ref):
    out_ref[...] = (a_ref[...].astype(F32) + b_ref[...].astype(F32)).astype(BF16)


def exchanged_sum(value, axis, bit, after=()):
    count = lax.axis_size(axis)
    other = lax.ppermute(value, axis, [(i, i ^ bit) for i in range(count)])
    return call(
        add_kernel,
        (value, other),
        [whole((WINDOW, 256))] * 2,
        shape((WINDOW, 256)),
        whole((WINDOW, 256)),
        [],
        (1 << 16, 3 << 17),
        2,
        after,
    )


def up_kernel(*refs):
    items, lows = refs[:4], refs[4:8]
    up_ref, block_ref = refs[8:10]
    outs = refs[10:14]
    acc_ref, var_ref, two_ref = refs[14:]
    low = lows[0][...].astype(F32)
    for other in lows[1:]:
        low = low + other[2 * TILE : 2 * TILE + WINDOW, :].astype(F32)
    low = low.astype(BF16).astype(F32)
    first = lax.broadcasted_iota(jnp.int32, (WINDOW, 128), 1) < RANK
    for h in range(2):
        packed = low[:, h * 128 : (h + 1) * 128]
        turned = pltpu.roll(packed, RANK, 1)
        two_ref[h] = jnp.where(first, packed, turned)
        two_ref[h + 2] = jnp.where(first, turned, packed)
    for k in range(NX):
        var_ref[k] = variant_columns(items[k], 128)
        acc_ref[k] = block_ref[k]
    half = lax.div(lax.broadcasted_iota(jnp.int32, (1, 128), 1), jnp.int32(RANK)).astype(F32)

    def step(c, carry):
        rhs = up_ref[pl.ds(pl.multiple_of(c * 512, 512), 512), :]
        for k in range(NX):
            pieces = []
            for i in range(4):
                wanted = half + (c * 8 + i * 2).astype(F32)
                pieces.append(jnp.where(var_ref[k] == wanted, two_ref[k], 0.0).astype(BF16))
            lhs = jnp.concatenate(pieces, axis=1)
            acc_ref[k] += jnp.dot(lhs, rhs, preferred_element_type=F32)
        return carry

    lax.fori_loop(0, VARS * RANK // 512, step, 0)
    for k in range(NX):
        outs[k][...] = acc_ref[k].astype(BF16)


def up(items, low, lows, factor, blocks, after=()):
    return call(
        up_kernel,
        (*items, low, *lows, factor, blocks),
        [whole((WINDOW + IDROWS, WIDTH))] * NX
        + [whole((WINDOW, 256))]
        + [whole(lows[0].shape)] * 3
        + [whole((VARS * RANK, WIDTH)), whole((NX, WINDOW, 256))],
        [shape((WINDOW, WIDTH))] * NX,
        [whole((WINDOW, WIDTH))] * NX,
        [pltpu.VMEM((NX, WINDOW, 256), F32), pltpu.VMEM((NX, WINDOW, 128), F32), pltpu.VMEM((NX, WINDOW, 128), F32)],
        (2 * 1024 * 256 * 2048, 3 << 20),
        10,
        after,
    )


def combine_kernel(ids_ref, h_ref, own_ref, plus_ref, r0, r1, r2, r3, first_ref, branch_ref):
    me = lax.axis_index("pool")
    ids = ids_ref[...]
    branch = own_ref[...] + plus_ref[...].astype(F32)
    delta = None
    for k, back in enumerate((r0, r1, r2, r3)):
        start = window_start(ids, lax.rem(me + k, NX))
        at = lax.broadcasted_iota(jnp.int32, (ROWS, WINDOW), 1) + start
        hot = (at == lax.broadcasted_iota(jnp.int32, (ROWS, WINDOW), 0)).astype(F32).astype(BF16)
        part = jnp.dot(hot, back[...], preferred_element_type=F32)
        delta = part if delta is None else delta + part
    branch = branch + delta
    branch_ref[...] = branch
    first_ref[...] = (h_ref[...].astype(F32) + branch).astype(BF16)


def combine(ids, hidden, own, plus, returned, after=()):
    half = (ROWS, WIDTH)
    return call(
        combine_kernel,
        (ids, hidden, own, plus, *returned),
        [whole((1, ROWS))] + [whole(half)] * 3 + [whole((WINDOW, WIDTH))] * NX,
        [shape(half), shape(half, F32)],
        [whole(half)] * 2,
        [],
        (2 * 512 * 1024 * 256, 2 << 20),
        8,
        after,
    )


def steps(
    hidden_input,
    attention_output,
    projection_weight,
    lowrank_down_factor,
    lowrank_up_factor,
    residual_block_mats,
    diagonal_block_index,
    row_variant_index,
):
    features = attention_output[0]
    weight = projection_weight[0]
    down_factor = lowrank_down_factor[0].reshape(VARS * RANK, WIDTH)
    up_factor = lowrank_up_factor[0].reshape(VARS * RANK, WIDTH)
    mats = residual_block_mats[0][:, 0]
    places = diagonal_block_index[0][:, 0]
    ids = row_variant_index.reshape(1, ROWS)

    own0, *first = pack((0,), weight, features)
    first_got = [shift(value, Y, hop) for value, hop in zip(first, HOPS)]
    sent = dispatch(ids, features, (first[0],))
    items = [sent[0]] + [shift(sent[k], "pool", k) for k in (1, 2, 3)]
    own1, *second = pack((1,), weight, None, None, (sent[0],))
    got1 = [shift(value, Y, hop) for value, hop in zip(second, HOPS)]
    low = down(items, down_factor)
    low1 = exchanged_sum(low, Z, 1)
    blocks = block_terms(items, mats, places, (low,))
    low2 = exchanged_sum(low1, Z, 2, (blocks,))
    low3 = exchanged_sum(low2, Z, 4)

    plus, minus = project(0, (0, 1), own0, features, first_got, None, (), (low2,))
    carried = (shift(plus, Z, 1), shift(minus, Z, -1))
    own2, *third = pack((2,), weight, None, low3)
    got2 = [shift(value, Y, hop) for value, hop in zip(third, HOPS)]
    own3, *fourth = pack((3,), weight, None, None, (third[0],))
    got3 = [shift(value, Y, hop) for value, hop in zip(fourth, HOPS)]
    plus, minus = project(1, (0, 1), own1, features, first_got, got1, carried)
    carried = (shift(plus, Z, 1), shift(minus, Z, -1))
    plus, minus = project(2, (0, 1), own2, features, first_got, got2, carried)
    carried = (shift(plus, Z, 1), shift(minus, Z, -1))
    served = up(items, low3, got2, up_factor, blocks, (plus,))
    returned = [served[0]] + [shift(served[k], "pool", -k) for k in (1, 2, 3)]
    (plus,) = project(3, (0,), own3, features, first_got, got3, carried[:1], (served[1],))
    arrived = shift(plus, Z, 1)
    (own,) = project(3, (1,), own3, features, first_got, got3, carried[1:], (plus,), F32)
    plus = arrived

    first_out, branch = combine(ids, hidden_input, own, plus, returned)
    carried = lax.ppermute(first_out, "section", [(0, 1)])
    begin = jnp.where(lax.axis_index("section") == 0, hidden_input, carried)
    return (begin.astype(F32) + branch).astype(BF16)[None]


def solution(mesh):
    finer = Mesh(
        mesh.devices.reshape(mesh.shape["pool"], mesh.shape["section"], NZ, NY),
        ("pool", "section", Z, Y),
    )
    placed = (
        P("pool", TENSOR),
        P("section", "pool", TENSOR),
        P("section", TENSOR, None),
        P("section", "pool", None, TENSOR),
        P("section", "pool", None, TENSOR),
        P("section", "pool", TENSOR, None, None),
        P("section", "pool", TENSOR),
        P("pool"),
    )
    return jax.shard_map(
        steps,
        mesh=finer,
        in_specs=placed,
        out_specs=P("section", "pool", TENSOR),
        check_vma=False,
    )
```

```python
import functools

import jax
import jax.numpy as jnp
from jax import lax
from jax.experimental import pallas as pl
from jax.experimental.pallas import tpu as pltpu
from jax.sharding import Mesh
from jax.sharding import PartitionSpec as P


Z, Y = "tensor_0", "tensor_1"
TENSOR = (Z, Y)
NZ, NY, NX = 8, 4, 4
ROWS, WIDTH, TILE = 512, 256, 256
WINDOW = 256
IDROWS = 16
VARS, RANK, BLK = 32, 64, 128
HOPS = (1, 3, 2)
F32, BF16 = jnp.float32, jnp.bfloat16
ANY = pl.BlockSpec(memory_space=pl.ANY)
HBM = pl.BlockSpec(memory_space=pltpu.HBM)
SMEM = pl.BlockSpec(memory_space=pltpu.SMEM)


def shift(value, axis, steps):
    count = lax.axis_size(axis)
    return lax.ppermute(value, axis, [(i, (i + steps) % count) for i in range(count)])


def cost(flops, nbytes):
    return pl.CostEstimate(flops=flops, bytes_accessed=nbytes, transcendentals=0)


def shape(dims, dtype=BF16):
    return pltpu.VMEM(dims, dtype)


def whole(dims, at=None):
    at = at or (0,) * len(dims)
    return pl.BlockSpec(dims, lambda: at)


def tiles_of(group):
    z = lax.axis_index(Z)
    return lax.rem(z + (4 - group), NZ), lax.rem(z + (group + NZ - 3), NZ)


def column(ztile, ytile):
    return pl.multiple_of((ztile * NY + ytile) * TILE, TILE)


def placed(value, spec):
    space = pltpu.HBM if spec is HBM else pltpu.VMEM
    if spec is SMEM:
        return value
    return pltpu.with_memory_space_constraint(value, space)


def call(kernel, args, in_specs, outs, out_specs, scratch, work, limit, after=()):
    n, m = len(args), len(after)
    args = [placed(arg, spec) for arg, spec in zip(args, in_specs)]

    def body(*refs):
        kernel(*refs[:n], *refs[n + m :])

    return pl.pallas_call(
        body,
        out_shape=outs,
        in_specs=list(in_specs) + [ANY] * m,
        out_specs=out_specs,
        scratch_shapes=scratch,
        cost_estimate=cost(*work),
        compiler_params=pltpu.CompilerParams(vmem_limit_bytes=limit << 20),
    )(*args, *after)


def parity():
    return lax.rem(lax.axis_index("pool"), 2)


def pack_kernel(groups, ahead, *refs):
    w_ref = refs[0]
    n_in = 2 if ahead else 1
    outs = refs[n_in : n_in + 3]
    owns = refs[n_in + 3 : n_in + 3 + len(groups)]
    sems = refs[-1]
    y, odd = lax.axis_index(Y), parity()
    copies = []
    for gi, group in enumerate(groups):
        plus, minus = tiles_of(group)
        mine = plus * (1 - odd) + minus * odd
        for ki, hop in enumerate(HOPS):
            if ahead and gi == 0:
                copies.append((refs[1], outs[ki].at[pl.ds(0, ROWS), :]))
            source = w_ref.at[:, pl.ds(column(mine, lax.rem(y + hop, NY)), TILE)]
            copies.append((source, outs[ki].at[pl.ds(ahead + gi * TILE, TILE), :]))
    for gi, group in enumerate(groups):
        for ti, ztile in enumerate(tiles_of(group)):
            source = w_ref.at[:, pl.ds(column(ztile, y), TILE)]
            copies.append((source, owns[gi].at[pl.ds(ti * TILE, TILE), :]))
    copies = [
        pltpu.make_async_copy(source, target, sems.at[i])
        for i, (source, target) in enumerate(copies)
    ]
    for copy in copies:
        copy.start()
    for copy in copies:
        copy.wait()


def pack(groups, weight, features=None, after=()):
    ahead = 0 if features is None else ROWS
    args, specs = [weight], [HBM]
    if ahead:
        args.append(features)
        specs.append(HBM)
    rows = ahead + len(groups) * TILE
    dims = [(rows, TILE)] * 3 + [(2 * TILE, TILE)] * len(groups)
    got = call(
        functools.partial(pack_kernel, groups, ahead),
        args,
        specs,
        [shape(d) for d in dims],
        [whole(d) for d in dims],
        [pltpu.SemaphoreType.DMA((3 + 5 * len(groups),))],
        (0, 6 * rows * TILE),
        8,
        after,
    )
    return got[:3], got[3:]


def join_kernel(base, a_ref, b_ref, c_ref, *outs):
    for gi, out in enumerate(outs):
        for ki, ref in enumerate((a_ref, b_ref, c_ref)):
            rows = slice(base + gi * TILE, base + (gi + 1) * TILE)
            out[ki * TILE : (ki + 1) * TILE, :] = ref[rows, :]


def join(got, base, after=()):
    return call(
        functools.partial(join_kernel, base),
        tuple(got),
        [whole(got[0].shape)] * 3,
        [shape((3 * TILE, TILE))] * 2,
        [whole((3 * TILE, TILE))] * 2,
        [],
        (0, 3 << 20),
        4,
        after,
    )


def swapped(value, second_pairing):
    if second_pairing:
        pairs = [(0, 3), (3, 0), (1, 2), (2, 1)]
    else:
        pairs = [(0, 1), (1, 0), (2, 3), (3, 2)]
    return lax.ppermute(value, "pool", pairs)


def project_kernel(which, has_in, own_ref, x_ref, p0, p1, p2, mine_ref, other_ref, *refs):
    n = len(which)
    carried, outs = (refs[:n], refs[n:]) if has_in else ((None,) * n, refs)
    even = parity() == 0
    mine, other = mine_ref[...], other_ref[...]
    lhs = jnp.concatenate([x_ref[...]] + [peer[0:ROWS, :] for peer in (p0, p1, p2)], axis=1)
    for c_ref, out, ti in zip(carried, outs, which):
        remote = lax.select(even, mine, other) if ti == 0 else lax.select(even, other, mine)
        rhs = jnp.concatenate([own_ref[ti * TILE : (ti + 1) * TILE, :], remote], axis=0)
        total = jnp.dot(lhs, rhs, preferred_element_type=F32)
        if has_in:
            total = total + c_ref[...].astype(F32)
        out[...] = total.astype(out.dtype)


def project(which, own, features, first_got, mine, other, carried, after=(), out_dtype=BF16):
    half = (ROWS, WIDTH)
    n = len(which)
    return call(
        functools.partial(project_kernel, which, bool(carried)),
        (own, features, *first_got, mine, other, *carried),
        [whole(half)] * 2
        + [whole(first_got[0].shape)] * 3
        + [whole((3 * TILE, TILE))] * 2
        + [whole(half)] * len(carried),
        [shape((ROWS, TILE), out_dtype)] * n,
        [whole((ROWS, TILE))] * n,
        [],
        (2 * ROWS * 1024 * TILE * n, 2 << 20),
        8,
        after,
    )


def window_start(ids, owner):
    before = jnp.sum((ids < owner * VARS).astype(jnp.int32))
    return jnp.minimum(before, ROWS - WINDOW)


def dispatch_kernel(ids_ref, x_ref, *outs):
    me = lax.axis_index("pool")
    ids = ids_ref[...]
    features = x_ref[...]
    for k in range(NX):
        owner = lax.rem(me + k, NX)
        start = window_start(ids, owner)
        at = lax.broadcasted_iota(jnp.int32, (WINDOW, ROWS), 0) + start
        hot = (at == lax.broadcasted_iota(jnp.int32, (WINDOW, ROWS), 1)).astype(F32).astype(BF16)
        outs[k][0:WINDOW, :] = jnp.dot(hot, features, preferred_element_type=F32).astype(BF16)
        local = jnp.broadcast_to((ids - owner * VARS).astype(F32), (IDROWS, ROWS)).astype(BF16)
        outs[k][WINDOW : WINDOW + IDROWS, :] = lax.dot_general(
            local, hot, (((1,), (1,)), ((), ())), preferred_element_type=F32
        ).astype(BF16)


def dispatch(ids, features, after=()):
    return call(
        dispatch_kernel,
        (ids, features),
        [whole((1, ROWS)), whole((ROWS, WIDTH))],
        [shape((WINDOW + IDROWS, WIDTH))] * NX,
        [whole((WINDOW + IDROWS, WIDTH))] * NX,
        [],
        (2 * 1024 * 512 * 256, 1 << 20),
        6,
        after,
    )


def spread_columns(row, lanes):
    diagonal = lax.broadcasted_iota(jnp.int32, (WINDOW, WINDOW), 0) == lax.broadcasted_iota(
        jnp.int32, (WINDOW, WINDOW), 1
    )
    row = jnp.broadcast_to(row.astype(F32), (WINDOW, WINDOW))
    spread = jnp.where(diagonal, row, 0.0).astype(BF16)
    return jnp.dot(spread, jnp.ones((WINDOW, lanes), BF16), preferred_element_type=F32)


def variant_columns(item_ref, lanes):
    return spread_columns(item_ref[WINDOW : WINDOW + 1, :], lanes)


def down_kernel(i0, i1, i2, i3, down_ref, out_ref, item_ref, fold_ref):
    for k, item in enumerate((i0, i1, i2, i3)):
        item_ref[k] = item[...]
    lane = lax.broadcasted_iota(jnp.int32, (1, 256), 1)
    part = lax.div(lane, jnp.int32(RANK)).astype(F32)

    def window(k, carry):
        item = item_ref.at[k]
        variant = variant_columns(item, 256)
        features = item[0:WINDOW, :]
        total = None
        for j in range(VARS * RANK // 256):
            value = lax.dot_general(
                features,
                down_ref[j * 256 : (j + 1) * 256, :],
                (((1,), (1,)), ((), ())),
                preferred_element_type=F32,
            )
            value = jnp.where(variant == part + float(j * 4), value, 0.0)
            total = value if total is None else total + value
        two = total[:, 0:128] + total[:, 128:256]
        fold_ref[k] = two + pltpu.roll(two, RANK, 1)
        return carry

    lax.fori_loop(0, NX, window, 0)
    low = lax.broadcasted_iota(jnp.int32, (WINDOW, 128), 1) < RANK
    for h in range(2):
        packed = jnp.where(low, fold_ref[h], fold_ref[h + 2]).astype(BF16)
        out_ref[:, h * 128 : (h + 1) * 128] = packed


def down(items, factor, after=()):
    return call(
        down_kernel,
        (*items, factor),
        [whole((WINDOW + IDROWS, WIDTH))] * NX + [whole((VARS * RANK, WIDTH))],
        shape((WINDOW, 256)),
        whole((WINDOW, 256)),
        [pltpu.VMEM((NX, WINDOW + IDROWS, WIDTH), BF16), pltpu.VMEM((NX, WINDOW, 128), F32)],
        (2 * 1024 * 256 * 2048, 2 << 20),
        8,
        after,
    )


def block_kernel(i0, i1, i2, i3, mats_ref, place_ref, out_ref, item_ref, rhs_ref):
    for k, item in enumerate((i0, i1, i2, i3)):
        item_ref[k] = item[...]
    shard = lax.axis_index(Z) * NY + lax.axis_index(Y)

    def lanes_of(v):
        return pl.ds(pl.multiple_of((place_ref[v] - shard * 2) * BLK, BLK), BLK)

    for v in range(VARS):
        rhs_ref[v * BLK : (v + 1) * BLK, :] = jnp.zeros((BLK, 256), BF16)
        rhs_ref[v * BLK : (v + 1) * BLK, lanes_of(v)] = mats_ref[v]

    def window(k, carry):
        item = item_ref.at[k]
        variant = variant_columns(item, 128)
        pieces = []
        for v in range(VARS):
            piece = item[0:WINDOW, lanes_of(v)].astype(F32)
            pieces.append(jnp.where(variant == float(v), piece, 0.0).astype(BF16))
        lhs = jnp.concatenate(pieces, axis=1)
        out_ref[k] = jnp.dot(lhs, rhs_ref[...], preferred_element_type=F32)
        return carry

    lax.fori_loop(0, NX, window, 0)


def block_terms(items, mats, places, after=()):
    return call(
        block_kernel,
        (*items, mats, places),
        [whole((WINDOW + IDROWS, WIDTH))] * NX + [whole((VARS, BLK, BLK)), SMEM],
        shape((NX, WINDOW, 256), F32),
        whole((NX, WINDOW, 256)),
        [pltpu.VMEM((NX, WINDOW + IDROWS, WIDTH), BF16), pltpu.VMEM((VARS * BLK, 256), BF16)],
        (2 * 1024 * 4096 * 256, 3 << 20),
        10,
        after,
    )


def add_kernel(a_ref, b_ref, out_ref):
    out_ref[...] = (a_ref[...].astype(F32) + b_ref[...].astype(F32)).astype(BF16)


def exchanged_sum(value, axis, bit, after=()):
    count = lax.axis_size(axis)
    other = lax.ppermute(value, axis, [(i, i ^ bit) for i in range(count)])
    return call(
        add_kernel,
        (value, other),
        [whole((WINDOW, 256))] * 2,
        shape((WINDOW, 256)),
        whole((WINDOW, 256)),
        [],
        (1 << 16, 3 << 17),
        2,
        after,
    )


def up_kernel(i0, i1, i2, i3, low_ref, up_ref, block_ref, *refs):
    outs, (item_ref, two_ref, out_ref) = refs[:NX], refs[NX:]
    for k, item in enumerate((i0, i1, i2, i3)):
        item_ref[k] = item[WINDOW : WINDOW + IDROWS, :]
    first = lax.broadcasted_iota(jnp.int32, (WINDOW, 128), 1) < RANK
    for h in range(2):
        packed = low_ref[:, h * 128 : (h + 1) * 128].astype(F32)
        turned = pltpu.roll(packed, RANK, 1)
        two_ref[h] = jnp.where(first, packed, turned)
        two_ref[h + 2] = jnp.where(first, turned, packed)
    half = lax.div(lax.broadcasted_iota(jnp.int32, (1, 128), 1), jnp.int32(RANK)).astype(F32)

    def window(k, carry):
        variant = spread_columns(item_ref[k, 0:1, :], 128)
        two = two_ref[k]
        pieces = []
        for i in range(VARS // 2):
            pieces.append(jnp.where(variant == half + float(2 * i), two, 0.0).astype(BF16))
        lhs = jnp.concatenate(pieces, axis=1)
        total = block_ref[k] + jnp.dot(lhs, up_ref[...], preferred_element_type=F32)
        out_ref[k] = total.astype(BF16)
        return carry

    lax.fori_loop(0, NX, window, 0)
    for k in range(NX):
        outs[k][...] = out_ref[k]


def up(items, low, factor, blocks, after=()):
    return call(
        up_kernel,
        (*items, low, factor, blocks),
        [whole((WINDOW + IDROWS, WIDTH))] * NX
        + [whole((WINDOW, 256)), whole((VARS * RANK, WIDTH)), whole((NX, WINDOW, 256))],
        [shape((WINDOW, WIDTH))] * NX,
        [whole((WINDOW, WIDTH))] * NX,
        [
            pltpu.VMEM((NX, IDROWS, WIDTH), BF16),
            pltpu.VMEM((NX, WINDOW, 128), F32),
            pltpu.VMEM((NX, WINDOW, WIDTH), BF16),
        ],
        (2 * 1024 * 256 * 2048, 3 << 20),
        10,
        after,
    )


def combine_kernel(ids_ref, h_ref, own_ref, plus_ref, r0, r1, r2, r3, first_ref, branch_ref):
    me = lax.axis_index("pool")
    ids = ids_ref[...]
    branch = own_ref[...] + plus_ref[...].astype(F32)
    delta = None
    for k, back in enumerate((r0, r1, r2, r3)):
        start = window_start(ids, lax.rem(me + k, NX))
        at = lax.broadcasted_iota(jnp.int32, (ROWS, WINDOW), 1) + start
        hot = (at == lax.broadcasted_iota(jnp.int32, (ROWS, WINDOW), 0)).astype(F32).astype(BF16)
        part = jnp.dot(hot, back[...], preferred_element_type=F32)
        delta = part if delta is None else delta + part
    branch = branch + delta
    branch_ref[...] = branch
    first_ref[...] = (h_ref[...].astype(F32) + branch).astype(BF16)


def combine(ids, hidden, own, plus, returned, after=()):
    half = (ROWS, WIDTH)
    return call(
        combine_kernel,
        (ids, hidden, own, plus, *returned),
        [whole((1, ROWS))] + [whole(half)] * 3 + [whole((WINDOW, WIDTH))] * NX,
        [shape(half), shape(half, F32)],
        [whole(half)] * 2,
        [],
        (2 * 512 * 1024 * 256, 2 << 20),
        8,
        after,
    )


def steps(
    hidden_input,
    attention_output,
    projection_weight,
    lowrank_down_factor,
    lowrank_up_factor,
    residual_block_mats,
    diagonal_block_index,
    row_variant_index,
):
    features = attention_output[0]
    weight = projection_weight[0]
    down_factor = lowrank_down_factor[0].reshape(VARS * RANK, WIDTH)
    up_factor = lowrank_up_factor[0].reshape(VARS * RANK, WIDTH)
    mats = residual_block_mats[0][:, 0]
    places = diagonal_block_index[0][:, 0]
    ids = row_variant_index.reshape(1, ROWS)

    first, (own0, own1) = pack((0, 1), weight, features)
    got = [shift(value, Y, hop) for value, hop in zip(first, HOPS)]
    sent = dispatch(ids, features, (first[0],))
    items = [sent[0]] + [shift(sent[k], "pool", k) for k in (1, 2, 3)]
    second, (own2, own3) = pack((2, 3), weight, None, (sent[0],))
    later = [shift(value, Y, hop) for value, hop in zip(second, HOPS)]
    low = down(items, down_factor, (second[0],))
    low1 = exchanged_sum(low, Z, 1)
    blocks = block_terms(items, mats, places, (low,))
    low2 = exchanged_sum(low1, Z, 2)
    mine0, mine1 = join(got, ROWS, (low1, blocks))
    other0 = swapped(mine0, False)
    other1 = swapped(mine1, True)
    low3 = exchanged_sum(low2, Z, 4)
    plus, minus = project((0, 1), own0, features, got, mine0, other0, (), (low2,))
    carried = (shift(plus, Z, 1), shift(minus, Z, -1))
    mine2, mine3 = join(later, 0, (plus,))
    other2 = swapped(mine2, False)
    other3 = swapped(mine3, True)
    low4 = exchanged_sum(low3, Y, 1)
    plus, minus = project((0, 1), own1, features, got, mine1, other1, carried)
    carried = (shift(plus, Z, 1), shift(minus, Z, -1))
    low5 = exchanged_sum(low4, Y, 2)
    plus, minus = project((0, 1), own2, features, got, mine2, other2, carried)
    carried = (shift(plus, Z, 1), shift(minus, Z, -1))
    served = up(items, low5, up_factor, blocks, (plus,))
    returned = [served[0]] + [shift(served[k], "pool", -k) for k in (1, 2, 3)]
    (plus,) = project(
        (0,), own3, features, got, mine3, other3, carried[:1], (served[1],)
    )
    arrived = shift(plus, Z, 1)
    (own,) = project((1,), own3, features, got, mine3, other3, carried[1:], (plus,), F32)
    plus = arrived

    first_out, branch = combine(ids, hidden_input, own, plus, returned)
    carried = lax.ppermute(first_out, "section", [(0, 1)])
    begin = jnp.where(lax.axis_index("section") == 0, hidden_input, carried)
    return (begin.astype(F32) + branch).astype(BF16)[None]


def solution(mesh):
    finer = Mesh(
        mesh.devices.reshape(mesh.shape["pool"], mesh.shape["section"], NZ, NY),
        ("pool", "section", Z, Y),
    )
    placed = (
        P("pool", TENSOR),
        P("section", "pool", TENSOR),
        P("section", TENSOR, None),
        P("section", "pool", None, TENSOR),
        P("section", "pool", None, TENSOR),
        P("section", "pool", TENSOR, None, None),
        P("section", "pool", TENSOR),
        P("pool"),
    )
    return jax.shard_map(
        steps,
        mesh=finer,
        in_specs=placed,
        out_specs=P("section", "pool", TENSOR),
        check_vma=False,
    )
```

```python
import functools

import jax
import jax.numpy as jnp
from jax import lax
from jax.experimental import pallas as pl
from jax.experimental.pallas import tpu as pltpu
from jax.sharding import Mesh
from jax.sharding import PartitionSpec as P


Z, Y = "tensor_0", "tensor_1"
TENSOR = (Z, Y)
NZ, NY, NX = 8, 4, 4
ROWS, WIDTH, TILE = 512, 256, 256
WINDOW = 256
IDROWS = 16
VARS, RANK, BLK = 32, 64, 128
HOPS = (1, 3, 2)
F32, BF16 = jnp.float32, jnp.bfloat16
ANY = pl.BlockSpec(memory_space=pl.ANY)
HBM = pl.BlockSpec(memory_space=pltpu.HBM)
SMEM = pl.BlockSpec(memory_space=pltpu.SMEM)


def shift(value, axis, steps):
    count = lax.axis_size(axis)
    return lax.ppermute(value, axis, [(i, (i + steps) % count) for i in range(count)])


def cost(flops, nbytes):
    return pl.CostEstimate(flops=flops, bytes_accessed=nbytes, transcendentals=0)


def shape(dims, dtype=BF16):
    return pltpu.VMEM(dims, dtype)


def whole(dims, at=None):
    at = at or (0,) * len(dims)
    return pl.BlockSpec(dims, lambda: at)


def tiles_of(group):
    z = lax.axis_index(Z)
    return lax.rem(z + (4 - group), NZ), lax.rem(z + (group + NZ - 3), NZ)


def column(ztile, ytile):
    return pl.multiple_of((ztile * NY + ytile) * TILE, TILE)


def placed(value, spec):
    space = pltpu.HBM if spec is HBM else pltpu.VMEM
    if spec is SMEM:
        return value
    return pltpu.with_memory_space_constraint(value, space)


def call(kernel, args, in_specs, outs, out_specs, scratch, work, limit, after=()):
    n, m = len(args), len(after)
    args = [placed(arg, spec) for arg, spec in zip(args, in_specs)]

    def body(*refs):
        kernel(*refs[:n], *refs[n + m :])

    return pl.pallas_call(
        body,
        out_shape=outs,
        in_specs=list(in_specs) + [ANY] * m,
        out_specs=out_specs,
        scratch_shapes=scratch,
        cost_estimate=cost(*work),
        compiler_params=pltpu.CompilerParams(vmem_limit_bytes=limit << 20),
    )(*args, *after)


def parity():
    return lax.rem(lax.axis_index("pool"), 2)


def pack_kernel(groups, ahead, *refs):
    w_ref = refs[0]
    n_in = 2 if ahead else 1
    outs = refs[n_in : n_in + 3]
    owns = refs[n_in + 3 : n_in + 3 + len(groups)]
    sems = refs[-1]
    y, odd = lax.axis_index(Y), parity()
    copies = []
    for gi, group in enumerate(groups):
        plus, minus = tiles_of(group)
        mine = plus * (1 - odd) + minus * odd
        for ki, hop in enumerate(HOPS):
            if ahead and gi == 0:
                copies.append((refs[1], outs[ki].at[pl.ds(0, ROWS), :]))
            source = w_ref.at[:, pl.ds(column(mine, lax.rem(y + hop, NY)), TILE)]
            copies.append((source, outs[ki].at[pl.ds(ahead + gi * TILE, TILE), :]))
    for gi, group in enumerate(groups):
        for ti, ztile in enumerate(tiles_of(group)):
            source = w_ref.at[:, pl.ds(column(ztile, y), TILE)]
            copies.append((source, owns[gi].at[pl.ds(ti * TILE, TILE), :]))
    copies = [
        pltpu.make_async_copy(source, target, sems.at[i])
        for i, (source, target) in enumerate(copies)
    ]
    for copy in copies:
        copy.start()
    for copy in copies:
        copy.wait()


def pack(groups, weight, features=None, after=()):
    ahead = 0 if features is None else ROWS
    args, specs = [weight], [HBM]
    if ahead:
        args.append(features)
        specs.append(HBM)
    rows = ahead + len(groups) * TILE
    dims = [(rows, TILE)] * 3 + [(2 * TILE, TILE)] * len(groups)
    got = call(
        functools.partial(pack_kernel, groups, ahead),
        args,
        specs,
        [shape(d) for d in dims],
        [whole(d) for d in dims],
        [pltpu.SemaphoreType.DMA((3 + 5 * len(groups),))],
        (0, 6 * rows * TILE),
        8,
        after,
    )
    return got[:3], got[3:]


def join_kernel(base, halves, a_ref, b_ref, c_ref, *outs):
    pos = 0
    for gi, split in enumerate(halves):
        for ki, ref in enumerate((a_ref, b_ref, c_ref)):
            first = base + gi * TILE
            if split:
                for side in range(2):
                    rows = slice(first + side * BLK, first + (side + 1) * BLK)
                    outs[pos + side][ki * BLK : (ki + 1) * BLK, :] = ref[rows, :]
            else:
                outs[pos][ki * TILE : (ki + 1) * TILE, :] = ref[first : first + TILE, :]
        pos += 2 if split else 1


def join(got, base, halves, after=()):
    dims = []
    for split in halves:
        dims += [(3 * BLK, TILE)] * 2 if split else [(3 * TILE, TILE)]
    return call(
        functools.partial(join_kernel, base, halves),
        tuple(got),
        [whole(got[0].shape)] * 3,
        [shape(d) for d in dims],
        [whole(d) for d in dims],
        [],
        (0, 3 << 20),
        4,
        after,
    )


def swapped(value, second_pairing):
    if second_pairing:
        pairs = [(0, 3), (3, 0), (1, 2), (2, 1)]
    else:
        pairs = [(0, 1), (1, 0), (2, 3), (3, 2)]
    return lax.ppermute(value, "pool", pairs)


def stacked(refs):
    if len(refs) == 1:
        return refs[0][...]
    low, high = refs
    pieces = []
    for ki in range(3):
        rows = slice(ki * BLK, (ki + 1) * BLK)
        pieces += [low[rows, :], high[rows, :]]
    return jnp.concatenate(pieces, axis=0)


def project_kernel(which, has_in, parts, own_ref, x_ref, p0, p1, p2, *refs):
    n = len(which)
    even = parity() == 0
    mine, other = stacked(refs[:parts]), stacked(refs[parts : 2 * parts])
    refs = refs[2 * parts :]
    carried, outs = (refs[:n], refs[n:]) if has_in else ((None,) * n, refs)
    lhs = jnp.concatenate([x_ref[...]] + [peer[0:ROWS, :] for peer in (p0, p1, p2)], axis=1)
    for c_ref, out, ti in zip(carried, outs, which):
        remote = lax.select(even, mine, other) if ti == 0 else lax.select(even, other, mine)
        rhs = jnp.concatenate([own_ref[ti * TILE : (ti + 1) * TILE, :], remote], axis=0)
        total = jnp.dot(lhs, rhs, preferred_element_type=F32)
        if has_in:
            total = total + c_ref[...].astype(F32)
        out[...] = total.astype(out.dtype)


def project(which, own, features, first_got, mine, other, carried, after=(), out_dtype=BF16):
    half = (ROWS, WIDTH)
    n, parts = len(which), len(mine)
    return call(
        functools.partial(project_kernel, which, bool(carried), parts),
        (own, features, *first_got, *mine, *other, *carried),
        [whole(half)] * 2
        + [whole(first_got[0].shape)] * 3
        + [whole(mine[0].shape)] * (2 * parts)
        + [whole(half)] * len(carried),
        [shape((ROWS, TILE), out_dtype)] * n,
        [whole((ROWS, TILE))] * n,
        [],
        (2 * ROWS * 1024 * TILE * n, 2 << 20),
        8,
        after,
    )


def window_start(ids, owner):
    before = jnp.sum((ids < owner * VARS).astype(jnp.int32))
    return jnp.minimum(before, ROWS - WINDOW)


def dispatch_kernel(ids_ref, x_ref, *outs):
    me = lax.axis_index("pool")
    ids = ids_ref[...]
    features = x_ref[...]
    for k in range(NX):
        owner = lax.rem(me + k, NX)
        start = window_start(ids, owner)
        at = lax.broadcasted_iota(jnp.int32, (WINDOW, ROWS), 0) + start
        hot = (at == lax.broadcasted_iota(jnp.int32, (WINDOW, ROWS), 1)).astype(F32).astype(BF16)
        outs[k][0:WINDOW, :] = jnp.dot(hot, features, preferred_element_type=F32).astype(BF16)
        local = jnp.broadcast_to((ids - owner * VARS).astype(F32), (IDROWS, ROWS)).astype(BF16)
        outs[k][WINDOW : WINDOW + IDROWS, :] = lax.dot_general(
            local, hot, (((1,), (1,)), ((), ())), preferred_element_type=F32
        ).astype(BF16)


def dispatch(ids, features, after=()):
    return call(
        dispatch_kernel,
        (ids, features),
        [whole((1, ROWS)), whole((ROWS, WIDTH))],
        [shape((WINDOW + IDROWS, WIDTH))] * NX,
        [whole((WINDOW + IDROWS, WIDTH))] * NX,
        [],
        (2 * 1024 * 512 * 256, 1 << 20),
        6,
        after,
    )


def spread_columns(row, lanes):
    diagonal = lax.broadcasted_iota(jnp.int32, (WINDOW, WINDOW), 0) == lax.broadcasted_iota(
        jnp.int32, (WINDOW, WINDOW), 1
    )
    row = jnp.broadcast_to(row.astype(F32), (WINDOW, WINDOW))
    spread = jnp.where(diagonal, row, 0.0).astype(BF16)
    return jnp.dot(spread, jnp.ones((WINDOW, lanes), BF16), preferred_element_type=F32)


def variant_columns(item_ref, lanes):
    return spread_columns(item_ref[WINDOW : WINDOW + 1, :], lanes)


def down_kernel(i0, i1, i2, i3, down_ref, out_ref, item_ref, fold_ref):
    for k, item in enumerate((i0, i1, i2, i3)):
        item_ref[k] = item[...]
    lane = lax.broadcasted_iota(jnp.int32, (1, 256), 1)
    part = lax.div(lane, jnp.int32(RANK)).astype(F32)

    def window(k, carry):
        item = item_ref.at[k]
        variant = variant_columns(item, 256)
        features = item[0:WINDOW, :]
        total = None
        for j in range(VARS * RANK // 256):
            value = lax.dot_general(
                features,
                down_ref[j * 256 : (j + 1) * 256, :],
                (((1,), (1,)), ((), ())),
                preferred_element_type=F32,
            )
            value = jnp.where(variant == part + float(j * 4), value, 0.0)
            total = value if total is None else total + value
        two = total[:, 0:128] + total[:, 128:256]
        fold_ref[k] = two + pltpu.roll(two, RANK, 1)
        return carry

    lax.fori_loop(0, NX, window, 0)
    low = lax.broadcasted_iota(jnp.int32, (WINDOW, 128), 1) < RANK
    for h in range(2):
        packed = jnp.where(low, fold_ref[h], fold_ref[h + 2]).astype(BF16)
        out_ref[:, h * 128 : (h + 1) * 128] = packed


def down(items, factor, after=()):
    return call(
        down_kernel,
        (*items, factor),
        [whole((WINDOW + IDROWS, WIDTH))] * NX + [whole((VARS * RANK, WIDTH))],
        shape((WINDOW, 256)),
        whole((WINDOW, 256)),
        [pltpu.VMEM((NX, WINDOW + IDROWS, WIDTH), BF16), pltpu.VMEM((NX, WINDOW, 128), F32)],
        (2 * 1024 * 256 * 2048, 2 << 20),
        8,
        after,
    )


def block_kernel(i0, i1, i2, i3, mats_ref, place_ref, out_ref, item_ref, rhs_ref):
    for k, item in enumerate((i0, i1, i2, i3)):
        item_ref[k] = item[...]
    shard = lax.axis_index(Z) * NY + lax.axis_index(Y)

    def lanes_of(v):
        return pl.ds(pl.multiple_of((place_ref[v] - shard * 2) * BLK, BLK), BLK)

    for v in range(VARS):
        rhs_ref[v * BLK : (v + 1) * BLK, :] = jnp.zeros((BLK, 256), BF16)
        rhs_ref[v * BLK : (v + 1) * BLK, lanes_of(v)] = mats_ref[v]

    def window(k, carry):
        item = item_ref.at[k]
        variant = variant_columns(item, 128)
        pieces = []
        for v in range(VARS):
            piece = item[0:WINDOW, lanes_of(v)].astype(F32)
            pieces.append(jnp.where(variant == float(v), piece, 0.0).astype(BF16))
        lhs = jnp.concatenate(pieces, axis=1)
        out_ref[k] = jnp.dot(lhs, rhs_ref[...], preferred_element_type=F32)
        return carry

    lax.fori_loop(0, NX, window, 0)


def block_terms(items, mats, places, after=()):
    return call(
        block_kernel,
        (*items, mats, places),
        [whole((WINDOW + IDROWS, WIDTH))] * NX + [whole((VARS, BLK, BLK)), SMEM],
        shape((NX, WINDOW, 256), F32),
        whole((NX, WINDOW, 256)),
        [pltpu.VMEM((NX, WINDOW + IDROWS, WIDTH), BF16), pltpu.VMEM((VARS * BLK, 256), BF16)],
        (2 * 1024 * 4096 * 256, 3 << 20),
        10,
        after,
    )


def add_kernel(a_ref, b_ref, out_ref):
    out_ref[...] = (a_ref[...].astype(F32) + b_ref[...].astype(F32)).astype(BF16)


def exchanged_sum(value, axis, bit, after=()):
    count = lax.axis_size(axis)
    other = lax.ppermute(value, axis, [(i, i ^ bit) for i in range(count)])
    return call(
        add_kernel,
        (value, other),
        [whole((WINDOW, 256))] * 2,
        shape((WINDOW, 256)),
        whole((WINDOW, 256)),
        [],
        (1 << 16, 3 << 17),
        2,
        after,
    )


def up_kernel(i0, i1, i2, i3, low_ref, up_ref, block_ref, *refs):
    outs, (item_ref, two_ref, out_ref) = refs[:NX], refs[NX:]
    for k, item in enumerate((i0, i1, i2, i3)):
        item_ref[k] = item[WINDOW : WINDOW + IDROWS, :]
    first = lax.broadcasted_iota(jnp.int32, (WINDOW, 128), 1) < RANK
    for h in range(2):
        packed = low_ref[:, h * 128 : (h + 1) * 128].astype(F32)
        turned = pltpu.roll(packed, RANK, 1)
        two_ref[h] = jnp.where(first, packed, turned)
        two_ref[h + 2] = jnp.where(first, turned, packed)
    half = lax.div(lax.broadcasted_iota(jnp.int32, (1, 128), 1), jnp.int32(RANK)).astype(F32)

    def window(k, carry):
        variant = spread_columns(item_ref[k, 0:1, :], 128)
        two = two_ref[k]
        pieces = []
        for i in range(VARS // 2):
            pieces.append(jnp.where(variant == half + float(2 * i), two, 0.0).astype(BF16))
        lhs = jnp.concatenate(pieces, axis=1)
        total = block_ref[k] + jnp.dot(lhs, up_ref[...], preferred_element_type=F32)
        out_ref[k] = total.astype(BF16)
        return carry

    lax.fori_loop(0, NX, window, 0)
    for k in range(NX):
        outs[k][...] = out_ref[k]


def up(items, low, factor, blocks, after=()):
    return call(
        up_kernel,
        (*items, low, factor, blocks),
        [whole((WINDOW + IDROWS, WIDTH))] * NX
        + [whole((WINDOW, 256)), whole((VARS * RANK, WIDTH)), whole((NX, WINDOW, 256))],
        [shape((WINDOW, WIDTH))] * NX,
        [whole((WINDOW, WIDTH))] * NX,
        [
            pltpu.VMEM((NX, IDROWS, WIDTH), BF16),
            pltpu.VMEM((NX, WINDOW, 128), F32),
            pltpu.VMEM((NX, WINDOW, WIDTH), BF16),
        ],
        (2 * 1024 * 256 * 2048, 3 << 20),
        10,
        after,
    )


def combine_kernel(ids_ref, h_ref, own_ref, plus_ref, r0, r1, r2, r3, first_ref, branch_ref):
    me = lax.axis_index("pool")
    ids = ids_ref[...]
    branch = own_ref[...] + plus_ref[...].astype(F32)
    delta = None
    for k, back in enumerate((r0, r1, r2, r3)):
        start = window_start(ids, lax.rem(me + k, NX))
        at = lax.broadcasted_iota(jnp.int32, (ROWS, WINDOW), 1) + start
        hot = (at == lax.broadcasted_iota(jnp.int32, (ROWS, WINDOW), 0)).astype(F32).astype(BF16)
        part = jnp.dot(hot, back[...], preferred_element_type=F32)
        delta = part if delta is None else delta + part
    branch = branch + delta
    branch_ref[...] = branch
    first_ref[...] = (h_ref[...].astype(F32) + branch).astype(BF16)


def combine(ids, hidden, own, plus, returned, after=()):
    half = (ROWS, WIDTH)
    return call(
        combine_kernel,
        (ids, hidden, own, plus, *returned),
        [whole((1, ROWS))] + [whole(half)] * 3 + [whole((WINDOW, WIDTH))] * NX,
        [shape(half), shape(half, F32)],
        [whole(half)] * 2,
        [],
        (2 * 512 * 1024 * 256, 2 << 20),
        8,
        after,
    )


def steps(
    hidden_input,
    attention_output,
    projection_weight,
    lowrank_down_factor,
    lowrank_up_factor,
    residual_block_mats,
    diagonal_block_index,
    row_variant_index,
):
    features = attention_output[0]
    weight = projection_weight[0]
    down_factor = lowrank_down_factor[0].reshape(VARS * RANK, WIDTH)
    up_factor = lowrank_up_factor[0].reshape(VARS * RANK, WIDTH)
    mats = residual_block_mats[0][:, 0]
    places = diagonal_block_index[0][:, 0]
    ids = row_variant_index.reshape(1, ROWS)

    first, (own0,) = pack((0,), weight, features)
    got = [shift(value, Y, hop) for value, hop in zip(first, HOPS)]
    sent = dispatch(ids, features, (first[0],))
    items = [sent[0]] + [shift(sent[k], "pool", k) for k in (1, 2, 3)]
    second, (own1, own2, own3) = pack((1, 2, 3), weight, None, (sent[0],))
    later = [shift(value, Y, hop) for value, hop in zip(second, HOPS)]
    low = down(items, down_factor, (second[0],))
    low1 = exchanged_sum(low, Z, 1)
    mine0 = join(got, ROWS, (True,), (low,))
    other0 = (shift(mine0[0], "pool", 1), shift(mine0[1], "pool", -1))
    low2 = exchanged_sum(low1, Z, 2)
    plus, minus = project((0, 1), own0, features, got, mine0, other0, (), (low1,))
    carried = (shift(plus, Z, 1), shift(minus, Z, -1))
    low3 = exchanged_sum(low2, Z, 4)
    *mine1, mine2, mine3 = join(later, 0, (True, False, False), (plus,))
    other1 = (shift(mine1[0], "pool", 1), shift(mine1[1], "pool", -1))
    other2 = swapped(mine2, False)
    other3 = swapped(mine3, True)
    plus, minus = project((0, 1), own1, features, got, mine1, other1, carried)
    carried = (shift(plus, Z, 1), shift(minus, Z, -1))
    blocks = block_terms(items, mats, places, (plus,))
    low4 = exchanged_sum(low3, Y, 1, (blocks,))
    low5 = exchanged_sum(low4, Y, 2)
    plus, minus = project((0, 1), own2, features, got, (mine2,), (other2,), carried)
    carried = (shift(plus, Z, 1), shift(minus, Z, -1))
    served = up(items, low5, up_factor, blocks, (plus,))
    returned = [served[0]] + [shift(served[k], "pool", -k) for k in (1, 2, 3)]
    (plus,) = project(
        (0,), own3, features, got, (mine3,), (other3,), carried[:1], (served[1],)
    )
    arrived = shift(plus, Z, 1)
    (own,) = project(
        (1,), own3, features, got, (mine3,), (other3,), carried[1:], (plus,), F32
    )
    plus = arrived

    first_out, branch = combine(ids, hidden_input, own, plus, returned)
    carried = lax.ppermute(first_out, "section", [(0, 1)])
    begin = jnp.where(lax.axis_index("section") == 0, hidden_input, carried)
    return (begin.astype(F32) + branch).astype(BF16)[None]


def solution(mesh):
    finer = Mesh(
        mesh.devices.reshape(mesh.shape["pool"], mesh.shape["section"], NZ, NY),
        ("pool", "section", Z, Y),
    )
    placed = (
        P("pool", TENSOR),
        P("section", "pool", TENSOR),
        P("section", TENSOR, None),
        P("section", "pool", None, TENSOR),
        P("section", "pool", None, TENSOR),
        P("section", "pool", TENSOR, None, None),
        P("section", "pool", TENSOR),
        P("pool"),
    )
    return jax.shard_map(
        steps,
        mesh=finer,
        in_specs=placed,
        out_specs=P("section", "pool", TENSOR),
        check_vma=False,
    )
```

```python
import functools

import jax
import jax.numpy as jnp
from jax import lax
from jax.experimental import pallas as pl
from jax.experimental.pallas import tpu as pltpu
from jax.sharding import Mesh
from jax.sharding import PartitionSpec as P


Z, Y = "tensor_0", "tensor_1"
TENSOR = (Z, Y)
NZ, NY, NX = 8, 4, 4
ROWS, WIDTH, TILE = 512, 256, 256
WINDOW = 256
IDROWS = 16
VARS, RANK, BLK = 32, 64, 128
HOPS = (1, 3, 2)
F32, BF16 = jnp.float32, jnp.bfloat16
ANY = pl.BlockSpec(memory_space=pl.ANY)
HBM = pl.BlockSpec(memory_space=pltpu.HBM)
SMEM = pl.BlockSpec(memory_space=pltpu.SMEM)


def shift(value, axis, steps):
    count = lax.axis_size(axis)
    return lax.ppermute(value, axis, [(i, (i + steps) % count) for i in range(count)])


def cost(flops, nbytes):
    return pl.CostEstimate(flops=flops, bytes_accessed=nbytes, transcendentals=0)


def shape(dims, dtype=BF16):
    return pltpu.VMEM(dims, dtype)


def whole(dims, at=None):
    at = at or (0,) * len(dims)
    return pl.BlockSpec(dims, lambda: at)


def tiles_of(group):
    z = lax.axis_index(Z)
    return lax.rem(z + (4 - group), NZ), lax.rem(z + (group + NZ - 3), NZ)


def column(ztile, ytile):
    return pl.multiple_of((ztile * NY + ytile) * TILE, TILE)


def placed(value, spec):
    space = pltpu.HBM if spec is HBM else pltpu.VMEM
    if spec is SMEM:
        return value
    return pltpu.with_memory_space_constraint(value, space)


def call(kernel, args, in_specs, outs, out_specs, scratch, work, limit, after=()):
    n, m = len(args), len(after)
    args = [placed(arg, spec) for arg, spec in zip(args, in_specs)]

    def body(*refs):
        kernel(*refs[:n], *refs[n + m :])

    return pl.pallas_call(
        body,
        out_shape=outs,
        in_specs=list(in_specs) + [ANY] * m,
        out_specs=out_specs,
        scratch_shapes=scratch,
        cost_estimate=cost(*work),
        compiler_params=pltpu.CompilerParams(vmem_limit_bytes=limit << 20),
    )(*args, *after)


def parity():
    return lax.rem(lax.axis_index("pool"), 2)


def pack_kernel(groups, ahead, *refs):
    w_ref = refs[0]
    n_in = 2 if ahead else 1
    outs = refs[n_in : n_in + 3]
    owns = refs[n_in + 3 : n_in + 3 + len(groups)]
    sems = refs[-1]
    y, odd = lax.axis_index(Y), parity()
    copies = []
    for gi, group in enumerate(groups):
        plus, minus = tiles_of(group)
        mine = plus * (1 - odd) + minus * odd
        for ki, hop in enumerate(HOPS):
            if ahead and gi == 0:
                copies.append((refs[1], outs[ki].at[pl.ds(0, ROWS), :]))
            source = w_ref.at[:, pl.ds(column(mine, lax.rem(y + hop, NY)), TILE)]
            copies.append((source, outs[ki].at[pl.ds(ahead + gi * TILE, TILE), :]))
    for gi, group in enumerate(groups):
        for ti, ztile in enumerate(tiles_of(group)):
            source = w_ref.at[:, pl.ds(column(ztile, y), TILE)]
            copies.append((source, owns[gi].at[pl.ds(ti * TILE, TILE), :]))
    copies = [
        pltpu.make_async_copy(source, target, sems.at[i])
        for i, (source, target) in enumerate(copies)
    ]
    for copy in copies:
        copy.start()
    for copy in copies:
        copy.wait()


def pack(groups, weight, features=None, after=()):
    ahead = 0 if features is None else ROWS
    args, specs = [weight], [HBM]
    if ahead:
        args.append(features)
        specs.append(HBM)
    rows = ahead + len(groups) * TILE
    dims = [(rows, TILE)] * 3 + [(2 * TILE, TILE)] * len(groups)
    got = call(
        functools.partial(pack_kernel, groups, ahead),
        args,
        specs,
        [shape(d) for d in dims],
        [whole(d) for d in dims],
        [pltpu.SemaphoreType.DMA((3 + 5 * len(groups),))],
        (0, 6 * rows * TILE),
        8,
        after,
    )
    return got[:3], got[3:]


def join_kernel(base, halves, a_ref, b_ref, c_ref, *outs):
    pos = 0
    for gi, split in enumerate(halves):
        for ki, ref in enumerate((a_ref, b_ref, c_ref)):
            first = base + gi * TILE
            if split:
                for side in range(2):
                    rows = slice(first + side * BLK, first + (side + 1) * BLK)
                    outs[pos + side][ki * BLK : (ki + 1) * BLK, :] = ref[rows, :]
            else:
                outs[pos][ki * TILE : (ki + 1) * TILE, :] = ref[first : first + TILE, :]
        pos += 2 if split else 1


def join(got, base, halves, after=()):
    dims = []
    for split in halves:
        dims += [(3 * BLK, TILE)] * 2 if split else [(3 * TILE, TILE)]
    return call(
        functools.partial(join_kernel, base, halves),
        tuple(got),
        [whole(got[0].shape)] * 3,
        [shape(d) for d in dims],
        [whole(d) for d in dims],
        [],
        (0, 3 << 20),
        4,
        after,
    )


def swapped(value, second_pairing):
    if second_pairing:
        pairs = [(0, 3), (3, 0), (1, 2), (2, 1)]
    else:
        pairs = [(0, 1), (1, 0), (2, 3), (3, 2)]
    return lax.ppermute(value, "pool", pairs)


def stacked(refs):
    if len(refs) == 1:
        return refs[0][...]
    low, high = refs
    pieces = []
    for ki in range(3):
        rows = slice(ki * BLK, (ki + 1) * BLK)
        pieces += [low[rows, :], high[rows, :]]
    return jnp.concatenate(pieces, axis=0)


def project_kernel(which, has_in, parts, own_ref, x_ref, p0, p1, p2, *refs):
    n = len(which)
    even = parity() == 0
    mine, other = stacked(refs[:parts]), stacked(refs[parts : 2 * parts])
    refs = refs[2 * parts :]
    carried, outs = (refs[:n], refs[n:]) if has_in else ((None,) * n, refs)
    lhs = jnp.concatenate([x_ref[...]] + [peer[0:ROWS, :] for peer in (p0, p1, p2)], axis=1)
    for c_ref, out, ti in zip(carried, outs, which):
        remote = lax.select(even, mine, other) if ti == 0 else lax.select(even, other, mine)
        rhs = jnp.concatenate([own_ref[ti * TILE : (ti + 1) * TILE, :], remote], axis=0)
        total = jnp.dot(lhs, rhs, preferred_element_type=F32)
        if has_in:
            total = total + c_ref[...].astype(F32)
        out[...] = total.astype(out.dtype)


def project(which, own, features, first_got, mine, other, carried, after=(), out_dtype=BF16):
    half = (ROWS, WIDTH)
    n, parts = len(which), len(mine)
    return call(
        functools.partial(project_kernel, which, bool(carried), parts),
        (own, features, *first_got, *mine, *other, *carried),
        [whole(half)] * 2
        + [whole(first_got[0].shape)] * 3
        + [whole(mine[0].shape)] * (2 * parts)
        + [whole(half)] * len(carried),
        [shape((ROWS, TILE), out_dtype)] * n,
        [whole((ROWS, TILE))] * n,
        [],
        (2 * ROWS * 1024 * TILE * n, 2 << 20),
        8,
        after,
    )


def window_start(ids, owner):
    before = jnp.sum((ids < owner * VARS).astype(jnp.int32))
    return jnp.minimum(before, ROWS - WINDOW)


def dispatch_kernel(ids_ref, x_ref, *outs):
    me = lax.axis_index("pool")
    ids = ids_ref[...]
    features = x_ref[...]
    for k in range(NX):
        owner = lax.rem(me + k, NX)
        start = window_start(ids, owner)
        at = lax.broadcasted_iota(jnp.int32, (WINDOW, ROWS), 0) + start
        hot = (at == lax.broadcasted_iota(jnp.int32, (WINDOW, ROWS), 1)).astype(F32).astype(BF16)
        outs[k][0:WINDOW, :] = jnp.dot(hot, features, preferred_element_type=F32).astype(BF16)
        local = jnp.broadcast_to((ids - owner * VARS).astype(F32), (IDROWS, ROWS)).astype(BF16)
        outs[k][WINDOW : WINDOW + IDROWS, :] = lax.dot_general(
            local, hot, (((1,), (1,)), ((), ())), preferred_element_type=F32
        ).astype(BF16)


def dispatch(ids, features, after=()):
    return call(
        dispatch_kernel,
        (ids, features),
        [whole((1, ROWS)), whole((ROWS, WIDTH))],
        [shape((WINDOW + IDROWS, WIDTH))] * NX,
        [whole((WINDOW + IDROWS, WIDTH))] * NX,
        [],
        (2 * 1024 * 512 * 256, 1 << 20),
        6,
        after,
    )


def spread_columns(row, lanes):
    diagonal = lax.broadcasted_iota(jnp.int32, (WINDOW, WINDOW), 0) == lax.broadcasted_iota(
        jnp.int32, (WINDOW, WINDOW), 1
    )
    row = jnp.broadcast_to(row.astype(F32), (WINDOW, WINDOW))
    spread = jnp.where(diagonal, row, 0.0).astype(BF16)
    return jnp.dot(spread, jnp.ones((WINDOW, lanes), BF16), preferred_element_type=F32)


def variant_columns(item_ref, lanes):
    return spread_columns(item_ref[WINDOW : WINDOW + 1, :], lanes)


def down_kernel(i0, i1, i2, i3, down_ref, out_ref, item_ref, fold_ref):
    for k, item in enumerate((i0, i1, i2, i3)):
        item_ref[k] = item[...]
    lane = lax.broadcasted_iota(jnp.int32, (1, 256), 1)
    part = lax.div(lane, jnp.int32(RANK)).astype(F32)

    def window(k, carry):
        item = item_ref.at[k]
        variant = variant_columns(item, 256)
        features = item[0:WINDOW, :]
        total = None
        for j in range(VARS * RANK // 256):
            value = lax.dot_general(
                features,
                down_ref[j * 256 : (j + 1) * 256, :],
                (((1,), (1,)), ((), ())),
                preferred_element_type=F32,
            )
            value = jnp.where(variant == part + float(j * 4), value, 0.0)
            total = value if total is None else total + value
        two = total[:, 0:128] + total[:, 128:256]
        fold_ref[k] = two + pltpu.roll(two, RANK, 1)
        return carry

    lax.fori_loop(0, NX, window, 0)
    low = lax.broadcasted_iota(jnp.int32, (WINDOW, 128), 1) < RANK
    for h in range(2):
        packed = jnp.where(low, fold_ref[h], fold_ref[h + 2]).astype(BF16)
        out_ref[:, h * 128 : (h + 1) * 128] = packed


def down(items, factor, after=()):
    return call(
        down_kernel,
        (*items, factor),
        [whole((WINDOW + IDROWS, WIDTH))] * NX + [whole((VARS * RANK, WIDTH))],
        shape((WINDOW, 256)),
        whole((WINDOW, 256)),
        [pltpu.VMEM((NX, WINDOW + IDROWS, WIDTH), BF16), pltpu.VMEM((NX, WINDOW, 128), F32)],
        (2 * 1024 * 256 * 2048, 2 << 20),
        8,
        after,
    )


def block_kernel(i0, i1, i2, i3, mats_ref, place_ref, out_ref, item_ref, rhs_ref):
    for k, item in enumerate((i0, i1, i2, i3)):
        item_ref[k] = item[...]
    shard = lax.axis_index(Z) * NY + lax.axis_index(Y)

    def lanes_of(v):
        return pl.ds(pl.multiple_of((place_ref[v] - shard * 2) * BLK, BLK), BLK)

    for v in range(VARS):
        rhs_ref[v * BLK : (v + 1) * BLK, :] = jnp.zeros((BLK, 256), BF16)
        rhs_ref[v * BLK : (v + 1) * BLK, lanes_of(v)] = mats_ref[v]

    def window(k, carry):
        item = item_ref.at[k]
        variant = variant_columns(item, 128)
        pieces = []
        for v in range(VARS):
            piece = item[0:WINDOW, lanes_of(v)].astype(F32)
            pieces.append(jnp.where(variant == float(v), piece, 0.0).astype(BF16))
        lhs = jnp.concatenate(pieces, axis=1)
        out_ref[k] = jnp.dot(lhs, rhs_ref[...], preferred_element_type=F32)
        return carry

    lax.fori_loop(0, NX, window, 0)


def block_terms(items, mats, places, after=()):
    return call(
        block_kernel,
        (*items, mats, places),
        [whole((WINDOW + IDROWS, WIDTH))] * NX + [whole((VARS, BLK, BLK)), SMEM],
        shape((NX, WINDOW, 256), F32),
        whole((NX, WINDOW, 256)),
        [pltpu.VMEM((NX, WINDOW + IDROWS, WIDTH), BF16), pltpu.VMEM((VARS * BLK, 256), BF16)],
        (2 * 1024 * 4096 * 256, 3 << 20),
        10,
        after,
    )


def add_kernel(a_ref, b_ref, out_ref):
    out_ref[...] = (a_ref[...].astype(F32) + b_ref[...].astype(F32)).astype(BF16)


def exchanged_sum(value, axis, bit, after=()):
    count = lax.axis_size(axis)
    other = lax.ppermute(value, axis, [(i, i ^ bit) for i in range(count)])
    return call(
        add_kernel,
        (value, other),
        [whole((WINDOW, 256))] * 2,
        shape((WINDOW, 256)),
        whole((WINDOW, 256)),
        [],
        (1 << 16, 3 << 17),
        2,
        after,
    )


def up_kernel(i0, i1, i2, i3, low_ref, up_ref, block_ref, *refs):
    outs, (item_ref, two_ref, out_ref) = refs[:NX], refs[NX:]
    for k, item in enumerate((i0, i1, i2, i3)):
        item_ref[k] = item[WINDOW : WINDOW + IDROWS, :]
    first = lax.broadcasted_iota(jnp.int32, (WINDOW, 128), 1) < RANK
    for h in range(2):
        packed = low_ref[:, h * 128 : (h + 1) * 128].astype(F32)
        turned = pltpu.roll(packed, RANK, 1)
        two_ref[h] = jnp.where(first, packed, turned)
        two_ref[h + 2] = jnp.where(first, turned, packed)
    half = lax.div(lax.broadcasted_iota(jnp.int32, (1, 128), 1), jnp.int32(RANK)).astype(F32)

    def window(k, carry):
        variant = spread_columns(item_ref[k, 0:1, :], 128)
        two = two_ref[k]
        pieces = []
        for i in range(VARS // 2):
            pieces.append(jnp.where(variant == half + float(2 * i), two, 0.0).astype(BF16))
        lhs = jnp.concatenate(pieces, axis=1)
        total = block_ref[k] + jnp.dot(lhs, up_ref[...], preferred_element_type=F32)
        out_ref[k] = total.astype(BF16)
        return carry

    lax.fori_loop(0, NX, window, 0)
    for k in range(NX):
        outs[k][...] = out_ref[k]


def up(items, low, factor, blocks, after=()):
    return call(
        up_kernel,
        (*items, low, factor, blocks),
        [whole((WINDOW + IDROWS, WIDTH))] * NX
        + [whole((WINDOW, 256)), whole((VARS * RANK, WIDTH)), whole((NX, WINDOW, 256))],
        [shape((WINDOW, WIDTH))] * NX,
        [whole((WINDOW, WIDTH))] * NX,
        [
            pltpu.VMEM((NX, IDROWS, WIDTH), BF16),
            pltpu.VMEM((NX, WINDOW, 128), F32),
            pltpu.VMEM((NX, WINDOW, WIDTH), BF16),
        ],
        (2 * 1024 * 256 * 2048, 3 << 20),
        10,
        after,
    )


def combine_kernel(ids_ref, h_ref, own_ref, plus_ref, r0, r1, r2, r3, first_ref, branch_ref):
    me = lax.axis_index("pool")
    ids = ids_ref[...]
    branch = own_ref[...] + plus_ref[...].astype(F32)
    delta = None
    for k, back in enumerate((r0, r1, r2, r3)):
        start = window_start(ids, lax.rem(me + k, NX))
        at = lax.broadcasted_iota(jnp.int32, (ROWS, WINDOW), 1) + start
        hot = (at == lax.broadcasted_iota(jnp.int32, (ROWS, WINDOW), 0)).astype(F32).astype(BF16)
        part = jnp.dot(hot, back[...], preferred_element_type=F32)
        delta = part if delta is None else delta + part
    branch = branch + delta
    branch_ref[...] = branch
    first_ref[...] = (h_ref[...].astype(F32) + branch).astype(BF16)


def combine(ids, hidden, own, plus, returned, after=()):
    half = (ROWS, WIDTH)
    return call(
        combine_kernel,
        (ids, hidden, own, plus, *returned),
        [whole((1, ROWS))] + [whole(half)] * 3 + [whole((WINDOW, WIDTH))] * NX,
        [shape(half), shape(half, F32)],
        [whole(half)] * 2,
        [],
        (2 * 512 * 1024 * 256, 2 << 20),
        8,
        after,
    )


def steps(
    hidden_input,
    attention_output,
    projection_weight,
    lowrank_down_factor,
    lowrank_up_factor,
    residual_block_mats,
    diagonal_block_index,
    row_variant_index,
):
    features = attention_output[0]
    weight = projection_weight[0]
    down_factor = lowrank_down_factor[0].reshape(VARS * RANK, WIDTH)
    up_factor = lowrank_up_factor[0].reshape(VARS * RANK, WIDTH)
    mats = residual_block_mats[0][:, 0]
    places = diagonal_block_index[0][:, 0]
    ids = row_variant_index.reshape(1, ROWS)

    first, (own0,) = pack((0,), weight, features)
    got = [shift(value, Y, hop) for value, hop in zip(first, HOPS)]
    sent = dispatch(ids, features, (first[0],))
    items = [sent[0]] + [shift(sent[k], "pool", k) for k in (1, 2, 3)]
    second, (own1, own2, own3) = pack((1, 2, 3), weight, None, (sent[0],))
    later = [shift(value, Y, hop) for value, hop in zip(second, HOPS)]
    low = down(items, down_factor, (second[0],))
    low1 = exchanged_sum(low, Z, 1)
    mine0 = join(got, ROWS, (True,), (low,))
    other0 = (shift(mine0[0], "pool", 1), shift(mine0[1], "pool", -1))
    low2 = exchanged_sum(low1, Z, 2)
    blocks = block_terms(items, mats, places, (low1, mine0[0]))
    plus, minus = project((0, 1), own0, features, got, mine0, other0, (), (blocks,))
    carried = (shift(plus, Z, 1), shift(minus, Z, -1))
    low3 = exchanged_sum(low2, Z, 4)
    *mine1, mine2, mine3 = join(later, 0, (True, False, False), (plus,))
    other1 = (shift(mine1[0], "pool", 1), shift(mine1[1], "pool", -1))
    other2 = swapped(mine2, False)
    other3 = swapped(mine3, True)
    plus, minus = project((0, 1), own1, features, got, mine1, other1, carried)
    carried = (shift(plus, Z, 1), shift(minus, Z, -1))
    low4 = exchanged_sum(low3, Y, 1)
    low5 = exchanged_sum(low4, Y, 2)
    plus, minus = project((0, 1), own2, features, got, (mine2,), (other2,), carried)
    carried = (shift(plus, Z, 1), shift(minus, Z, -1))
    served = up(items, low5, up_factor, blocks, (plus,))
    returned = [served[0]] + [shift(served[k], "pool", -k) for k in (1, 2, 3)]
    (plus,) = project(
        (0,), own3, features, got, (mine3,), (other3,), carried[:1], (served[1],)
    )
    arrived = shift(plus, Z, 1)
    (own,) = project(
        (1,), own3, features, got, (mine3,), (other3,), carried[1:], (plus,), F32
    )
    plus = arrived

    first_out, branch = combine(ids, hidden_input, own, plus, returned)
    carried = lax.ppermute(first_out, "section", [(0, 1)])
    begin = jnp.where(lax.axis_index("section") == 0, hidden_input, carried)
    return (begin.astype(F32) + branch).astype(BF16)[None]


def solution(mesh):
    finer = Mesh(
        mesh.devices.reshape(mesh.shape["pool"], mesh.shape["section"], NZ, NY),
        ("pool", "section", Z, Y),
    )
    placed = (
        P("pool", TENSOR),
        P("section", "pool", TENSOR),
        P("section", TENSOR, None),
        P("section", "pool", None, TENSOR),
        P("section", "pool", None, TENSOR),
        P("section", "pool", TENSOR, None, None),
        P("section", "pool", TENSOR),
        P("pool"),
    )
    return jax.shard_map(
        steps,
        mesh=finer,
        in_specs=placed,
        out_specs=P("section", "pool", TENSOR),
        check_vma=False,
    )
```

```python
import functools

import jax
import jax.numpy as jnp
from jax import lax
from jax.experimental import pallas as pl
from jax.experimental.pallas import tpu as pltpu
from jax.sharding import Mesh
from jax.sharding import PartitionSpec as P


Z, Y = "tensor_0", "tensor_1"
TENSOR = (Z, Y)
NZ, NY, NX = 8, 4, 4
ROWS, WIDTH, TILE = 512, 256, 256
WINDOW = 256
IDROWS = 16
VARS, RANK, BLK = 32, 64, 128
HOPS = (1, 3, 2)
F32, BF16 = jnp.float32, jnp.bfloat16
ANY = pl.BlockSpec(memory_space=pl.ANY)
HBM = pl.BlockSpec(memory_space=pltpu.HBM)
SMEM = pl.BlockSpec(memory_space=pltpu.SMEM)


def shift(value, axis, steps):
    count = lax.axis_size(axis)
    return lax.ppermute(value, axis, [(i, (i + steps) % count) for i in range(count)])


def cost(flops, nbytes):
    return pl.CostEstimate(flops=flops, bytes_accessed=nbytes, transcendentals=0)


def shape(dims, dtype=BF16):
    return pltpu.VMEM(dims, dtype)


def whole(dims, at=None):
    at = at or (0,) * len(dims)
    return pl.BlockSpec(dims, lambda: at)


def tiles_of(group):
    z = lax.axis_index(Z)
    return lax.rem(z + (4 - group), NZ), lax.rem(z + (group + NZ - 3), NZ)


def column(ztile, ytile):
    return pl.multiple_of((ztile * NY + ytile) * TILE, TILE)


def placed(value, spec):
    space = pltpu.HBM if spec is HBM else pltpu.VMEM
    if spec is SMEM:
        return value
    return pltpu.with_memory_space_constraint(value, space)


def call(kernel, args, in_specs, outs, out_specs, scratch, work, limit, after=()):
    n, m = len(args), len(after)
    args = [placed(arg, spec) for arg, spec in zip(args, in_specs)]

    def body(*refs):
        kernel(*refs[:n], *refs[n + m :])

    return pl.pallas_call(
        body,
        out_shape=outs,
        in_specs=list(in_specs) + [ANY] * m,
        out_specs=out_specs,
        scratch_shapes=scratch,
        cost_estimate=cost(*work),
        compiler_params=pltpu.CompilerParams(vmem_limit_bytes=limit << 20),
    )(*args, *after)


def parity():
    return lax.rem(lax.axis_index("pool"), 2)


def pack_kernel(groups, ahead, *refs):
    w_ref = refs[0]
    n_in = 2 if ahead else 1
    outs = refs[n_in : n_in + 3]
    owns = refs[n_in + 3 : n_in + 3 + len(groups)]
    sems = refs[-1]
    y, odd = lax.axis_index(Y), parity()
    copies = []
    for gi, group in enumerate(groups):
        plus, minus = tiles_of(group)
        wanted = (plus, minus) if ahead else (plus * (1 - odd) + minus * odd,)
        for ki, hop in enumerate(HOPS):
            if ahead:
                copies.append((refs[1], outs[ki].at[pl.ds(0, ROWS), :]))
            for ti, ztile in enumerate(wanted):
                source = w_ref.at[:, pl.ds(column(ztile, lax.rem(y + hop, NY)), TILE)]
                first = ahead + (gi + ti) * TILE
                copies.append((source, outs[ki].at[pl.ds(first, TILE), :]))
    for gi, group in enumerate(groups):
        for ti, ztile in enumerate(tiles_of(group)):
            source = w_ref.at[:, pl.ds(column(ztile, y), TILE)]
            copies.append((source, owns[gi].at[pl.ds(ti * TILE, TILE), :]))
    copies = [
        pltpu.make_async_copy(source, target, sems.at[i])
        for i, (source, target) in enumerate(copies)
    ]
    for copy in copies:
        copy.start()
    for copy in copies:
        copy.wait()


def pack(groups, weight, features=None, after=()):
    args, specs, rows = [weight], [HBM], len(groups) * TILE
    ahead = 0
    if features is not None:
        ahead, rows = ROWS, ROWS + 2 * TILE
        args.append(features)
        specs.append(HBM)
    dims = [(rows, TILE)] * 3 + [(2 * TILE, TILE)] * len(groups)
    got = call(
        functools.partial(pack_kernel, groups, ahead),
        args,
        specs,
        [shape(d) for d in dims],
        [whole(d) for d in dims],
        [pltpu.SemaphoreType.DMA((11 if ahead else 5 * len(groups),))],
        (0, 6 * rows * TILE),
        8,
        after,
    )
    return got[:3], got[3:]


def join_kernel(base, halves, a_ref, b_ref, c_ref, *outs):
    pos = 0
    for gi, split in enumerate(halves):
        for ki, ref in enumerate((a_ref, b_ref, c_ref)):
            first = base + gi * TILE
            if split:
                for side in range(2):
                    rows = slice(first + side * BLK, first + (side + 1) * BLK)
                    outs[pos + side][ki * BLK : (ki + 1) * BLK, :] = ref[rows, :]
            else:
                outs[pos][ki * TILE : (ki + 1) * TILE, :] = ref[first : first + TILE, :]
        pos += 2 if split else 1


def join(got, base, halves, after=()):
    dims = []
    for split in halves:
        dims += [(3 * BLK, TILE)] * 2 if split else [(3 * TILE, TILE)]
    return call(
        functools.partial(join_kernel, base, halves),
        tuple(got),
        [whole(got[0].shape)] * 3,
        [shape(d) for d in dims],
        [whole(d) for d in dims],
        [],
        (0, 3 << 20),
        4,
        after,
    )


def swapped(value, second_pairing):
    if second_pairing:
        pairs = [(0, 3), (3, 0), (1, 2), (2, 1)]
    else:
        pairs = [(0, 1), (1, 0), (2, 3), (3, 2)]
    return lax.ppermute(value, "pool", pairs)


def stacked(refs):
    if len(refs) == 1:
        return refs[0][...]
    low, high = refs
    pieces = []
    for ki in range(3):
        rows = slice(ki * BLK, (ki + 1) * BLK)
        pieces += [low[rows, :], high[rows, :]]
    return jnp.concatenate(pieces, axis=0)


def project_kernel(which, has_in, parts, own_ref, x_ref, p0, p1, p2, *refs):
    n = len(which)
    even = parity() == 0
    if parts:
        mine, other = stacked(refs[:parts]), stacked(refs[parts : 2 * parts])
    refs = refs[2 * parts :]
    carried, outs = (refs[:n], refs[n:]) if has_in else ((None,) * n, refs)
    lhs = jnp.concatenate([x_ref[...]] + [peer[0:ROWS, :] for peer in (p0, p1, p2)], axis=1)
    for c_ref, out, ti in zip(carried, outs, which):
        if parts == 0:
            rows = slice(ROWS + ti * TILE, ROWS + (ti + 1) * TILE)
            remote = jnp.concatenate([peer[rows, :] for peer in (p0, p1, p2)], axis=0)
        elif ti == 0:
            remote = lax.select(even, mine, other)
        else:
            remote = lax.select(even, other, mine)
        rhs = jnp.concatenate([own_ref[ti * TILE : (ti + 1) * TILE, :], remote], axis=0)
        total = jnp.dot(lhs, rhs, preferred_element_type=F32)
        if has_in:
            total = total + c_ref[...].astype(F32)
        out[...] = total.astype(out.dtype)


def project(which, own, features, first_got, mine, other, carried, after=(), out_dtype=BF16):
    half = (ROWS, WIDTH)
    n, parts = len(which), len(mine)
    return call(
        functools.partial(project_kernel, which, bool(carried), parts),
        (own, features, *first_got, *mine, *other, *carried),
        [whole(half)] * 2
        + [whole(first_got[0].shape)] * 3
        + [whole(value.shape) for value in (*mine, *other)]
        + [whole(half)] * len(carried),
        [shape((ROWS, TILE), out_dtype)] * n,
        [whole((ROWS, TILE))] * n,
        [],
        (2 * ROWS * 1024 * TILE * n, 2 << 20),
        8,
        after,
    )


def window_start(ids, owner):
    before = jnp.sum((ids < owner * VARS).astype(jnp.int32))
    return jnp.minimum(before, ROWS - WINDOW)


def dispatch_kernel(ids_ref, x_ref, *outs):
    me = lax.axis_index("pool")
    ids = ids_ref[...]
    features = x_ref[...]
    for k in range(NX):
        owner = lax.rem(me + k, NX)
        start = window_start(ids, owner)
        at = lax.broadcasted_iota(jnp.int32, (WINDOW, ROWS), 0) + start
        hot = (at == lax.broadcasted_iota(jnp.int32, (WINDOW, ROWS), 1)).astype(F32).astype(BF16)
        outs[k][0:WINDOW, :] = jnp.dot(hot, features, preferred_element_type=F32).astype(BF16)
        local = jnp.broadcast_to((ids - owner * VARS).astype(F32), (IDROWS, ROWS)).astype(BF16)
        outs[k][WINDOW : WINDOW + IDROWS, :] = lax.dot_general(
            local, hot, (((1,), (1,)), ((), ())), preferred_element_type=F32
        ).astype(BF16)


def dispatch(ids, features, after=()):
    return call(
        dispatch_kernel,
        (ids, features),
        [whole((1, ROWS)), whole((ROWS, WIDTH))],
        [shape((WINDOW + IDROWS, WIDTH))] * NX,
        [whole((WINDOW + IDROWS, WIDTH))] * NX,
        [],
        (2 * 1024 * 512 * 256, 1 << 20),
        6,
        after,
    )


def spread_columns(row, lanes):
    diagonal = lax.broadcasted_iota(jnp.int32, (WINDOW, WINDOW), 0) == lax.broadcasted_iota(
        jnp.int32, (WINDOW, WINDOW), 1
    )
    row = jnp.broadcast_to(row.astype(F32), (WINDOW, WINDOW))
    spread = jnp.where(diagonal, row, 0.0).astype(BF16)
    return jnp.dot(spread, jnp.ones((WINDOW, lanes), BF16), preferred_element_type=F32)


def variant_columns(item_ref, lanes):
    return spread_columns(item_ref[WINDOW : WINDOW + 1, :], lanes)


def down_kernel(i0, i1, i2, i3, down_ref, out_ref, item_ref, fold_ref):
    for k, item in enumerate((i0, i1, i2, i3)):
        item_ref[k] = item[...]
    lane = lax.broadcasted_iota(jnp.int32, (1, 256), 1)
    part = lax.div(lane, jnp.int32(RANK)).astype(F32)

    def window(k, carry):
        item = item_ref.at[k]
        variant = variant_columns(item, 256)
        features = item[0:WINDOW, :]
        total = None
        for j in range(VARS * RANK // 256):
            value = lax.dot_general(
                features,
                down_ref[j * 256 : (j + 1) * 256, :],
                (((1,), (1,)), ((), ())),
                preferred_element_type=F32,
            )
            value = jnp.where(variant == part + float(j * 4), value, 0.0)
            total = value if total is None else total + value
        two = total[:, 0:128] + total[:, 128:256]
        fold_ref[k] = two + pltpu.roll(two, RANK, 1)
        return carry

    lax.fori_loop(0, NX, window, 0)
    low = lax.broadcasted_iota(jnp.int32, (WINDOW, 128), 1) < RANK
    for h in range(2):
        packed = jnp.where(low, fold_ref[h], fold_ref[h + 2]).astype(BF16)
        out_ref[:, h * 128 : (h + 1) * 128] = packed


def down(items, factor, after=()):
    return call(
        down_kernel,
        (*items, factor),
        [whole((WINDOW + IDROWS, WIDTH))] * NX + [whole((VARS * RANK, WIDTH))],
        shape((WINDOW, 256)),
        whole((WINDOW, 256)),
        [pltpu.VMEM((NX, WINDOW + IDROWS, WIDTH), BF16), pltpu.VMEM((NX, WINDOW, 128), F32)],
        (2 * 1024 * 256 * 2048, 2 << 20),
        8,
        after,
    )


def block_kernel(i0, i1, i2, i3, mats_ref, place_ref, out_ref, item_ref, rhs_ref):
    for k, item in enumerate((i0, i1, i2, i3)):
        item_ref[k] = item[...]
    shard = lax.axis_index(Z) * NY + lax.axis_index(Y)

    def lanes_of(v):
        return pl.ds(pl.multiple_of((place_ref[v] - shard * 2) * BLK, BLK), BLK)

    for v in range(VARS):
        rhs_ref[v * BLK : (v + 1) * BLK, :] = jnp.zeros((BLK, 256), BF16)
        rhs_ref[v * BLK : (v + 1) * BLK, lanes_of(v)] = mats_ref[v]

    def window(k, carry):
        item = item_ref.at[k]
        variant = variant_columns(item, 128)
        pieces = []
        for v in range(VARS):
            piece = item[0:WINDOW, lanes_of(v)].astype(F32)
            pieces.append(jnp.where(variant == float(v), piece, 0.0).astype(BF16))
        lhs = jnp.concatenate(pieces, axis=1)
        out_ref[k] = jnp.dot(lhs, rhs_ref[...], preferred_element_type=F32)
        return carry

    lax.fori_loop(0, NX, window, 0)


def block_terms(items, mats, places, after=()):
    return call(
        block_kernel,
        (*items, mats, places),
        [whole((WINDOW + IDROWS, WIDTH))] * NX + [whole((VARS, BLK, BLK)), SMEM],
        shape((NX, WINDOW, 256), F32),
        whole((NX, WINDOW, 256)),
        [pltpu.VMEM((NX, WINDOW + IDROWS, WIDTH), BF16), pltpu.VMEM((VARS * BLK, 256), BF16)],
        (2 * 1024 * 4096 * 256, 3 << 20),
        10,
        after,
    )


def add_kernel(a_ref, b_ref, out_ref):
    out_ref[...] = (a_ref[...].astype(F32) + b_ref[...].astype(F32)).astype(BF16)


def exchanged_sum(value, axis, bit, after=()):
    count = lax.axis_size(axis)
    other = lax.ppermute(value, axis, [(i, i ^ bit) for i in range(count)])
    return call(
        add_kernel,
        (value, other),
        [whole((WINDOW, 256))] * 2,
        shape((WINDOW, 256)),
        whole((WINDOW, 256)),
        [],
        (1 << 16, 3 << 17),
        2,
        after,
    )


def up_kernel(i0, i1, i2, i3, l0, l1, l2, l3, up_ref, block_ref, *refs):
    outs, (item_ref, two_ref, out_ref) = refs[:NX], refs[NX:]
    low = l0[...].astype(F32) + l1[...].astype(F32) + l2[...].astype(F32) + l3[...].astype(F32)
    low = low.astype(BF16).astype(F32)
    for k, item in enumerate((i0, i1, i2, i3)):
        item_ref[k] = item[WINDOW : WINDOW + IDROWS, :]
    first = lax.broadcasted_iota(jnp.int32, (WINDOW, 128), 1) < RANK
    for h in range(2):
        packed = low[:, h * 128 : (h + 1) * 128]
        turned = pltpu.roll(packed, RANK, 1)
        two_ref[h] = jnp.where(first, packed, turned)
        two_ref[h + 2] = jnp.where(first, turned, packed)
    half = lax.div(lax.broadcasted_iota(jnp.int32, (1, 128), 1), jnp.int32(RANK)).astype(F32)

    def window(k, carry):
        variant = spread_columns(item_ref[k, 0:1, :], 128)
        two = two_ref[k]
        pieces = []
        for i in range(VARS // 2):
            pieces.append(jnp.where(variant == half + float(2 * i), two, 0.0).astype(BF16))
        lhs = jnp.concatenate(pieces, axis=1)
        total = block_ref[k] + jnp.dot(lhs, up_ref[...], preferred_element_type=F32)
        out_ref[k] = total.astype(BF16)
        return carry

    lax.fori_loop(0, NX, window, 0)
    for k in range(NX):
        outs[k][...] = out_ref[k]


def up(items, lows, factor, blocks, after=()):
    return call(
        up_kernel,
        (*items, *lows, factor, blocks),
        [whole((WINDOW + IDROWS, WIDTH))] * NX
        + [whole((WINDOW, 256))] * 4
        + [whole((VARS * RANK, WIDTH)), whole((NX, WINDOW, 256))],
        [shape((WINDOW, WIDTH))] * NX,
        [whole((WINDOW, WIDTH))] * NX,
        [
            pltpu.VMEM((NX, IDROWS, WIDTH), BF16),
            pltpu.VMEM((NX, WINDOW, 128), F32),
            pltpu.VMEM((NX, WINDOW, WIDTH), BF16),
        ],
        (2 * 1024 * 256 * 2048, 3 << 20),
        10,
        after,
    )


def combine_kernel(ids_ref, h_ref, own_ref, plus_ref, r0, r1, r2, r3, first_ref, branch_ref):
    me = lax.axis_index("pool")
    ids = ids_ref[...]
    branch = own_ref[...] + plus_ref[...].astype(F32)
    delta = None
    for k, back in enumerate((r0, r1, r2, r3)):
        start = window_start(ids, lax.rem(me + k, NX))
        at = lax.broadcasted_iota(jnp.int32, (ROWS, WINDOW), 1) + start
        hot = (at == lax.broadcasted_iota(jnp.int32, (ROWS, WINDOW), 0)).astype(F32).astype(BF16)
        part = jnp.dot(hot, back[...], preferred_element_type=F32)
        delta = part if delta is None else delta + part
    branch = branch + delta
    branch_ref[...] = branch
    first_ref[...] = (h_ref[...].astype(F32) + branch).astype(BF16)


def combine(ids, hidden, own, plus, returned, after=()):
    half = (ROWS, WIDTH)
    return call(
        combine_kernel,
        (ids, hidden, own, plus, *returned),
        [whole((1, ROWS))] + [whole(half)] * 3 + [whole((WINDOW, WIDTH))] * NX,
        [shape(half), shape(half, F32)],
        [whole(half)] * 2,
        [],
        (2 * 512 * 1024 * 256, 2 << 20),
        8,
        after,
    )


def steps(
    hidden_input,
    attention_output,
    projection_weight,
    lowrank_down_factor,
    lowrank_up_factor,
    residual_block_mats,
    diagonal_block_index,
    row_variant_index,
):
    features = attention_output[0]
    weight = projection_weight[0]
    down_factor = lowrank_down_factor[0].reshape(VARS * RANK, WIDTH)
    up_factor = lowrank_up_factor[0].reshape(VARS * RANK, WIDTH)
    mats = residual_block_mats[0][:, 0]
    places = diagonal_block_index[0][:, 0]
    ids = row_variant_index.reshape(1, ROWS)

    first, (own0,) = pack((0,), weight, features)
    got = [shift(value, Y, hop) for value, hop in zip(first, HOPS)]
    sent = dispatch(ids, features, (first[0],))
    items = [sent[0]] + [shift(sent[k], "pool", k) for k in (1, 2, 3)]
    second, (own1,) = pack((1,), weight, None, (sent[0],))
    got1 = [shift(value, Y, hop) for value, hop in zip(second, HOPS)]
    low = down(items, down_factor, (second[0],))
    third, (own2, own3) = pack((2, 3), weight, None, (low,))
    got2 = [shift(value, Y, hop) for value, hop in zip(third, HOPS)]
    low1 = exchanged_sum(low, Z, 1)
    low2 = exchanged_sum(low1, Z, 2)
    plus, minus = project((0, 1), own0, features, got, (), (), (), (low1,))
    carried = (shift(plus, Z, 1), shift(minus, Z, -1))
    mine1 = join(got1, 0, (True,), (plus,))
    other1 = (shift(mine1[0], "pool", 1), shift(mine1[1], "pool", -1))
    low3 = exchanged_sum(low2, Z, 4)
    plus, minus = project((0, 1), own1, features, got, mine1, other1, carried)
    mine2, mine3 = join(got2, 0, (False, False), (plus,))
    other2 = swapped(mine2, False)
    carried = (shift(plus, Z, 1), shift(minus, Z, -1))
    other3 = swapped(mine3, True)
    lows = [low3] + [shift(low3, Y, hop) for hop in HOPS]
    blocks = block_terms(items, mats, places, (plus,))
    plus, minus = project((0, 1), own2, features, got, (mine2,), (other2,), carried, (blocks,))
    carried = (shift(plus, Z, 1), shift(minus, Z, -1))
    served = up(items, lows, up_factor, blocks, (plus,))
    returned = [served[0]] + [shift(served[k], "pool", -k) for k in (1, 2, 3)]
    (plus,) = project(
        (0,), own3, features, got, (mine3,), (other3,), carried[:1], (served[1],)
    )
    arrived = shift(plus, Z, 1)
    (own,) = project(
        (1,), own3, features, got, (mine3,), (other3,), carried[1:], (plus,), F32
    )
    plus = arrived

    first_out, branch = combine(ids, hidden_input, own, plus, returned)
    carried = lax.ppermute(first_out, "section", [(0, 1)])
    begin = jnp.where(lax.axis_index("section") == 0, hidden_input, carried)
    return (begin.astype(F32) + branch).astype(BF16)[None]


def solution(mesh):
    finer = Mesh(
        mesh.devices.reshape(mesh.shape["pool"], mesh.shape["section"], NZ, NY),
        ("pool", "section", Z, Y),
    )
    placed = (
        P("pool", TENSOR),
        P("section", "pool", TENSOR),
        P("section", TENSOR, None),
        P("section", "pool", None, TENSOR),
        P("section", "pool", None, TENSOR),
        P("section", "pool", TENSOR, None, None),
        P("section", "pool", TENSOR),
        P("pool"),
    )
    return jax.shard_map(
        steps,
        mesh=finer,
        in_specs=placed,
        out_specs=P("section", "pool", TENSOR),
        check_vma=False,
    )
```

```python
import functools

import jax
import jax.numpy as jnp
from jax import lax
from jax.experimental import pallas as pl
from jax.experimental.pallas import tpu as pltpu
from jax.sharding import Mesh
from jax.sharding import PartitionSpec as P


Z, Y = "tensor_0", "tensor_1"
TENSOR = (Z, Y)
NZ, NY, NX = 8, 4, 4
ROWS, WIDTH, TILE = 512, 256, 256
WINDOW = 256
IDROWS = 16
VARS, RANK, BLK = 32, 64, 128
HOPS = (1, 3, 2)
F32, BF16 = jnp.float32, jnp.bfloat16
ANY = pl.BlockSpec(memory_space=pl.ANY)
HBM = pl.BlockSpec(memory_space=pltpu.HBM)
SMEM = pl.BlockSpec(memory_space=pltpu.SMEM)


def shift(value, axis, steps):
    count = lax.axis_size(axis)
    return lax.ppermute(value, axis, [(i, (i + steps) % count) for i in range(count)])


def cost(flops, nbytes):
    return pl.CostEstimate(flops=flops, bytes_accessed=nbytes, transcendentals=0)


def shape(dims, dtype=BF16):
    return pltpu.VMEM(dims, dtype)


def whole(dims, at=None):
    at = at or (0,) * len(dims)
    return pl.BlockSpec(dims, lambda: at)


def tiles_of(group):
    z = lax.axis_index(Z)
    return lax.rem(z + (4 - group), NZ), lax.rem(z + (group + NZ - 3), NZ)


def column(ztile, ytile):
    return pl.multiple_of((ztile * NY + ytile) * TILE, TILE)


def placed(value, spec):
    space = pltpu.HBM if spec is HBM else pltpu.VMEM
    if spec is SMEM:
        return value
    return pltpu.with_memory_space_constraint(value, space)


def call(kernel, args, in_specs, outs, out_specs, scratch, work, limit, after=()):
    n, m = len(args), len(after)
    args = [placed(arg, spec) for arg, spec in zip(args, in_specs)]

    def body(*refs):
        kernel(*refs[:n], *refs[n + m :])

    return pl.pallas_call(
        body,
        out_shape=outs,
        in_specs=list(in_specs) + [ANY] * m,
        out_specs=out_specs,
        scratch_shapes=scratch,
        cost_estimate=cost(*work),
        compiler_params=pltpu.CompilerParams(vmem_limit_bytes=limit << 20),
    )(*args, *after)


def parity():
    return lax.rem(lax.axis_index("pool"), 2)


def pack_kernel(groups, ahead, *refs):
    w_ref = refs[0]
    n_in = 2 if ahead else 1
    outs = refs[n_in : n_in + 3]
    owns = refs[n_in + 3 : n_in + 3 + len(groups)]
    sems = refs[-1]
    y, odd = lax.axis_index(Y), parity()
    copies = []
    for gi, group in enumerate(groups):
        plus, minus = tiles_of(group)
        wanted = (plus, minus) if ahead else (plus * (1 - odd) + minus * odd,)
        for ki, hop in enumerate(HOPS):
            if ahead:
                copies.append((refs[1], outs[ki].at[pl.ds(0, ROWS), :]))
            for ti, ztile in enumerate(wanted):
                source = w_ref.at[:, pl.ds(column(ztile, lax.rem(y + hop, NY)), TILE)]
                first = ahead + (gi + ti) * TILE
                copies.append((source, outs[ki].at[pl.ds(first, TILE), :]))
    for gi, group in enumerate(groups):
        for ti, ztile in enumerate(tiles_of(group)):
            source = w_ref.at[:, pl.ds(column(ztile, y), TILE)]
            copies.append((source, owns[gi].at[pl.ds(ti * TILE, TILE), :]))
    copies = [
        pltpu.make_async_copy(source, target, sems.at[i])
        for i, (source, target) in enumerate(copies)
    ]
    for copy in copies:
        copy.start()
    for copy in copies:
        copy.wait()


def pack(groups, weight, features=None, after=()):
    args, specs, rows = [weight], [HBM], len(groups) * TILE
    ahead = 0
    if features is not None:
        ahead, rows = ROWS, ROWS + 2 * TILE
        args.append(features)
        specs.append(HBM)
    dims = [(rows, TILE)] * 3 + [(2 * TILE, TILE)] * len(groups)
    got = call(
        functools.partial(pack_kernel, groups, ahead),
        args,
        specs,
        [shape(d) for d in dims],
        [whole(d) for d in dims],
        [pltpu.SemaphoreType.DMA((11 if ahead else 5 * len(groups),))],
        (0, 6 * rows * TILE),
        8,
        after,
    )
    return got[:3], got[3:]


def join_kernel(base, halves, a_ref, b_ref, c_ref, *outs):
    pos = 0
    for gi, split in enumerate(halves):
        for ki, ref in enumerate((a_ref, b_ref, c_ref)):
            first = base + gi * TILE
            if split:
                for side in range(2):
                    rows = slice(first + side * BLK, first + (side + 1) * BLK)
                    outs[pos + side][ki * BLK : (ki + 1) * BLK, :] = ref[rows, :]
            else:
                outs[pos][ki * TILE : (ki + 1) * TILE, :] = ref[first : first + TILE, :]
        pos += 2 if split else 1


def join(got, base, halves, after=()):
    dims = []
    for split in halves:
        dims += [(3 * BLK, TILE)] * 2 if split else [(3 * TILE, TILE)]
    return call(
        functools.partial(join_kernel, base, halves),
        tuple(got),
        [whole(got[0].shape)] * 3,
        [shape(d) for d in dims],
        [whole(d) for d in dims],
        [],
        (0, 3 << 20),
        4,
        after,
    )


def swapped(value, second_pairing):
    if second_pairing:
        pairs = [(0, 3), (3, 0), (1, 2), (2, 1)]
    else:
        pairs = [(0, 1), (1, 0), (2, 3), (3, 2)]
    return lax.ppermute(value, "pool", pairs)


def stacked(refs):
    if len(refs) == 1:
        return refs[0][...]
    low, high = refs
    pieces = []
    for ki in range(3):
        rows = slice(ki * BLK, (ki + 1) * BLK)
        pieces += [low[rows, :], high[rows, :]]
    return jnp.concatenate(pieces, axis=0)


def project_kernel(which, has_in, parts, own_ref, x_ref, p0, p1, p2, *refs):
    n = len(which)
    even = parity() == 0
    if parts:
        mine, other = stacked(refs[:parts]), stacked(refs[parts : 2 * parts])
    refs = refs[2 * parts :]
    carried, outs = (refs[:n], refs[n:]) if has_in else ((None,) * n, refs)
    lhs = jnp.concatenate([x_ref[...]] + [peer[0:ROWS, :] for peer in (p0, p1, p2)], axis=1)
    for c_ref, out, ti in zip(carried, outs, which):
        if parts == 0:
            rows = slice(ROWS + ti * TILE, ROWS + (ti + 1) * TILE)
            remote = jnp.concatenate([peer[rows, :] for peer in (p0, p1, p2)], axis=0)
        elif ti == 0:
            remote = lax.select(even, mine, other)
        else:
            remote = lax.select(even, other, mine)
        rhs = jnp.concatenate([own_ref[ti * TILE : (ti + 1) * TILE, :], remote], axis=0)
        total = jnp.dot(lhs, rhs, preferred_element_type=F32)
        if has_in:
            total = total + c_ref[...].astype(F32)
        out[...] = total.astype(out.dtype)


def project(which, own, features, first_got, mine, other, carried, after=(), out_dtype=BF16):
    half = (ROWS, WIDTH)
    n, parts = len(which), len(mine)
    return call(
        functools.partial(project_kernel, which, bool(carried), parts),
        (own, features, *first_got, *mine, *other, *carried),
        [whole(half)] * 2
        + [whole(first_got[0].shape)] * 3
        + [whole(value.shape) for value in (*mine, *other)]
        + [whole(half)] * len(carried),
        [shape((ROWS, TILE), out_dtype)] * n,
        [whole((ROWS, TILE))] * n,
        [],
        (2 * ROWS * 1024 * TILE * n, 2 << 20),
        8,
        after,
    )


def window_start(ids, owner):
    before = jnp.sum((ids < owner * VARS).astype(jnp.int32))
    return jnp.minimum(before, ROWS - WINDOW)


def dispatch_kernel(ids_ref, x_ref, *outs):
    me = lax.axis_index("pool")
    ids = ids_ref[...]
    features = x_ref[...]
    for k in range(NX):
        owner = lax.rem(me + k, NX)
        start = window_start(ids, owner)
        at = lax.broadcasted_iota(jnp.int32, (WINDOW, ROWS), 0) + start
        hot = (at == lax.broadcasted_iota(jnp.int32, (WINDOW, ROWS), 1)).astype(F32).astype(BF16)
        outs[k][0:WINDOW, :] = jnp.dot(hot, features, preferred_element_type=F32).astype(BF16)
        local = jnp.broadcast_to((ids - owner * VARS).astype(F32), (IDROWS, ROWS)).astype(BF16)
        outs[k][WINDOW : WINDOW + IDROWS, :] = lax.dot_general(
            local, hot, (((1,), (1,)), ((), ())), preferred_element_type=F32
        ).astype(BF16)


def dispatch(ids, features, after=()):
    return call(
        dispatch_kernel,
        (ids, features),
        [whole((1, ROWS)), whole((ROWS, WIDTH))],
        [shape((WINDOW + IDROWS, WIDTH))] * NX,
        [whole((WINDOW + IDROWS, WIDTH))] * NX,
        [],
        (2 * 1024 * 512 * 256, 1 << 20),
        6,
        after,
    )


def spread_columns(row, lanes):
    diagonal = lax.broadcasted_iota(jnp.int32, (WINDOW, WINDOW), 0) == lax.broadcasted_iota(
        jnp.int32, (WINDOW, WINDOW), 1
    )
    row = jnp.broadcast_to(row.astype(F32), (WINDOW, WINDOW))
    spread = jnp.where(diagonal, row, 0.0).astype(BF16)
    return jnp.dot(spread, jnp.ones((WINDOW, lanes), BF16), preferred_element_type=F32)


def variant_columns(item_ref, lanes):
    return spread_columns(item_ref[WINDOW : WINDOW + 1, :], lanes)


def down_kernel(i0, i1, i2, i3, down_ref, out_ref, item_ref, fold_ref):
    for k, item in enumerate((i0, i1, i2, i3)):
        item_ref[k] = item[...]
    lane = lax.broadcasted_iota(jnp.int32, (1, 256), 1)
    part = lax.div(lane, jnp.int32(RANK)).astype(F32)

    def window(k, carry):
        item = item_ref.at[k]
        variant = variant_columns(item, 256)
        features = item[0:WINDOW, :]
        total = None
        for j in range(VARS * RANK // 256):
            value = lax.dot_general(
                features,
                down_ref[j * 256 : (j + 1) * 256, :],
                (((1,), (1,)), ((), ())),
                preferred_element_type=F32,
            )
            value = jnp.where(variant == part + float(j * 4), value, 0.0)
            total = value if total is None else total + value
        two = total[:, 0:128] + total[:, 128:256]
        fold_ref[k] = two + pltpu.roll(two, RANK, 1)
        return carry

    lax.fori_loop(0, NX, window, 0)
    low = lax.broadcasted_iota(jnp.int32, (WINDOW, 128), 1) < RANK
    for h in range(2):
        packed = jnp.where(low, fold_ref[h], fold_ref[h + 2]).astype(BF16)
        out_ref[:, h * 128 : (h + 1) * 128] = packed


def down(items, factor, after=()):
    return call(
        down_kernel,
        (*items, factor),
        [whole((WINDOW + IDROWS, WIDTH))] * NX + [whole((VARS * RANK, WIDTH))],
        shape((WINDOW, 256)),
        whole((WINDOW, 256)),
        [pltpu.VMEM((NX, WINDOW + IDROWS, WIDTH), BF16), pltpu.VMEM((NX, WINDOW, 128), F32)],
        (2 * 1024 * 256 * 2048, 2 << 20),
        8,
        after,
    )


def block_kernel(i0, i1, i2, i3, mats_ref, place_ref, out_ref, item_ref, rhs_ref):
    for k, item in enumerate((i0, i1, i2, i3)):
        item_ref[k] = item[...]
    shard = lax.axis_index(Z) * NY + lax.axis_index(Y)
    for v in range(VARS):
        first = (v // 2) * BLK
        lanes = slice((v % 2) * BLK, (v % 2 + 1) * BLK)
        rhs_ref[first : first + BLK, lanes] = mats_ref[v]

    def window(k, carry):
        item = item_ref.at[k]
        ids = item[WINDOW : WINDOW + 1, :].astype(F32)
        code = jnp.full(ids.shape, 64.0, F32)
        for v in range(VARS):
            place = (place_ref[v] - shard * 2).astype(F32)
            code = jnp.where(ids == float(v), v // 2 + 16.0 * (v % 2) + 32.0 * place, code)
        code = spread_columns(code, 128)
        upper = (code >= 32.0) & (code < 64.0)
        rest = jnp.where(upper, code - 32.0, code)
        odd = rest >= 16.0
        pair = jnp.where(odd, rest - 16.0, rest).astype(BF16)
        low = item[0:WINDOW, 0:BLK].astype(F32)
        high = item[0:WINDOW, BLK : 2 * BLK].astype(F32)
        picked = jnp.where(upper, high, low).astype(BF16)
        zero = jnp.zeros_like(picked)
        pieces = [jnp.where(pair == jnp.bfloat16(p), picked, zero) for p in range(VARS // 2)]
        both = jnp.dot(jnp.concatenate(pieces, axis=1), rhs_ref[...], preferred_element_type=F32)
        one = jnp.where(odd, both[:, BLK:], both[:, 0:BLK])
        out_ref[k, :, 0:BLK] = jnp.where(upper, 0.0, one)
        out_ref[k, :, BLK : 2 * BLK] = jnp.where(upper, one, 0.0)
        return carry

    lax.fori_loop(0, NX, window, 0)


def block_terms(items, mats, places, after=()):
    return call(
        block_kernel,
        (*items, mats, places),
        [whole((WINDOW + IDROWS, WIDTH))] * NX + [whole((VARS, BLK, BLK)), SMEM],
        shape((NX, WINDOW, 256), F32),
        whole((NX, WINDOW, 256)),
        [pltpu.VMEM((NX, WINDOW + IDROWS, WIDTH), BF16), pltpu.VMEM((VARS * BLK // 2, 256), BF16)],
        (2 * 1024 * 2048 * 256, 3 << 20),
        10,
        after,
    )


def add_kernel(a_ref, b_ref, out_ref):
    out_ref[...] = (a_ref[...].astype(F32) + b_ref[...].astype(F32)).astype(BF16)


def exchanged_sum(value, axis, bit, after=()):
    count = lax.axis_size(axis)
    other = lax.ppermute(value, axis, [(i, i ^ bit) for i in range(count)])
    return call(
        add_kernel,
        (value, other),
        [whole((WINDOW, 256))] * 2,
        shape((WINDOW, 256)),
        whole((WINDOW, 256)),
        [],
        (1 << 16, 3 << 17),
        2,
        after,
    )


def up_kernel(i0, i1, i2, i3, l0, l1, l2, l3, up_ref, block_ref, *refs):
    outs, (item_ref, two_ref, out_ref) = refs[:NX], refs[NX:]
    low = l0[...].astype(F32) + l1[...].astype(F32) + l2[...].astype(F32) + l3[...].astype(F32)
    low = low.astype(BF16).astype(F32)
    for k, item in enumerate((i0, i1, i2, i3)):
        item_ref[k] = item[WINDOW : WINDOW + IDROWS, :]
    first = lax.broadcasted_iota(jnp.int32, (WINDOW, 128), 1) < RANK
    for h in range(2):
        packed = low[:, h * 128 : (h + 1) * 128]
        turned = pltpu.roll(packed, RANK, 1)
        two_ref[h] = jnp.where(first, packed, turned)
        two_ref[h + 2] = jnp.where(first, turned, packed)
    half = lax.div(lax.broadcasted_iota(jnp.int32, (1, 128), 1), jnp.int32(RANK)).astype(F32)

    def window(k, carry):
        variant = (spread_columns(item_ref[k, 0:1, :], 128) - half).astype(BF16)
        two = two_ref[k].astype(BF16)
        zero = jnp.zeros_like(two)
        pieces = []
        for i in range(VARS // 2):
            pieces.append(jnp.where(variant == jnp.bfloat16(2 * i), two, zero))
        lhs = jnp.concatenate(pieces, axis=1)
        total = block_ref[k] + jnp.dot(lhs, up_ref[...], preferred_element_type=F32)
        out_ref[k] = total.astype(BF16)
        return carry

    lax.fori_loop(0, NX, window, 0)
    for k in range(NX):
        outs[k][...] = out_ref[k]


def up(items, lows, factor, blocks, after=()):
    return call(
        up_kernel,
        (*items, *lows, factor, blocks),
        [whole((WINDOW + IDROWS, WIDTH))] * NX
        + [whole((WINDOW, 256))] * 4
        + [whole((VARS * RANK, WIDTH)), whole((NX, WINDOW, 256))],
        [shape((WINDOW, WIDTH))] * NX,
        [whole((WINDOW, WIDTH))] * NX,
        [
            pltpu.VMEM((NX, IDROWS, WIDTH), BF16),
            pltpu.VMEM((NX, WINDOW, 128), F32),
            pltpu.VMEM((NX, WINDOW, WIDTH), BF16),
        ],
        (2 * 1024 * 256 * 2048, 3 << 20),
        10,
        after,
    )


def combine_kernel(ids_ref, h_ref, own_ref, plus_ref, r0, r1, r2, r3, first_ref, branch_ref):
    me = lax.axis_index("pool")
    ids = ids_ref[...]
    branch = own_ref[...] + plus_ref[...].astype(F32)
    delta = None
    for k, back in enumerate((r0, r1, r2, r3)):
        start = window_start(ids, lax.rem(me + k, NX))
        at = lax.broadcasted_iota(jnp.int32, (ROWS, WINDOW), 1) + start
        hot = (at == lax.broadcasted_iota(jnp.int32, (ROWS, WINDOW), 0)).astype(F32).astype(BF16)
        part = jnp.dot(hot, back[...], preferred_element_type=F32)
        delta = part if delta is None else delta + part
    branch = branch + delta
    branch_ref[...] = branch
    first_ref[...] = (h_ref[...].astype(F32) + branch).astype(BF16)


def combine(ids, hidden, own, plus, returned, after=()):
    half = (ROWS, WIDTH)
    return call(
        combine_kernel,
        (ids, hidden, own, plus, *returned),
        [whole((1, ROWS))] + [whole(half)] * 3 + [whole((WINDOW, WIDTH))] * NX,
        [shape(half), shape(half, F32)],
        [whole(half)] * 2,
        [],
        (2 * 512 * 1024 * 256, 2 << 20),
        8,
        after,
    )


def steps(
    hidden_input,
    attention_output,
    projection_weight,
    lowrank_down_factor,
    lowrank_up_factor,
    residual_block_mats,
    diagonal_block_index,
    row_variant_index,
):
    features = attention_output[0]
    weight = projection_weight[0]
    down_factor = lowrank_down_factor[0].reshape(VARS * RANK, WIDTH)
    up_factor = lowrank_up_factor[0].reshape(VARS * RANK, WIDTH)
    mats = residual_block_mats[0][:, 0]
    places = diagonal_block_index[0][:, 0]
    ids = row_variant_index.reshape(1, ROWS)

    first, (own0,) = pack((0,), weight, features)
    got = [shift(value, Y, hop) for value, hop in zip(first, HOPS)]
    sent = dispatch(ids, features, (first[0],))
    items = [sent[0]] + [shift(sent[k], "pool", k) for k in (1, 2, 3)]
    second, (own1,) = pack((1,), weight, None, (sent[0],))
    got1 = [shift(value, Y, hop) for value, hop in zip(second, HOPS)]
    low = down(items, down_factor, (second[0],))
    third, (own2, own3) = pack((2, 3), weight, None, (low,))
    got2 = [shift(value, Y, hop) for value, hop in zip(third, HOPS)]
    low1 = exchanged_sum(low, Z, 1)
    low2 = exchanged_sum(low1, Z, 2)
    plus, minus = project((0, 1), own0, features, got, (), (), (), (low1,))
    carried = (shift(plus, Z, 1), shift(minus, Z, -1))
    mine1 = join(got1, 0, (True,), (plus,))
    other1 = (shift(mine1[0], "pool", 1), shift(mine1[1], "pool", -1))
    low3 = exchanged_sum(low2, Z, 4)
    plus, minus = project((0, 1), own1, features, got, mine1, other1, carried)
    mine2, mine3 = join(got2, 0, (False, False), (plus,))
    other2 = swapped(mine2, False)
    carried = (shift(plus, Z, 1), shift(minus, Z, -1))
    other3 = swapped(mine3, True)
    lows = [low3] + [shift(low3, Y, hop) for hop in HOPS]
    blocks = block_terms(items, mats, places, (plus,))
    plus, minus = project((0, 1), own2, features, got, (mine2,), (other2,), carried, (blocks,))
    carried = (shift(plus, Z, 1), shift(minus, Z, -1))
    served = up(items, lows, up_factor, blocks, (plus,))
    returned = [served[0]] + [shift(served[k], "pool", -k) for k in (1, 2, 3)]
    (plus,) = project(
        (0,), own3, features, got, (mine3,), (other3,), carried[:1], (served[1],)
    )
    arrived = shift(plus, Z, 1)
    (own,) = project(
        (1,), own3, features, got, (mine3,), (other3,), carried[1:], (plus,), F32
    )
    plus = arrived

    first_out, branch = combine(ids, hidden_input, own, plus, returned)
    carried = lax.ppermute(first_out, "section", [(0, 1)])
    begin = jnp.where(lax.axis_index("section") == 0, hidden_input, carried)
    return (begin.astype(F32) + branch).astype(BF16)[None]


def solution(mesh):
    finer = Mesh(
        mesh.devices.reshape(mesh.shape["pool"], mesh.shape["section"], NZ, NY),
        ("pool", "section", Z, Y),
    )
    placed = (
        P("pool", TENSOR),
        P("section", "pool", TENSOR),
        P("section", TENSOR, None),
        P("section", "pool", None, TENSOR),
        P("section", "pool", None, TENSOR),
        P("section", "pool", TENSOR, None, None),
        P("section", "pool", TENSOR),
        P("pool"),
    )
    return jax.shard_map(
        steps,
        mesh=finer,
        in_specs=placed,
        out_specs=P("section", "pool", TENSOR),
        check_vma=False,
    )
```

```python
import functools

import jax
import jax.numpy as jnp
from jax import lax
from jax.experimental import pallas as pl
from jax.experimental.pallas import tpu as pltpu
from jax.sharding import Mesh
from jax.sharding import PartitionSpec as P


Z, Y = "tensor_0", "tensor_1"
TENSOR = (Z, Y)
NZ, NY, NX = 8, 4, 4
ROWS, WIDTH, TILE = 512, 256, 256
WINDOW = 256
IDROWS = 16
VARS, RANK, BLK = 32, 64, 128
HOPS = (1, 3, 2)
F32, BF16 = jnp.float32, jnp.bfloat16
ANY = pl.BlockSpec(memory_space=pl.ANY)
HBM = pl.BlockSpec(memory_space=pltpu.HBM)
SMEM = pl.BlockSpec(memory_space=pltpu.SMEM)


def shift(value, axis, steps):
    count = lax.axis_size(axis)
    return lax.ppermute(value, axis, [(i, (i + steps) % count) for i in range(count)])


def cost(flops, nbytes):
    return pl.CostEstimate(flops=flops, bytes_accessed=nbytes, transcendentals=0)


def shape(dims, dtype=BF16):
    return pltpu.VMEM(dims, dtype)


def whole(dims, at=None):
    at = at or (0,) * len(dims)
    return pl.BlockSpec(dims, lambda: at)


def tiles_of(group):
    z = lax.axis_index(Z)
    return lax.rem(z + (4 - group), NZ), lax.rem(z + (group + NZ - 3), NZ)


def column(ztile, ytile):
    return pl.multiple_of((ztile * NY + ytile) * TILE, TILE)


def placed(value, spec):
    space = pltpu.HBM if spec is HBM else pltpu.VMEM
    if spec is SMEM:
        return value
    return pltpu.with_memory_space_constraint(value, space)


def call(kernel, args, in_specs, outs, out_specs, scratch, work, limit, after=()):
    n, m = len(args), len(after)
    args = [placed(arg, spec) for arg, spec in zip(args, in_specs)]

    def body(*refs):
        kernel(*refs[:n], *refs[n + m :])

    return pl.pallas_call(
        body,
        out_shape=outs,
        in_specs=list(in_specs) + [ANY] * m,
        out_specs=out_specs,
        scratch_shapes=scratch,
        cost_estimate=cost(*work),
        compiler_params=pltpu.CompilerParams(vmem_limit_bytes=limit << 20),
    )(*args, *after)


def parity():
    return lax.rem(lax.axis_index("pool"), 2)


def pack_kernel(groups, ahead, *refs):
    w_ref = refs[0]
    n_in = 2 if ahead else 1
    outs = refs[n_in : n_in + 3]
    owns = refs[n_in + 3 : n_in + 3 + len(groups)]
    sems = refs[-1]
    y, odd = lax.axis_index(Y), parity()
    copies = []
    for gi, group in enumerate(groups):
        plus, minus = tiles_of(group)
        wanted = (plus, minus) if ahead else (plus * (1 - odd) + minus * odd,)
        for ki, hop in enumerate(HOPS):
            if ahead:
                copies.append((refs[1], outs[ki].at[pl.ds(0, ROWS), :]))
            for ti, ztile in enumerate(wanted):
                source = w_ref.at[:, pl.ds(column(ztile, lax.rem(y + hop, NY)), TILE)]
                first = ahead + (gi + ti) * TILE
                copies.append((source, outs[ki].at[pl.ds(first, TILE), :]))
    for gi, group in enumerate(groups):
        for ti, ztile in enumerate(tiles_of(group)):
            source = w_ref.at[:, pl.ds(column(ztile, y), TILE)]
            copies.append((source, owns[gi].at[pl.ds(ti * TILE, TILE), :]))
    copies = [
        pltpu.make_async_copy(source, target, sems.at[i])
        for i, (source, target) in enumerate(copies)
    ]
    for copy in copies:
        copy.start()
    for copy in copies:
        copy.wait()


def pack(groups, weight, features=None, after=()):
    args, specs, rows = [weight], [HBM], len(groups) * TILE
    ahead = 0
    if features is not None:
        ahead, rows = ROWS, ROWS + 2 * TILE
        args.append(features)
        specs.append(HBM)
    dims = [(rows, TILE)] * 3 + [(2 * TILE, TILE)] * len(groups)
    got = call(
        functools.partial(pack_kernel, groups, ahead),
        args,
        specs,
        [shape(d) for d in dims],
        [whole(d) for d in dims],
        [pltpu.SemaphoreType.DMA((11 if ahead else 5 * len(groups),))],
        (0, 6 * rows * TILE),
        8,
        after,
    )
    return got[:3], got[3:]


def join_kernel(base, halves, a_ref, b_ref, c_ref, *outs):
    pos = 0
    for gi, split in enumerate(halves):
        for ki, ref in enumerate((a_ref, b_ref, c_ref)):
            first = base + gi * TILE
            if split:
                for side in range(2):
                    rows = slice(first + side * BLK, first + (side + 1) * BLK)
                    outs[pos + side][ki * BLK : (ki + 1) * BLK, :] = ref[rows, :]
            else:
                outs[pos][ki * TILE : (ki + 1) * TILE, :] = ref[first : first + TILE, :]
        pos += 2 if split else 1


def join(got, base, halves, after=()):
    dims = []
    for split in halves:
        dims += [(3 * BLK, TILE)] * 2 if split else [(3 * TILE, TILE)]
    return call(
        functools.partial(join_kernel, base, halves),
        tuple(got),
        [whole(got[0].shape)] * 3,
        [shape(d) for d in dims],
        [whole(d) for d in dims],
        [],
        (0, 3 << 20),
        4,
        after,
    )


def swapped(value, second_pairing):
    if second_pairing:
        pairs = [(0, 3), (3, 0), (1, 2), (2, 1)]
    else:
        pairs = [(0, 1), (1, 0), (2, 3), (3, 2)]
    return lax.ppermute(value, "pool", pairs)


def stacked(refs):
    if len(refs) == 1:
        return refs[0][...]
    low, high = refs
    pieces = []
    for ki in range(3):
        rows = slice(ki * BLK, (ki + 1) * BLK)
        pieces += [low[rows, :], high[rows, :]]
    return jnp.concatenate(pieces, axis=0)


def project_kernel(which, has_in, parts, own_ref, x_ref, p0, p1, p2, *refs):
    n = len(which)
    even = parity() == 0
    if parts:
        mine, other = stacked(refs[:parts]), stacked(refs[parts : 2 * parts])
    refs = refs[2 * parts :]
    carried, outs = (refs[:n], refs[n:]) if has_in else ((None,) * n, refs)
    lhs = jnp.concatenate([x_ref[...]] + [peer[0:ROWS, :] for peer in (p0, p1, p2)], axis=1)
    for c_ref, out, ti in zip(carried, outs, which):
        if parts == 0:
            rows = slice(ROWS + ti * TILE, ROWS + (ti + 1) * TILE)
            remote = jnp.concatenate([peer[rows, :] for peer in (p0, p1, p2)], axis=0)
        elif ti == 0:
            remote = lax.select(even, mine, other)
        else:
            remote = lax.select(even, other, mine)
        rhs = jnp.concatenate([own_ref[ti * TILE : (ti + 1) * TILE, :], remote], axis=0)
        total = jnp.dot(lhs, rhs, preferred_element_type=F32)
        if has_in:
            total = total + c_ref[...].astype(F32)
        out[...] = total.astype(out.dtype)


def project(which, own, features, first_got, mine, other, carried, after=(), out_dtype=BF16):
    half = (ROWS, WIDTH)
    n, parts = len(which), len(mine)
    return call(
        functools.partial(project_kernel, which, bool(carried), parts),
        (own, features, *first_got, *mine, *other, *carried),
        [whole(half)] * 2
        + [whole(first_got[0].shape)] * 3
        + [whole(value.shape) for value in (*mine, *other)]
        + [whole(half)] * len(carried),
        [shape((ROWS, TILE), out_dtype)] * n,
        [whole((ROWS, TILE))] * n,
        [],
        (2 * ROWS * 1024 * TILE * n, 2 << 20),
        8,
        after,
    )


def window_start(ids, owner):
    before = jnp.sum((ids < owner * VARS).astype(jnp.int32))
    return jnp.minimum(before, ROWS - WINDOW)


def dispatch_kernel(ids_ref, x_ref, *outs):
    me = lax.axis_index("pool")
    ids = ids_ref[...]
    features = x_ref[...]
    for k in range(NX):
        owner = lax.rem(me + k, NX)
        start = window_start(ids, owner)
        at = lax.broadcasted_iota(jnp.int32, (WINDOW, ROWS), 0) + start
        hot = (at == lax.broadcasted_iota(jnp.int32, (WINDOW, ROWS), 1)).astype(F32).astype(BF16)
        outs[k][0:WINDOW, :] = jnp.dot(hot, features, preferred_element_type=F32).astype(BF16)
        local = jnp.broadcast_to((ids - owner * VARS).astype(F32), (IDROWS, ROWS)).astype(BF16)
        outs[k][WINDOW : WINDOW + IDROWS, :] = lax.dot_general(
            local, hot, (((1,), (1,)), ((), ())), preferred_element_type=F32
        ).astype(BF16)


def dispatch(ids, features, after=()):
    return call(
        dispatch_kernel,
        (ids, features),
        [whole((1, ROWS)), whole((ROWS, WIDTH))],
        [shape((WINDOW + IDROWS, WIDTH))] * NX,
        [whole((WINDOW + IDROWS, WIDTH))] * NX,
        [],
        (2 * 1024 * 512 * 256, 1 << 20),
        6,
        after,
    )


def spread_columns(row, lanes):
    diagonal = lax.broadcasted_iota(jnp.int32, (WINDOW, WINDOW), 0) == lax.broadcasted_iota(
        jnp.int32, (WINDOW, WINDOW), 1
    )
    row = jnp.broadcast_to(row.astype(F32), (WINDOW, WINDOW))
    spread = jnp.where(diagonal, row, 0.0).astype(BF16)
    return jnp.dot(spread, jnp.ones((WINDOW, lanes), BF16), preferred_element_type=F32)


def variant_columns(item_ref, lanes):
    return spread_columns(item_ref[WINDOW : WINDOW + 1, :], lanes)


def down_kernel(i0, i1, i2, i3, down_ref, out_ref, item_ref, fold_ref):
    for k, item in enumerate((i0, i1, i2, i3)):
        item_ref[k] = item[...]
    lane = lax.broadcasted_iota(jnp.int32, (1, 256), 1)
    part = lax.div(lane, jnp.int32(RANK)).astype(F32)

    def window(k, carry):
        item = item_ref.at[k]
        variant = variant_columns(item, 256)
        features = item[0:WINDOW, :]
        total = None
        for j in range(VARS * RANK // 256):
            value = lax.dot_general(
                features,
                down_ref[j * 256 : (j + 1) * 256, :],
                (((1,), (1,)), ((), ())),
                preferred_element_type=F32,
            )
            value = jnp.where(variant == part + float(j * 4), value, 0.0)
            total = value if total is None else total + value
        two = total[:, 0:128] + total[:, 128:256]
        fold_ref[k] = two + pltpu.roll(two, RANK, 1)
        return carry

    lax.fori_loop(0, NX, window, 0)
    low = lax.broadcasted_iota(jnp.int32, (WINDOW, 128), 1) < RANK
    for h in range(2):
        packed = jnp.where(low, fold_ref[h], fold_ref[h + 2]).astype(BF16)
        out_ref[:, h * 128 : (h + 1) * 128] = packed


def down(items, factor, after=()):
    return call(
        down_kernel,
        (*items, factor),
        [whole((WINDOW + IDROWS, WIDTH))] * NX + [whole((VARS * RANK, WIDTH))],
        shape((WINDOW, 256)),
        whole((WINDOW, 256)),
        [pltpu.VMEM((NX, WINDOW + IDROWS, WIDTH), BF16), pltpu.VMEM((NX, WINDOW, 128), F32)],
        (2 * 1024 * 256 * 2048, 2 << 20),
        8,
        after,
    )


def block_kernel(i0, i1, i2, i3, mats_ref, place_ref, out_ref, item_ref, rhs_ref):
    for k, item in enumerate((i0, i1, i2, i3)):
        item_ref[k] = item[...]
    shard = lax.axis_index(Z) * NY + lax.axis_index(Y)
    for v in range(VARS):
        first = (v // 2) * BLK
        lanes = slice((v % 2) * BLK, (v % 2 + 1) * BLK)
        rhs_ref[first : first + BLK, lanes] = mats_ref[v]

    rows, kept = [], []
    for k in range(NX):
        item = item_ref.at[k]
        ids = item[WINDOW : WINDOW + 1, :].astype(F32)
        code = jnp.full(ids.shape, 64.0, F32)
        for v in range(VARS):
            place = (place_ref[v] - shard * 2).astype(F32)
            code = jnp.where(ids == float(v), v // 2 + 16.0 * (v % 2) + 32.0 * place, code)
        code = spread_columns(code, 128)
        upper = (code >= 32.0) & (code < 64.0)
        rest = jnp.where(upper, code - 32.0, code)
        odd = rest >= 16.0
        pair = jnp.where(odd, rest - 16.0, rest).astype(BF16)
        low = item[0:WINDOW, 0:BLK].astype(F32)
        high = item[0:WINDOW, BLK : 2 * BLK].astype(F32)
        picked = jnp.where(upper, high, low).astype(BF16)
        zero = jnp.zeros_like(picked)
        pieces = [jnp.where(pair == jnp.bfloat16(p), picked, zero) for p in range(VARS // 2)]
        rows.append(jnp.concatenate(pieces, axis=1))
        kept.append((upper, odd))
    lhs = jnp.concatenate(rows, axis=0)
    every = jnp.dot(lhs, rhs_ref[...], preferred_element_type=F32)
    for k, (upper, odd) in enumerate(kept):
        both = every[k * WINDOW : (k + 1) * WINDOW, :]
        one = jnp.where(odd, both[:, BLK:], both[:, 0:BLK])
        out_ref[k, :, 0:BLK] = jnp.where(upper, 0.0, one)
        out_ref[k, :, BLK : 2 * BLK] = jnp.where(upper, one, 0.0)


def block_terms(items, mats, places, after=()):
    return call(
        block_kernel,
        (*items, mats, places),
        [whole((WINDOW + IDROWS, WIDTH))] * NX + [whole((VARS, BLK, BLK)), SMEM],
        shape((NX, WINDOW, 256), F32),
        whole((NX, WINDOW, 256)),
        [pltpu.VMEM((NX, WINDOW + IDROWS, WIDTH), BF16), pltpu.VMEM((VARS * BLK // 2, 256), BF16)],
        (2 * 1024 * 2048 * 256, 3 << 20),
        10,
        after,
    )


def add_kernel(a_ref, b_ref, out_ref):
    out_ref[...] = (a_ref[...].astype(F32) + b_ref[...].astype(F32)).astype(BF16)


def exchanged_sum(value, axis, partner, after=()):
    other = lax.ppermute(value, axis, list(enumerate(partner)))
    return call(
        add_kernel,
        (value, other),
        [whole((WINDOW, 256))] * 2,
        shape((WINDOW, 256)),
        whole((WINDOW, 256)),
        [],
        (1 << 16, 3 << 17),
        2,
        after,
    )


def up_kernel(i0, i1, i2, i3, l0, l1, l2, l3, up_ref, block_ref, *refs):
    outs, (item_ref, two_ref, out_ref) = refs[:NX], refs[NX:]
    low = l0[...].astype(F32) + l1[...].astype(F32) + l2[...].astype(F32) + l3[...].astype(F32)
    low = low.astype(BF16).astype(F32)
    for k, item in enumerate((i0, i1, i2, i3)):
        item_ref[k] = item[WINDOW : WINDOW + IDROWS, :]
    first = lax.broadcasted_iota(jnp.int32, (WINDOW, 128), 1) < RANK
    for h in range(2):
        packed = low[:, h * 128 : (h + 1) * 128]
        turned = pltpu.roll(packed, RANK, 1)
        two_ref[h] = jnp.where(first, packed, turned)
        two_ref[h + 2] = jnp.where(first, turned, packed)
    half = lax.div(lax.broadcasted_iota(jnp.int32, (1, 128), 1), jnp.int32(RANK)).astype(F32)

    rows = []
    for k in range(NX):
        variant = (spread_columns(item_ref[k, 0:1, :], 128) - half).astype(BF16)
        two = two_ref[k].astype(BF16)
        zero = jnp.zeros_like(two)
        pieces = []
        for i in range(VARS // 2):
            pieces.append(jnp.where(variant == jnp.bfloat16(2 * i), two, zero))
        rows.append(jnp.concatenate(pieces, axis=1))
    lhs = jnp.concatenate(rows, axis=0)
    total = jnp.dot(lhs, up_ref[...], preferred_element_type=F32)
    for k in range(NX):
        outs[k][...] = (block_ref[k] + total[k * WINDOW : (k + 1) * WINDOW, :]).astype(BF16)


def up(items, lows, factor, blocks, after=()):
    return call(
        up_kernel,
        (*items, *lows, factor, blocks),
        [whole((WINDOW + IDROWS, WIDTH))] * NX
        + [whole((WINDOW, 256))] * 4
        + [whole((VARS * RANK, WIDTH)), whole((NX, WINDOW, 256))],
        [shape((WINDOW, WIDTH))] * NX,
        [whole((WINDOW, WIDTH))] * NX,
        [
            pltpu.VMEM((NX, IDROWS, WIDTH), BF16),
            pltpu.VMEM((NX, WINDOW, 128), F32),
            pltpu.VMEM((NX, WINDOW, WIDTH), BF16),
        ],
        (2 * 1024 * 256 * 2048, 3 << 20),
        10,
        after,
    )


def combine_kernel(ids_ref, h_ref, own_ref, plus_ref, r0, r1, r2, r3, first_ref, branch_ref):
    me = lax.axis_index("pool")
    ids = ids_ref[...]
    branch = own_ref[...] + plus_ref[...].astype(F32)
    delta = None
    for k, back in enumerate((r0, r1, r2, r3)):
        start = window_start(ids, lax.rem(me + k, NX))
        at = lax.broadcasted_iota(jnp.int32, (ROWS, WINDOW), 1) + start
        hot = (at == lax.broadcasted_iota(jnp.int32, (ROWS, WINDOW), 0)).astype(F32).astype(BF16)
        part = jnp.dot(hot, back[...], preferred_element_type=F32)
        delta = part if delta is None else delta + part
    branch = branch + delta
    branch_ref[...] = branch
    first_ref[...] = (h_ref[...].astype(F32) + branch).astype(BF16)


def combine(ids, hidden, own, plus, returned, after=()):
    half = (ROWS, WIDTH)
    return call(
        combine_kernel,
        (ids, hidden, own, plus, *returned),
        [whole((1, ROWS))] + [whole(half)] * 3 + [whole((WINDOW, WIDTH))] * NX,
        [shape(half), shape(half, F32)],
        [whole(half)] * 2,
        [],
        (2 * 512 * 1024 * 256, 2 << 20),
        8,
        after,
    )


def steps(
    hidden_input,
    attention_output,
    projection_weight,
    lowrank_down_factor,
    lowrank_up_factor,
    residual_block_mats,
    diagonal_block_index,
    row_variant_index,
):
    features = attention_output[0]
    weight = projection_weight[0]
    down_factor = lowrank_down_factor[0].reshape(VARS * RANK, WIDTH)
    up_factor = lowrank_up_factor[0].reshape(VARS * RANK, WIDTH)
    mats = residual_block_mats[0][:, 0]
    places = diagonal_block_index[0][:, 0]
    ids = row_variant_index.reshape(1, ROWS)

    first, (own0,) = pack((0,), weight, features)
    got = [shift(value, Y, hop) for value, hop in zip(first, HOPS)]
    sent = dispatch(ids, features, (first[0],))
    items = [sent[0]] + [shift(sent[k], "pool", k) for k in (1, 2, 3)]
    second, (own1,) = pack((1,), weight, None, (sent[0],))
    got1 = [shift(value, Y, hop) for value, hop in zip(second, HOPS)]
    low = down(items, down_factor, (second[0],))
    third, (own2, own3) = pack((2, 3), weight, None, (low,))
    got2 = [shift(value, Y, hop) for value, hop in zip(third, HOPS)]
    low1 = exchanged_sum(low, Z, (1, 0, 3, 2, 5, 4, 7, 6))
    low2 = exchanged_sum(low1, Z, (2, 3, 0, 1, 6, 7, 4, 5))
    plus, minus = project((0, 1), own0, features, got, (), (), (), (low1,))
    carried = (shift(plus, Z, 1), shift(minus, Z, -1))
    mine1 = join(got1, 0, (True,), (plus,))
    other1 = (shift(mine1[0], "pool", 1), shift(mine1[1], "pool", -1))
    low3 = exchanged_sum(low2, Z, (6, 7, 4, 5, 2, 3, 0, 1))
    plus, minus = project((0, 1), own1, features, got, mine1, other1, carried)
    mine2, mine3 = join(got2, 0, (False, False), (plus,))
    other2 = swapped(mine2, False)
    carried = (shift(plus, Z, 1), shift(minus, Z, -1))
    other3 = swapped(mine3, True)
    lows = [low3] + [shift(low3, Y, hop) for hop in HOPS]
    blocks = block_terms(items, mats, places, (plus,))
    plus, minus = project((0, 1), own2, features, got, (mine2,), (other2,), carried, (blocks,))
    carried = (shift(plus, Z, 1), shift(minus, Z, -1))
    served = up(items, lows, up_factor, blocks, (plus,))
    returned = [served[0]] + [shift(served[k], "pool", -k) for k in (1, 2, 3)]
    (plus,) = project(
        (0,), own3, features, got, (mine3,), (other3,), carried[:1], (served[1],)
    )
    arrived = shift(plus, Z, 1)
    (own,) = project(
        (1,), own3, features, got, (mine3,), (other3,), carried[1:], (plus,), F32
    )
    plus = arrived

    first_out, branch = combine(ids, hidden_input, own, plus, returned)
    carried = lax.ppermute(first_out, "section", [(0, 1)])
    begin = jnp.where(lax.axis_index("section") == 0, hidden_input, carried)
    return (begin.astype(F32) + branch).astype(BF16)[None]


def solution(mesh):
    finer = Mesh(
        mesh.devices.reshape(mesh.shape["pool"], mesh.shape["section"], NZ, NY),
        ("pool", "section", Z, Y),
    )
    placed = (
        P("pool", TENSOR),
        P("section", "pool", TENSOR),
        P("section", TENSOR, None),
        P("section", "pool", None, TENSOR),
        P("section", "pool", None, TENSOR),
        P("section", "pool", TENSOR, None, None),
        P("section", "pool", TENSOR),
        P("pool"),
    )
    return jax.shard_map(
        steps,
        mesh=finer,
        in_specs=placed,
        out_specs=P("section", "pool", TENSOR),
        check_vma=False,
    )
```

```python
import functools

import jax
import jax.numpy as jnp
from jax import lax
from jax.experimental import pallas as pl
from jax.experimental.pallas import tpu as pltpu
from jax.sharding import Mesh
from jax.sharding import PartitionSpec as P


Z, Y = "tensor_0", "tensor_1"
TENSOR = (Z, Y)
NZ, NY, NX = 8, 4, 4
ROWS, WIDTH, TILE = 512, 256, 256
WINDOW = 256
IDROWS = 16
VARS, RANK, BLK = 32, 64, 128
HOPS = (1, 3, 2)
F32, BF16 = jnp.float32, jnp.bfloat16
ANY = pl.BlockSpec(memory_space=pl.ANY)
HBM = pl.BlockSpec(memory_space=pltpu.HBM)
SMEM = pl.BlockSpec(memory_space=pltpu.SMEM)


def shift(value, axis, steps):
    count = lax.axis_size(axis)
    return lax.ppermute(value, axis, [(i, (i + steps) % count) for i in range(count)])


def cost(flops, nbytes):
    return pl.CostEstimate(flops=flops, bytes_accessed=nbytes, transcendentals=0)


def shape(dims, dtype=BF16):
    return pltpu.VMEM(dims, dtype)


def whole(dims, at=None):
    at = at or (0,) * len(dims)
    return pl.BlockSpec(dims, lambda: at)


def tiles_of(group):
    z = lax.axis_index(Z)
    return lax.rem(z + (4 - group), NZ), lax.rem(z + (group + NZ - 3), NZ)


def column(ztile, ytile):
    return pl.multiple_of((ztile * NY + ytile) * TILE, TILE)


def placed(value, spec):
    space = pltpu.HBM if spec is HBM else pltpu.VMEM
    if spec is SMEM:
        return value
    return pltpu.with_memory_space_constraint(value, space)


def call(kernel, args, in_specs, outs, out_specs, scratch, work, limit, after=()):
    n, m = len(args), len(after)
    args = [placed(arg, spec) for arg, spec in zip(args, in_specs)]

    def body(*refs):
        kernel(*refs[:n], *refs[n + m :])

    return pl.pallas_call(
        body,
        out_shape=outs,
        in_specs=list(in_specs) + [ANY] * m,
        out_specs=out_specs,
        scratch_shapes=scratch,
        cost_estimate=cost(*work),
        compiler_params=pltpu.CompilerParams(vmem_limit_bytes=limit << 20),
    )(*args, *after)


def parity():
    return lax.rem(lax.axis_index("pool"), 2)


def pack_body(sets, ahead, *refs):
    w_ref, sems = refs[0], refs[-1]
    groups = [group for members in sets for group in members]
    rest = refs[2:] if ahead else refs[1:]
    outs, owns = rest[: 3 * len(sets)], rest[3 * len(sets) : 3 * len(sets) + len(groups)]
    y, odd = lax.axis_index(Y), parity()
    copies = []
    for si, members in enumerate(sets):
        for gi, group in enumerate(members):
            plus, minus = tiles_of(group)
            wanted = (plus, minus) if ahead else (plus * (1 - odd) + minus * odd,)
            for ki, hop in enumerate(HOPS):
                out = outs[3 * si + ki]
                if ahead:
                    copies.append((refs[1], out.at[pl.ds(0, ROWS), :]))
                for ti, ztile in enumerate(wanted):
                    source = w_ref.at[:, pl.ds(column(ztile, lax.rem(y + hop, NY)), TILE)]
                    copies.append((source, out.at[pl.ds(ahead + (gi + ti) * TILE, TILE), :]))
    for own, group in zip(owns, groups):
        for ti, ztile in enumerate(tiles_of(group)):
            source = w_ref.at[:, pl.ds(column(ztile, y), TILE)]
            copies.append((source, own.at[pl.ds(ti * TILE, TILE), :]))
    copies = [
        pltpu.make_async_copy(source, target, sems.at[i])
        for i, (source, target) in enumerate(copies)
    ]
    for copy in copies:
        copy.start()
    for copy in copies:
        copy.wait()


def pack(sets, weight, features=None, after=()):
    args, specs = [weight], [HBM]
    ahead, count = 0, sum(len(members) for members in sets)
    dims = []
    if features is not None:
        ahead = ROWS
        args.append(features)
        specs.append(HBM)
    for members in sets:
        dims += [(ROWS + 2 * TILE if ahead else len(members) * TILE, TILE)] * 3
    dims += [(2 * TILE, TILE)] * count
    got = call(
        functools.partial(pack_body, sets, ahead),
        args,
        specs,
        [shape(d) for d in dims],
        [whole(d) for d in dims],
        [pltpu.SemaphoreType.DMA((11 if ahead else 5 * count,))],
        (0, 20 * count * TILE * TILE),
        8,
        after,
    )
    return [got[3 * i : 3 * i + 3] for i in range(len(sets))], got[3 * len(sets) :]


def join_kernel(base, halves, a_ref, b_ref, c_ref, *outs):
    pos = 0
    for gi, split in enumerate(halves):
        for ki, ref in enumerate((a_ref, b_ref, c_ref)):
            first = base + gi * TILE
            if split:
                for side in range(2):
                    rows = slice(first + side * BLK, first + (side + 1) * BLK)
                    outs[pos + side][ki * BLK : (ki + 1) * BLK, :] = ref[rows, :]
            else:
                outs[pos][ki * TILE : (ki + 1) * TILE, :] = ref[first : first + TILE, :]
        pos += 2 if split else 1


def join(got, base, halves, after=()):
    dims = []
    for split in halves:
        dims += [(3 * BLK, TILE)] * 2 if split else [(3 * TILE, TILE)]
    return call(
        functools.partial(join_kernel, base, halves),
        tuple(got),
        [whole(got[0].shape)] * 3,
        [shape(d) for d in dims],
        [whole(d) for d in dims],
        [],
        (0, 3 << 20),
        4,
        after,
    )


def swapped(value, second_pairing):
    if second_pairing:
        pairs = [(0, 3), (3, 0), (1, 2), (2, 1)]
    else:
        pairs = [(0, 1), (1, 0), (2, 3), (3, 2)]
    return lax.ppermute(value, "pool", pairs)


def stacked(refs):
    if len(refs) == 1:
        return refs[0][...]
    low, high = refs
    pieces = []
    for ki in range(3):
        rows = slice(ki * BLK, (ki + 1) * BLK)
        pieces += [low[rows, :], high[rows, :]]
    return jnp.concatenate(pieces, axis=0)


def project_kernel(which, has_in, parts, own_ref, x_ref, p0, p1, p2, *refs):
    n = len(which)
    even = parity() == 0
    if parts:
        mine, other = stacked(refs[:parts]), stacked(refs[parts : 2 * parts])
    refs = refs[2 * parts :]
    carried, outs = (refs[:n], refs[n:]) if has_in else ((None,) * n, refs)
    lhs = jnp.concatenate([x_ref[...]] + [peer[0:ROWS, :] for peer in (p0, p1, p2)], axis=1)
    for c_ref, out, ti in zip(carried, outs, which):
        if parts == 0:
            rows = slice(ROWS + ti * TILE, ROWS + (ti + 1) * TILE)
            remote = jnp.concatenate([peer[rows, :] for peer in (p0, p1, p2)], axis=0)
        elif ti == 0:
            remote = lax.select(even, mine, other)
        else:
            remote = lax.select(even, other, mine)
        rhs = jnp.concatenate([own_ref[ti * TILE : (ti + 1) * TILE, :], remote], axis=0)
        total = jnp.dot(lhs, rhs, preferred_element_type=F32)
        if has_in:
            total = total + c_ref[...].astype(F32)
        out[...] = total.astype(out.dtype)


def project(which, own, features, first_got, mine, other, carried, after=(), out_dtype=BF16):
    half = (ROWS, WIDTH)
    n, parts = len(which), len(mine)
    return call(
        functools.partial(project_kernel, which, bool(carried), parts),
        (own, features, *first_got, *mine, *other, *carried),
        [whole(half)] * 2
        + [whole(first_got[0].shape)] * 3
        + [whole(value.shape) for value in (*mine, *other)]
        + [whole(half)] * len(carried),
        [shape((ROWS, TILE), out_dtype)] * n,
        [whole((ROWS, TILE))] * n,
        [],
        (2 * ROWS * 1024 * TILE * n, 2 << 20),
        8,
        after,
    )


def window_start(ids, owner):
    before = jnp.sum((ids < owner * VARS).astype(jnp.int32))
    return jnp.minimum(before, ROWS - WINDOW)


def dispatch_kernel(ids_ref, x_ref, *outs):
    me = lax.axis_index("pool")
    ids = ids_ref[...]
    features = x_ref[...]
    for k in range(NX):
        owner = lax.rem(me + k, NX)
        start = window_start(ids, owner)
        at = lax.broadcasted_iota(jnp.int32, (WINDOW, ROWS), 0) + start
        hot = (at == lax.broadcasted_iota(jnp.int32, (WINDOW, ROWS), 1)).astype(F32).astype(BF16)
        outs[k][0:WINDOW, :] = jnp.dot(hot, features, preferred_element_type=F32).astype(BF16)
        local = jnp.broadcast_to((ids - owner * VARS).astype(F32), (IDROWS, ROWS)).astype(BF16)
        outs[k][WINDOW : WINDOW + IDROWS, :] = lax.dot_general(
            local, hot, (((1,), (1,)), ((), ())), preferred_element_type=F32
        ).astype(BF16)


def dispatch(ids, features, after=()):
    return call(
        dispatch_kernel,
        (ids, features),
        [whole((1, ROWS)), whole((ROWS, WIDTH))],
        [shape((WINDOW + IDROWS, WIDTH))] * NX,
        [whole((WINDOW + IDROWS, WIDTH))] * NX,
        [],
        (2 * 1024 * 512 * 256, 1 << 20),
        6,
        after,
    )


def spread_columns(row, lanes):
    diagonal = lax.broadcasted_iota(jnp.int32, (WINDOW, WINDOW), 0) == lax.broadcasted_iota(
        jnp.int32, (WINDOW, WINDOW), 1
    )
    row = jnp.broadcast_to(row.astype(F32), (WINDOW, WINDOW))
    spread = jnp.where(diagonal, row, 0.0).astype(BF16)
    return jnp.dot(spread, jnp.ones((WINDOW, lanes), BF16), preferred_element_type=F32)


def variant_columns(item_ref, lanes):
    return spread_columns(item_ref[WINDOW : WINDOW + 1, :], lanes)


def down_kernel(i0, i1, i2, i3, down_ref, out_ref, item_ref, fold_ref):
    for k, item in enumerate((i0, i1, i2, i3)):
        item_ref[k] = item[...]
    lane = lax.broadcasted_iota(jnp.int32, (1, 256), 1)
    part = lax.div(lane, jnp.int32(RANK)).astype(F32)

    def window(k, carry):
        item = item_ref.at[k]
        variant = variant_columns(item, 256)
        features = item[0:WINDOW, :]
        total = None
        for j in range(VARS * RANK // 256):
            value = lax.dot_general(
                features,
                down_ref[j * 256 : (j + 1) * 256, :],
                (((1,), (1,)), ((), ())),
                preferred_element_type=F32,
            )
            value = jnp.where(variant == part + float(j * 4), value, 0.0)
            total = value if total is None else total + value
        two = total[:, 0:128] + total[:, 128:256]
        fold_ref[k] = two + pltpu.roll(two, RANK, 1)
        return carry

    lax.fori_loop(0, NX, window, 0)
    low = lax.broadcasted_iota(jnp.int32, (WINDOW, 128), 1) < RANK
    for h in range(2):
        packed = jnp.where(low, fold_ref[h], fold_ref[h + 2]).astype(BF16)
        out_ref[:, h * 128 : (h + 1) * 128] = packed


def down(items, factor, after=()):
    return call(
        down_kernel,
        (*items, factor),
        [whole((WINDOW + IDROWS, WIDTH))] * NX + [whole((VARS * RANK, WIDTH))],
        shape((WINDOW, 256)),
        whole((WINDOW, 256)),
        [pltpu.VMEM((NX, WINDOW + IDROWS, WIDTH), BF16), pltpu.VMEM((NX, WINDOW, 128), F32)],
        (2 * 1024 * 256 * 2048, 2 << 20),
        8,
        after,
    )


def block_kernel(i0, i1, i2, i3, mats_ref, place_ref, out_ref, item_ref, rhs_ref):
    for k, item in enumerate((i0, i1, i2, i3)):
        item_ref[k] = item[...]
    shard = lax.axis_index(Z) * NY + lax.axis_index(Y)
    for v in range(VARS):
        first = (v // 2) * BLK
        lanes = slice((v % 2) * BLK, (v % 2 + 1) * BLK)
        rhs_ref[first : first + BLK, lanes] = mats_ref[v]

    rows, kept = [], []
    for k in range(NX):
        item = item_ref.at[k]
        ids = item[WINDOW : WINDOW + 1, :].astype(F32)
        code = jnp.full(ids.shape, 64.0, F32)
        for v in range(VARS):
            place = (place_ref[v] - shard * 2).astype(F32)
            code = jnp.where(ids == float(v), v // 2 + 16.0 * (v % 2) + 32.0 * place, code)
        code = spread_columns(code, 128)
        upper = (code >= 32.0) & (code < 64.0)
        rest = jnp.where(upper, code - 32.0, code)
        odd = rest >= 16.0
        pair = jnp.where(odd, rest - 16.0, rest).astype(BF16)
        low = item[0:WINDOW, 0:BLK].astype(F32)
        high = item[0:WINDOW, BLK : 2 * BLK].astype(F32)
        picked = jnp.where(upper, high, low).astype(BF16)
        zero = jnp.zeros_like(picked)
        pieces = [jnp.where(pair == jnp.bfloat16(p), picked, zero) for p in range(VARS // 2)]
        rows.append(jnp.concatenate(pieces, axis=1))
        kept.append((upper, odd))
    lhs = jnp.concatenate(rows, axis=0)
    every = jnp.dot(lhs, rhs_ref[...], preferred_element_type=F32)
    for k, (upper, odd) in enumerate(kept):
        both = every[k * WINDOW : (k + 1) * WINDOW, :]
        one = jnp.where(odd, both[:, BLK:], both[:, 0:BLK])
        out_ref[k, :, 0:BLK] = jnp.where(upper, 0.0, one)
        out_ref[k, :, BLK : 2 * BLK] = jnp.where(upper, one, 0.0)


def block_terms(items, mats, places, after=()):
    return call(
        block_kernel,
        (*items, mats, places),
        [whole((WINDOW + IDROWS, WIDTH))] * NX + [whole((VARS, BLK, BLK)), SMEM],
        shape((NX, WINDOW, 256), F32),
        whole((NX, WINDOW, 256)),
        [pltpu.VMEM((NX, WINDOW + IDROWS, WIDTH), BF16), pltpu.VMEM((VARS * BLK // 2, 256), BF16)],
        (2 * 1024 * 2048 * 256, 3 << 20),
        10,
        after,
    )


def add_kernel(a_ref, b_ref, out_ref):
    out_ref[...] = (a_ref[...].astype(F32) + b_ref[...].astype(F32)).astype(BF16)


def exchanged_sum(value, axis, partner, after=()):
    other = lax.ppermute(value, axis, list(enumerate(partner)))
    return call(
        add_kernel,
        (value, other),
        [whole((WINDOW, 256))] * 2,
        shape((WINDOW, 256)),
        whole((WINDOW, 256)),
        [],
        (1 << 16, 3 << 17),
        2,
        after,
    )


def up_kernel(i0, i1, i2, i3, l0, l1, l2, l3, up_ref, block_ref, *refs):
    outs, (item_ref, two_ref, out_ref) = refs[:NX], refs[NX:]
    low = l0[...].astype(F32) + l1[...].astype(F32) + l2[...].astype(F32) + l3[...].astype(F32)
    low = low.astype(BF16).astype(F32)
    for k, item in enumerate((i0, i1, i2, i3)):
        item_ref[k] = item[WINDOW : WINDOW + IDROWS, :]
    first = lax.broadcasted_iota(jnp.int32, (WINDOW, 128), 1) < RANK
    for h in range(2):
        packed = low[:, h * 128 : (h + 1) * 128]
        turned = pltpu.roll(packed, RANK, 1)
        two_ref[h] = jnp.where(first, packed, turned)
        two_ref[h + 2] = jnp.where(first, turned, packed)
    half = lax.div(lax.broadcasted_iota(jnp.int32, (1, 128), 1), jnp.int32(RANK)).astype(F32)

    rows = []
    for k in range(NX):
        variant = (spread_columns(item_ref[k, 0:1, :], 128) - half).astype(BF16)
        two = two_ref[k].astype(BF16)
        zero = jnp.zeros_like(two)
        pieces = []
        for i in range(VARS // 2):
            pieces.append(jnp.where(variant == jnp.bfloat16(2 * i), two, zero))
        rows.append(jnp.concatenate(pieces, axis=1))
    lhs = jnp.concatenate(rows, axis=0)
    total = jnp.dot(lhs, up_ref[...], preferred_element_type=F32)
    for k in range(NX):
        outs[k][...] = (block_ref[k] + total[k * WINDOW : (k + 1) * WINDOW, :]).astype(BF16)


def up(items, lows, factor, blocks, after=()):
    return call(
        up_kernel,
        (*items, *lows, factor, blocks),
        [whole((WINDOW + IDROWS, WIDTH))] * NX
        + [whole((WINDOW, 256))] * 4
        + [whole((VARS * RANK, WIDTH)), whole((NX, WINDOW, 256))],
        [shape((WINDOW, WIDTH))] * NX,
        [whole((WINDOW, WIDTH))] * NX,
        [
            pltpu.VMEM((NX, IDROWS, WIDTH), BF16),
            pltpu.VMEM((NX, WINDOW, 128), F32),
            pltpu.VMEM((NX, WINDOW, WIDTH), BF16),
        ],
        (2 * 1024 * 256 * 2048, 3 << 20),
        10,
        after,
    )


def combine_kernel(ids_ref, h_ref, own_ref, plus_ref, r0, r1, r2, r3, first_ref, branch_ref):
    me = lax.axis_index("pool")
    ids = ids_ref[...]
    branch = own_ref[...] + plus_ref[...].astype(F32)
    delta = None
    for k, back in enumerate((r0, r1, r2, r3)):
        start = window_start(ids, lax.rem(me + k, NX))
        at = lax.broadcasted_iota(jnp.int32, (ROWS, WINDOW), 1) + start
        hot = (at == lax.broadcasted_iota(jnp.int32, (ROWS, WINDOW), 0)).astype(F32).astype(BF16)
        part = jnp.dot(hot, back[...], preferred_element_type=F32)
        delta = part if delta is None else delta + part
    branch = branch + delta
    branch_ref[...] = branch
    first_ref[...] = (h_ref[...].astype(F32) + branch).astype(BF16)


def combine(ids, hidden, own, plus, returned, after=()):
    half = (ROWS, WIDTH)
    return call(
        combine_kernel,
        (ids, hidden, own, plus, *returned),
        [whole((1, ROWS))] + [whole(half)] * 3 + [whole((WINDOW, WIDTH))] * NX,
        [shape(half), shape(half, F32)],
        [whole(half)] * 2,
        [],
        (2 * 512 * 1024 * 256, 2 << 20),
        8,
        after,
    )


def steps(
    hidden_input,
    attention_output,
    projection_weight,
    lowrank_down_factor,
    lowrank_up_factor,
    residual_block_mats,
    diagonal_block_index,
    row_variant_index,
):
    features = attention_output[0]
    weight = projection_weight[0]
    down_factor = lowrank_down_factor[0].reshape(VARS * RANK, WIDTH)
    up_factor = lowrank_up_factor[0].reshape(VARS * RANK, WIDTH)
    mats = residual_block_mats[0][:, 0]
    places = diagonal_block_index[0][:, 0]
    ids = row_variant_index.reshape(1, ROWS)

    (first,), (own0,) = pack(((0,),), weight, features)
    got = [shift(value, Y, hop) for value, hop in zip(first, HOPS)]
    sent = dispatch(ids, features, (first[0],))
    items = [sent[0]] + [shift(sent[k], "pool", k) for k in (1, 2, 3)]
    (second, third), (own1, own2, own3) = pack(((1,), (2, 3)), weight, None, (sent[0],))
    got1 = [shift(value, Y, hop) for value, hop in zip(second, HOPS)]
    low = down(items, down_factor, (second[0],))
    got2 = [shift(value, Y, hop) for value, hop in zip(third, HOPS)]
    low1 = exchanged_sum(low, Z, (1, 0, 3, 2, 5, 4, 7, 6))
    low2 = exchanged_sum(low1, Z, (2, 3, 0, 1, 6, 7, 4, 5))
    plus, minus = project((0, 1), own0, features, got, (), (), (), (low1,))
    carried = (shift(plus, Z, 1), shift(minus, Z, -1))
    mine1 = join(got1, 0, (True,), (plus,))
    other1 = (shift(mine1[0], "pool", 1), shift(mine1[1], "pool", -1))
    low3 = exchanged_sum(low2, Z, (6, 7, 4, 5, 2, 3, 0, 1))
    plus, minus = project((0, 1), own1, features, got, mine1, other1, carried)
    mine2, mine3 = join(got2, 0, (False, False), (plus,))
    other2 = swapped(mine2, False)
    carried = (shift(plus, Z, 1), shift(minus, Z, -1))
    other3 = swapped(mine3, True)
    lows = [low3] + [shift(low3, Y, hop) for hop in HOPS]
    blocks = block_terms(items, mats, places, (plus,))
    plus, minus = project((0, 1), own2, features, got, (mine2,), (other2,), carried, (blocks,))
    carried = (shift(plus, Z, 1), shift(minus, Z, -1))
    served = up(items, lows, up_factor, blocks, (plus,))
    returned = [served[0]] + [shift(served[k], "pool", -k) for k in (1, 2, 3)]
    (plus,) = project(
        (0,), own3, features, got, (mine3,), (other3,), carried[:1], (served[1],)
    )
    arrived = shift(plus, Z, 1)
    (own,) = project(
        (1,), own3, features, got, (mine3,), (other3,), carried[1:], (plus,), F32
    )
    plus = arrived

    first_out, branch = combine(ids, hidden_input, own, plus, returned)
    carried = lax.ppermute(first_out, "section", [(0, 1)])
    begin = jnp.where(lax.axis_index("section") == 0, hidden_input, carried)
    return (begin.astype(F32) + branch).astype(BF16)[None]


def solution(mesh):
    finer = Mesh(
        mesh.devices.reshape(mesh.shape["pool"], mesh.shape["section"], NZ, NY),
        ("pool", "section", Z, Y),
    )
    placed = (
        P("pool", TENSOR),
        P("section", "pool", TENSOR),
        P("section", TENSOR, None),
        P("section", "pool", None, TENSOR),
        P("section", "pool", None, TENSOR),
        P("section", "pool", TENSOR, None, None),
        P("section", "pool", TENSOR),
        P("pool"),
    )
    return jax.shard_map(
        steps,
        mesh=finer,
        in_specs=placed,
        out_specs=P("section", "pool", TENSOR),
        check_vma=False,
    )
```

```python
import functools

import jax
import jax.numpy as jnp
from jax import lax
from jax.experimental import pallas as pl
from jax.experimental.pallas import tpu as pltpu
from jax.sharding import Mesh
from jax.sharding import PartitionSpec as P


Z, Y = "tensor_0", "tensor_1"
TENSOR = (Z, Y)
NZ, NY, NX = 8, 4, 4
ROWS, WIDTH, TILE = 512, 256, 256
WINDOW = 256
IDROWS = 16
VARS, RANK, BLK = 32, 64, 128
HOPS = (1, 3, 2)
F32, BF16 = jnp.float32, jnp.bfloat16
ANY = pl.BlockSpec(memory_space=pl.ANY)
HBM = pl.BlockSpec(memory_space=pltpu.HBM)
SMEM = pl.BlockSpec(memory_space=pltpu.SMEM)


def shift(value, axis, steps):
    count = lax.axis_size(axis)
    return lax.ppermute(value, axis, [(i, (i + steps) % count) for i in range(count)])


def cost(flops, nbytes):
    return pl.CostEstimate(flops=flops, bytes_accessed=nbytes, transcendentals=0)


def shape(dims, dtype=BF16):
    return pltpu.VMEM(dims, dtype)


def whole(dims, at=None):
    at = at or (0,) * len(dims)
    return pl.BlockSpec(dims, lambda: at)


def tiles_of(group):
    z = lax.axis_index(Z)
    return lax.rem(z + (4 - group), NZ), lax.rem(z + (group + NZ - 3), NZ)


def column(ztile, ytile):
    return pl.multiple_of((ztile * NY + ytile) * TILE, TILE)


def placed(value, spec):
    space = pltpu.HBM if spec is HBM else pltpu.VMEM
    if spec is SMEM:
        return value
    return pltpu.with_memory_space_constraint(value, space)


def call(kernel, args, in_specs, outs, out_specs, scratch, work, limit, after=()):
    n, m = len(args), len(after)
    args = [placed(arg, spec) for arg, spec in zip(args, in_specs)]

    def body(*refs):
        kernel(*refs[:n], *refs[n + m :])

    return pl.pallas_call(
        body,
        out_shape=outs,
        in_specs=list(in_specs) + [ANY] * m,
        out_specs=out_specs,
        scratch_shapes=scratch,
        cost_estimate=cost(*work),
        compiler_params=pltpu.CompilerParams(vmem_limit_bytes=limit << 20),
    )(*args, *after)


def parity():
    return lax.rem(lax.axis_index("pool"), 2)


def pack_body(sets, ahead, *refs):
    w_ref, sems = refs[0], refs[-1]
    groups = [group for members in sets for group in members]
    rest = refs[2:] if ahead else refs[1:]
    outs, owns = rest[: 3 * len(sets)], rest[3 * len(sets) : 3 * len(sets) + len(groups)]
    y, odd = lax.axis_index(Y), parity()
    copies = []
    for si, members in enumerate(sets):
        for gi, group in enumerate(members):
            plus, minus = tiles_of(group)
            wanted = (plus, minus) if ahead else (plus * (1 - odd) + minus * odd,)
            for ki, hop in enumerate(HOPS):
                out = outs[3 * si + ki]
                if ahead:
                    copies.append((refs[1], out.at[pl.ds(0, ROWS), :]))
                for ti, ztile in enumerate(wanted):
                    source = w_ref.at[:, pl.ds(column(ztile, lax.rem(y + hop, NY)), TILE)]
                    copies.append((source, out.at[pl.ds(ahead + (gi + ti) * TILE, TILE), :]))
    for own, group in zip(owns, groups):
        for ti, ztile in enumerate(tiles_of(group)):
            source = w_ref.at[:, pl.ds(column(ztile, y), TILE)]
            copies.append((source, own.at[pl.ds(ti * TILE, TILE), :]))
    copies = [
        pltpu.make_async_copy(source, target, sems.at[i])
        for i, (source, target) in enumerate(copies)
    ]
    for copy in copies:
        copy.start()
    for copy in copies:
        copy.wait()


def pack(sets, weight, features=None, after=()):
    args, specs = [weight], [HBM]
    ahead, count = 0, sum(len(members) for members in sets)
    dims = []
    if features is not None:
        ahead = ROWS
        args.append(features)
        specs.append(HBM)
    for members in sets:
        dims += [(ROWS + 2 * TILE if ahead else len(members) * TILE, TILE)] * 3
    dims += [(2 * TILE, TILE)] * count
    got = call(
        functools.partial(pack_body, sets, ahead),
        args,
        specs,
        [shape(d) for d in dims],
        [whole(d) for d in dims],
        [pltpu.SemaphoreType.DMA((11 if ahead else 5 * count,))],
        (0, 20 * count * TILE * TILE),
        8,
        after,
    )
    return [got[3 * i : 3 * i + 3] for i in range(len(sets))], got[3 * len(sets) :]


def join_kernel(base, halves, a_ref, b_ref, c_ref, *outs):
    pos = 0
    for gi, split in enumerate(halves):
        for ki, ref in enumerate((a_ref, b_ref, c_ref)):
            first = base + gi * TILE
            if split:
                for side in range(2):
                    rows = slice(first + side * BLK, first + (side + 1) * BLK)
                    outs[pos + side][ki * BLK : (ki + 1) * BLK, :] = ref[rows, :]
            else:
                outs[pos][ki * TILE : (ki + 1) * TILE, :] = ref[first : first + TILE, :]
        pos += 2 if split else 1


def join(got, base, halves, after=()):
    dims = []
    for split in halves:
        dims += [(3 * BLK, TILE)] * 2 if split else [(3 * TILE, TILE)]
    return call(
        functools.partial(join_kernel, base, halves),
        tuple(got),
        [whole(got[0].shape)] * 3,
        [shape(d) for d in dims],
        [whole(d) for d in dims],
        [],
        (0, 3 << 20),
        4,
        after,
    )


def spread_over_pools(values, sign):
    moved = {0: values[0]}
    for k in HOPS:
        moved[k] = shift(values[k], "pool", sign * k)
    return [moved[k] for k in range(NX)]


def swapped(value, second_pairing):
    if second_pairing:
        pairs = [(0, 3), (3, 0), (1, 2), (2, 1)]
    else:
        pairs = [(0, 1), (1, 0), (2, 3), (3, 2)]
    return lax.ppermute(value, "pool", pairs)


def stacked(refs):
    if len(refs) == 1:
        return refs[0][...]
    low, high = refs
    pieces = []
    for ki in range(3):
        rows = slice(ki * BLK, (ki + 1) * BLK)
        pieces += [low[rows, :], high[rows, :]]
    return jnp.concatenate(pieces, axis=0)


def project_kernel(which, has_in, parts, own_ref, x_ref, p0, p1, p2, *refs):
    n = len(which)
    even = parity() == 0
    if parts:
        mine, other = stacked(refs[:parts]), stacked(refs[parts : 2 * parts])
    refs = refs[2 * parts :]
    carried, outs = (refs[:n], refs[n:]) if has_in else ((None,) * n, refs)
    lhs = jnp.concatenate([x_ref[...]] + [peer[0:ROWS, :] for peer in (p0, p1, p2)], axis=1)
    for c_ref, out, ti in zip(carried, outs, which):
        if parts == 0:
            rows = slice(ROWS + ti * TILE, ROWS + (ti + 1) * TILE)
            remote = jnp.concatenate([peer[rows, :] for peer in (p0, p1, p2)], axis=0)
        elif ti == 0:
            remote = lax.select(even, mine, other)
        else:
            remote = lax.select(even, other, mine)
        rhs = jnp.concatenate([own_ref[ti * TILE : (ti + 1) * TILE, :], remote], axis=0)
        total = jnp.dot(lhs, rhs, preferred_element_type=F32)
        if has_in:
            total = total + c_ref[...].astype(F32)
        out[...] = total.astype(out.dtype)


def project(which, own, features, first_got, mine, other, carried, after=(), out_dtype=BF16):
    half = (ROWS, WIDTH)
    n, parts = len(which), len(mine)
    return call(
        functools.partial(project_kernel, which, bool(carried), parts),
        (own, features, *first_got, *mine, *other, *carried),
        [whole(half)] * 2
        + [whole(first_got[0].shape)] * 3
        + [whole(value.shape) for value in (*mine, *other)]
        + [whole(half)] * len(carried),
        [shape((ROWS, TILE), out_dtype)] * n,
        [whole((ROWS, TILE))] * n,
        [],
        (2 * ROWS * 1024 * TILE * n, 2 << 20),
        8,
        after,
    )


def window_start(ids, owner):
    before = jnp.sum((ids < owner * VARS).astype(jnp.int32))
    return jnp.minimum(before, ROWS - WINDOW)


def dispatch_kernel(ids_ref, x_ref, *outs):
    me = lax.axis_index("pool")
    ids = ids_ref[...]
    features = x_ref[...]
    for k in range(NX):
        owner = lax.rem(me + k, NX)
        start = window_start(ids, owner)
        at = lax.broadcasted_iota(jnp.int32, (WINDOW, ROWS), 0) + start
        hot = (at == lax.broadcasted_iota(jnp.int32, (WINDOW, ROWS), 1)).astype(F32).astype(BF16)
        outs[k][0:WINDOW, :] = jnp.dot(hot, features, preferred_element_type=F32).astype(BF16)
        local = jnp.broadcast_to((ids - owner * VARS).astype(F32), (IDROWS, ROWS)).astype(BF16)
        outs[k][WINDOW : WINDOW + IDROWS, :] = lax.dot_general(
            local, hot, (((1,), (1,)), ((), ())), preferred_element_type=F32
        ).astype(BF16)


def dispatch(ids, features, after=()):
    return call(
        dispatch_kernel,
        (ids, features),
        [whole((1, ROWS)), whole((ROWS, WIDTH))],
        [shape((WINDOW + IDROWS, WIDTH))] * NX,
        [whole((WINDOW + IDROWS, WIDTH))] * NX,
        [],
        (2 * 1024 * 512 * 256, 1 << 20),
        6,
        after,
    )


def spread_columns(row, lanes):
    diagonal = lax.broadcasted_iota(jnp.int32, (WINDOW, WINDOW), 0) == lax.broadcasted_iota(
        jnp.int32, (WINDOW, WINDOW), 1
    )
    row = jnp.broadcast_to(row.astype(F32), (WINDOW, WINDOW))
    spread = jnp.where(diagonal, row, 0.0).astype(BF16)
    return jnp.dot(spread, jnp.ones((WINDOW, lanes), BF16), preferred_element_type=F32)


def variant_columns(item_ref, lanes):
    return spread_columns(item_ref[WINDOW : WINDOW + 1, :], lanes)


def down_kernel(i0, i1, i2, i3, down_ref, out_ref, item_ref, fold_ref):
    for k, item in enumerate((i0, i1, i2, i3)):
        item_ref[k] = item[...]
    lane = lax.broadcasted_iota(jnp.int32, (1, 256), 1)
    part = lax.div(lane, jnp.int32(RANK)).astype(F32)

    def window(k, carry):
        item = item_ref.at[k]
        variant = variant_columns(item, 256)
        features = item[0:WINDOW, :]
        total = None
        for j in range(VARS * RANK // 256):
            value = lax.dot_general(
                features,
                down_ref[j * 256 : (j + 1) * 256, :],
                (((1,), (1,)), ((), ())),
                preferred_element_type=F32,
            )
            value = jnp.where(variant == part + float(j * 4), value, 0.0)
            total = value if total is None else total + value
        two = total[:, 0:128] + total[:, 128:256]
        fold_ref[k] = two + pltpu.roll(two, RANK, 1)
        return carry

    lax.fori_loop(0, NX, window, 0)
    low = lax.broadcasted_iota(jnp.int32, (WINDOW, 128), 1) < RANK
    for h in range(2):
        packed = jnp.where(low, fold_ref[h], fold_ref[h + 2]).astype(BF16)
        out_ref[:, h * 128 : (h + 1) * 128] = packed


def down(items, factor, after=()):
    return call(
        down_kernel,
        (*items, factor),
        [whole((WINDOW + IDROWS, WIDTH))] * NX + [whole((VARS * RANK, WIDTH))],
        shape((WINDOW, 256)),
        whole((WINDOW, 256)),
        [pltpu.VMEM((NX, WINDOW + IDROWS, WIDTH), BF16), pltpu.VMEM((NX, WINDOW, 128), F32)],
        (2 * 1024 * 256 * 2048, 2 << 20),
        8,
        after,
    )


def block_kernel(i0, i1, i2, i3, mats_ref, place_ref, out_ref, item_ref, rhs_ref):
    for k, item in enumerate((i0, i1, i2, i3)):
        item_ref[k] = item[...]
    shard = lax.axis_index(Z) * NY + lax.axis_index(Y)
    for v in range(VARS):
        first = (v // 2) * BLK
        lanes = slice((v % 2) * BLK, (v % 2 + 1) * BLK)
        rhs_ref[first : first + BLK, lanes] = mats_ref[v]

    rows, kept = [], []
    for k in range(NX):
        item = item_ref.at[k]
        ids = item[WINDOW : WINDOW + 1, :].astype(F32)
        code = jnp.full(ids.shape, 64.0, F32)
        for v in range(VARS):
            place = (place_ref[v] - shard * 2).astype(F32)
            code = jnp.where(ids == float(v), v // 2 + 16.0 * (v % 2) + 32.0 * place, code)
        code = spread_columns(code, 128)
        upper = (code >= 32.0) & (code < 64.0)
        rest = jnp.where(upper, code - 32.0, code)
        odd = rest >= 16.0
        pair = jnp.where(odd, rest - 16.0, rest).astype(BF16)
        low = item[0:WINDOW, 0:BLK].astype(F32)
        high = item[0:WINDOW, BLK : 2 * BLK].astype(F32)
        picked = jnp.where(upper, high, low).astype(BF16)
        zero = jnp.zeros_like(picked)
        pieces = [jnp.where(pair == jnp.bfloat16(p), picked, zero) for p in range(VARS // 2)]
        rows.append(jnp.concatenate(pieces, axis=1))
        kept.append((upper, odd))
    lhs = jnp.concatenate(rows, axis=0)
    every = jnp.dot(lhs, rhs_ref[...], preferred_element_type=F32)
    for k, (upper, odd) in enumerate(kept):
        both = every[k * WINDOW : (k + 1) * WINDOW, :]
        one = jnp.where(odd, both[:, BLK:], both[:, 0:BLK])
        out_ref[k, :, 0:BLK] = jnp.where(upper, 0.0, one)
        out_ref[k, :, BLK : 2 * BLK] = jnp.where(upper, one, 0.0)


def block_terms(items, mats, places, after=()):
    return call(
        block_kernel,
        (*items, mats, places),
        [whole((WINDOW + IDROWS, WIDTH))] * NX + [whole((VARS, BLK, BLK)), SMEM],
        shape((NX, WINDOW, 256), F32),
        whole((NX, WINDOW, 256)),
        [pltpu.VMEM((NX, WINDOW + IDROWS, WIDTH), BF16), pltpu.VMEM((VARS * BLK // 2, 256), BF16)],
        (2 * 1024 * 2048 * 256, 3 << 20),
        10,
        after,
    )


def add_kernel(a_ref, b_ref, out_ref):
    out_ref[...] = (a_ref[...].astype(F32) + b_ref[...].astype(F32)).astype(BF16)


def exchanged_sum(value, axis, partner, after=()):
    other = lax.ppermute(value, axis, list(enumerate(partner)))
    return call(
        add_kernel,
        (value, other),
        [whole((WINDOW, 256))] * 2,
        shape((WINDOW, 256)),
        whole((WINDOW, 256)),
        [],
        (1 << 16, 3 << 17),
        2,
        after,
    )


def up_kernel(i0, i1, i2, i3, l0, l1, l2, l3, up_ref, block_ref, *refs):
    outs, (item_ref, two_ref, out_ref) = refs[:NX], refs[NX:]
    low = l0[...].astype(F32) + l1[...].astype(F32) + l2[...].astype(F32) + l3[...].astype(F32)
    low = low.astype(BF16).astype(F32)
    for k, item in enumerate((i0, i1, i2, i3)):
        item_ref[k] = item[WINDOW : WINDOW + IDROWS, :]
    first = lax.broadcasted_iota(jnp.int32, (WINDOW, 128), 1) < RANK
    for h in range(2):
        packed = low[:, h * 128 : (h + 1) * 128]
        turned = pltpu.roll(packed, RANK, 1)
        two_ref[h] = jnp.where(first, packed, turned)
        two_ref[h + 2] = jnp.where(first, turned, packed)
    half = lax.div(lax.broadcasted_iota(jnp.int32, (1, 128), 1), jnp.int32(RANK)).astype(F32)

    rows = []
    for k in range(NX):
        variant = (spread_columns(item_ref[k, 0:1, :], 128) - half).astype(BF16)
        two = two_ref[k].astype(BF16)
        zero = jnp.zeros_like(two)
        pieces = []
        for i in range(VARS // 2):
            pieces.append(jnp.where(variant == jnp.bfloat16(2 * i), two, zero))
        rows.append(jnp.concatenate(pieces, axis=1))
    lhs = jnp.concatenate(rows, axis=0)
    total = jnp.dot(lhs, up_ref[...], preferred_element_type=F32)
    for k in range(NX):
        outs[k][...] = (block_ref[k] + total[k * WINDOW : (k + 1) * WINDOW, :]).astype(BF16)


def up(items, lows, factor, blocks, after=()):
    return call(
        up_kernel,
        (*items, *lows, factor, blocks),
        [whole((WINDOW + IDROWS, WIDTH))] * NX
        + [whole((WINDOW, 256))] * 4
        + [whole((VARS * RANK, WIDTH)), whole((NX, WINDOW, 256))],
        [shape((WINDOW, WIDTH))] * NX,
        [whole((WINDOW, WIDTH))] * NX,
        [
            pltpu.VMEM((NX, IDROWS, WIDTH), BF16),
            pltpu.VMEM((NX, WINDOW, 128), F32),
            pltpu.VMEM((NX, WINDOW, WIDTH), BF16),
        ],
        (2 * 1024 * 256 * 2048, 3 << 20),
        10,
        after,
    )


def combine_kernel(ids_ref, h_ref, own_ref, plus_ref, r0, r1, r2, r3, first_ref, branch_ref):
    me = lax.axis_index("pool")
    ids = ids_ref[...]
    branch = own_ref[...] + plus_ref[...].astype(F32)
    delta = None
    for k, back in enumerate((r0, r1, r2, r3)):
        start = window_start(ids, lax.rem(me + k, NX))
        at = lax.broadcasted_iota(jnp.int32, (ROWS, WINDOW), 1) + start
        hot = (at == lax.broadcasted_iota(jnp.int32, (ROWS, WINDOW), 0)).astype(F32).astype(BF16)
        part = jnp.dot(hot, back[...], preferred_element_type=F32)
        delta = part if delta is None else delta + part
    branch = branch + delta
    branch_ref[...] = branch
    first_ref[...] = (h_ref[...].astype(F32) + branch).astype(BF16)


def combine(ids, hidden, own, plus, returned, after=()):
    half = (ROWS, WIDTH)
    return call(
        combine_kernel,
        (ids, hidden, own, plus, *returned),
        [whole((1, ROWS))] + [whole(half)] * 3 + [whole((WINDOW, WIDTH))] * NX,
        [shape(half), shape(half, F32)],
        [whole(half)] * 2,
        [],
        (2 * 512 * 1024 * 256, 2 << 20),
        8,
        after,
    )


def steps(
    hidden_input,
    attention_output,
    projection_weight,
    lowrank_down_factor,
    lowrank_up_factor,
    residual_block_mats,
    diagonal_block_index,
    row_variant_index,
):
    features = attention_output[0]
    weight = projection_weight[0]
    down_factor = lowrank_down_factor[0].reshape(VARS * RANK, WIDTH)
    up_factor = lowrank_up_factor[0].reshape(VARS * RANK, WIDTH)
    mats = residual_block_mats[0][:, 0]
    places = diagonal_block_index[0][:, 0]
    ids = row_variant_index.reshape(1, ROWS)

    (first,), (own0,) = pack(((0,),), weight, features)
    got = [shift(value, Y, hop) for value, hop in zip(first, HOPS)]
    sent = dispatch(ids, features, (first[0],))
    items = spread_over_pools(sent, 1)
    (second, third), (own1, own2, own3) = pack(((1,), (2, 3)), weight, None, (sent[0],))
    got1 = [shift(value, Y, hop) for value, hop in zip(second, HOPS)]
    low = down(items, down_factor, (second[0],))
    got2 = [shift(value, Y, hop) for value, hop in zip(third, HOPS)]
    low1 = exchanged_sum(low, Z, (1, 0, 3, 2, 5, 4, 7, 6))
    low2 = exchanged_sum(low1, Z, (2, 3, 0, 1, 6, 7, 4, 5))
    plus, minus = project((0, 1), own0, features, got, (), (), (), (low1,))
    carried = (shift(plus, Z, 1), shift(minus, Z, -1))
    mine1 = join(got1, 0, (True,), (plus,))
    other1 = (shift(mine1[0], "pool", 1), shift(mine1[1], "pool", -1))
    low3 = exchanged_sum(low2, Z, (6, 7, 4, 5, 2, 3, 0, 1))
    plus, minus = project((0, 1), own1, features, got, mine1, other1, carried)
    mine2, mine3 = join(got2, 0, (False, False), (plus,))
    other2 = swapped(mine2, False)
    carried = (shift(plus, Z, 1), shift(minus, Z, -1))
    other3 = swapped(mine3, True)
    lows = [low3] + [shift(low3, Y, hop) for hop in HOPS]
    blocks = block_terms(items, mats, places, (plus,))
    plus, minus = project((0, 1), own2, features, got, (mine2,), (other2,), carried, (blocks,))
    carried = (shift(plus, Z, 1), shift(minus, Z, -1))
    served = up(items, lows, up_factor, blocks, (plus,))
    returned = spread_over_pools(served, -1)
    (plus,) = project(
        (0,), own3, features, got, (mine3,), (other3,), carried[:1], (served[1],)
    )
    arrived = shift(plus, Z, 1)
    (own,) = project(
        (1,), own3, features, got, (mine3,), (other3,), carried[1:], (plus,), F32
    )
    plus = arrived

    first_out, branch = combine(ids, hidden_input, own, plus, returned)
    carried = lax.ppermute(first_out, "section", [(0, 1)])
    begin = jnp.where(lax.axis_index("section") == 0, hidden_input, carried)
    return (begin.astype(F32) + branch).astype(BF16)[None]


def solution(mesh):
    finer = Mesh(
        mesh.devices.reshape(mesh.shape["pool"], mesh.shape["section"], NZ, NY),
        ("pool", "section", Z, Y),
    )
    placed = (
        P("pool", TENSOR),
        P("section", "pool", TENSOR),
        P("section", TENSOR, None),
        P("section", "pool", None, TENSOR),
        P("section", "pool", None, TENSOR),
        P("section", "pool", TENSOR, None, None),
        P("section", "pool", TENSOR),
        P("pool"),
    )
    return jax.shard_map(
        steps,
        mesh=finer,
        in_specs=placed,
        out_specs=P("section", "pool", TENSOR),
        check_vma=False,
    )
```
